32 devices in a mesh: dp: 8 (over z, y), tensor: 4 (over x, core).
Axes of the slice: x: 2, y: 2, z: 4, core: 2. Of those that a mesh axis runs over, the one named last changes fastest.
Arguments:
- tokens: bfloat16 [16384, 768], P(('dp', 'tensor')), may hold values from -6 to 6
- segments: int32 [8, 2048], P('dp', 'tensor'), may hold values from 0 to 3, never falling along the last dimension, each value on 1 to 1024 neighbouring positions
- query_proj: bfloat16 [768, 768], P('dp', 'tensor'), may hold values from -0.3125 to 0.3125
- query_bias: float32 [768], P(('dp', 'tensor')), may hold values from -3 to 3
- key_proj: bfloat16 [768, 768], P('dp', 'tensor'), may hold values from -0.21875 to 0.21875
- value_proj: bfloat16 [768, 768], P('dp', 'tensor'), may hold values from -0.21875 to 0.21875
- value_bias: float32 [768], P(('dp', 'tensor')), may hold values from -3 to 3
- merge_proj: bfloat16 [768, 768], P('tensor', 'dp'), may hold values from -1.75 to 1.75
- merge_bias: float32 [768], P(('dp', 'tensor')), may hold values from -3 to 3
- first_gain: float32 [768], P(('dp', 'tensor')), may hold values from 0.5 to 1.5
- first_shift: float32 [768], P(('dp', 'tensor')), may hold values from -3 to 3
- expand_proj: bfloat16 [768, 3072], P('dp', 'tensor'), may hold values from -0.21875 to 0.21875
- expand_bias: float32 [3072], P(('dp', 'tensor')), may hold values from -3 to 3
- shrink_proj: bfloat16 [3072, 768], P('tensor', 'dp'), may hold values from -0.15625 to 0.15625
- shrink_bias: float32 [768], P(('dp', 'tensor')), may hold values from -3 to 3
- second_gain: float32 [768], P(('dp', 'tensor')), may hold values from 0.5 to 1.5
- second_shift: float32 [768], P(('dp', 'tensor')), may hold values from -3 to 3
- cotangent: bfloat16 [16384, 768], P(('dp', 'tensor')), may hold values from -6 to 6
Outputs:
- output: bfloat16 [16384, 768], P(('dp', 'tensor'))
- tokens_grad: bfloat16 [16384, 768], P(('dp', 'tensor'))
- querygrad: float32 [768, 768], P('dp', 'tensor')
- qbiasgrad: float32 [768], P(('dp', 'tensor'))
- keygrad: float32 [768, 768], P('dp', 'tensor')
- valuegrad: float32 [768, 768], P('dp', 'tensor')
- vbiasgrad: float32 [768], P(('dp', 'tensor'))
- mergegrad: float32 [768, 768], P('tensor', 'dp')
- mbiasgrad: float32 [768], P(('dp', 'tensor'))
- fgaingrad: float32 [768], P(('dp', 'tensor'))
- fshiftgrad: float32 [768], P(('dp', 'tensor'))
- expandgrad: float32 [768, 3072], P('dp', 'tensor')
- ebiasgrad: float32 [3072], P(('dp', 'tensor'))
- shrinkgrad: float32 [3072, 768], P('tensor', 'dp')
- sbiasgrad: float32 [768], P(('dp', 'tensor'))
- sgaingrad: float32 [768], P(('dp', 'tensor'))
- sshiftgrad: float32 [768], P(('dp', 'tensor'))
The draws below stay inside these ranges and needn't reach their ends.
Inputs may be any that keep to these rules, and one draw needn't show every extreme that they name: `segments`: along each sequence the segment numbers never fall; each of the 4 numbers marks 1 to 1024 positions of every sequence.
All inputs are finite; a program needn't handle non-finite values.
Results may differ from the reference program's by a relative error of at most 0.023.
Values may be sent and summed in bfloat16 or wider, within the bound.
No kernel may reach another device: no remote copies, remote signals or barrier semaphores. Data moves between devices by JAX's collectives and lax.ppermute only.
A program may use at most 128 MiB of HBM per device.

```python
import math
import jax
import jax.numpy as jnp
import numpy as np
from jax import lax

D = 768
HEADS = 12
HD = 64
FF = 3072
SEQ_LEN = 2048
DOCS = 4
TOKENS = 16384
N_DP = 8


def spiked(entries, own_key, source, target, parts, factor):
    owner, partner = [(jnp.arange(entries.shape[position]) // (entries.shape[position] // parts)).reshape([-1 if axis == position else 1 for axis in range(entries.ndim)]) for position in (source, target)]
    chosen = jax.random.permutation(own_key, parts)[partner]
    strong = (owner == chosen) | (owner == (partner + parts // 2) % parts)
    return jnp.where(strong, factor * entries, entries)


def block_levels(rng, extent, cuts, least, largest):
    loudness = 1.0
    for axis_at, blocks in cuts:
        draws = jax.random.uniform(jax.random.fold_in(jax.random.fold_in(rng, 6), axis_at), (blocks,), jnp.float32, least / len(cuts), largest / len(cuts))
        loudness = loudness * jnp.repeat(jnp.exp(draws), extent[axis_at] // blocks).reshape((-1,) + (1,) * (len(extent) - 1 - axis_at))
    return loudness


def profile(number_of, total, bound, slope):
    weights = [(1 << 20) // math.isqrt(grade ** slope) + 1 for grade in range(2, number_of + 1)]
    surplus, counts = total - bound - (number_of - 1), [1] * (number_of - 1)
    while surplus > 0:
        movable = [i for i in range(number_of - 1) if counts[i] < bound]
        whole, budget = sum([weights[i] for i in movable]), surplus
        for i in movable:
            addition = min(bound - counts[i], max(1, budget * weights[i] // whole), surplus)
            counts[i] = counts[i] + addition
            surplus = surplus - addition
    return np.array([bound] + counts)


def ragged(own_key, count, total, reach, slope):
    if count == 2:
        one = jax.random.randint(own_key, (), max(1, total - reach), min(reach, total - 1) + 1)
        return jnp.stack([one, total - one])
    sizes = jnp.asarray(profile(count, total, reach, slope), jnp.int32)
    pairs = (count - 1) // 2
    giver, sink = sizes[1:1 + 2 * pairs:2], sizes[2:2 + 2 * pairs:2]
    margin = jnp.minimum(giver - 1, reach - sink)
    moved = jax.random.randint(jax.random.fold_in(own_key, 1), (pairs,), 0, 1 << 20) % (margin + 1)
    sizes = sizes.at[1:1 + 2 * pairs:2].set(giver - moved).at[2:2 + 2 * pairs:2].set(sink + moved)
    return sizes[jax.random.permutation(jax.random.fold_in(own_key, 2), count)]


def scatter_about(rng, dims, deviation, most, split=(), held_as=jnp.bfloat16):
    values = jax.random.normal(rng, dims, jnp.float32) * deviation
    if len(split) > 0:
        values = block_levels(rng, dims, split, -0.22, 0.18) * values
    return jnp.clip(values, min=-most, max=most).astype(held_as)


def noise_with(stream_key, shape, deviation, most, cuts, heavy, dtype=jnp.bfloat16):
    values = deviation * jax.random.normal(stream_key, shape, jnp.float32)
    if cuts:
        values = values * block_levels(stream_key, shape, cuts, -0.22, 0.18)
    return jnp.clip(spiked(values, jax.random.fold_in(stream_key, 3), *heavy), -most, most).astype(dtype)


def setup_inputs(seed: int = 0) -> dict:
    seeds = jax.random.split(jax.random.key(seed), 19)
    tokens = noise_with(seeds[0], (TOKENS, D), 1.0, 6.0, ((0, 32),), (0, 1, 32, 2.75))
    segments = jax.vmap(lambda own: jnp.searchsorted(jnp.cumsum(ragged(own, DOCS, SEQ_LEN, SEQ_LEN // 2, 2)), jnp.arange(SEQ_LEN), side="right"))(jax.random.split(seeds[1], N_DP)).reshape((N_DP, SEQ_LEN)).astype(jnp.int32)
    query_proj = scatter_about(seeds[2], (D, D), (D // 2) ** -0.5, 0.3125, ((0, 8), (1, 4)))
    query_bias = scatter_about(seeds[3], (D,), 0.5, 3.0, ((0, 32),), jnp.float32)
    key_proj = scatter_about(seeds[4], (D, D), D ** -0.5, 0.21875, ((0, 8), (1, 4)))
    value_proj = scatter_about(seeds[5], (D, D), D ** -0.5, 0.21875, ((0, 8), (1, 4)))
    value_bias = scatter_about(seeds[6], (D,), 0.5, 3.0, ((0, 32),), jnp.float32)
    merge_proj = scatter_about(seeds[7], (D, D), (D // 64) ** -0.5, 1.75, ((0, 4), (1, 8)))
    merge_bias = scatter_about(seeds[8], (D,), 0.5, 3.0, ((0, 32),), jnp.float32)
    first_gain = jnp.clip(1.0 + 0.1 * jax.random.normal(seeds[9], (D,), jnp.float32), 0.5, 1.5)
    first_shift = scatter_about(seeds[10], (D,), 0.5, 3.0, ((0, 32),), jnp.float32)
    expand_proj = scatter_about(seeds[11], (D, FF), D ** -0.5, 0.21875, ((0, 8), (1, 4)))
    expand_bias = scatter_about(seeds[12], (FF,), 0.5, 3.0, ((0, 32),), jnp.float32)
    shrink_proj = scatter_about(seeds[13], (FF, D), (FF // 2) ** -0.5, 0.15625, ((0, 4), (1, 8)))
    shrink_bias = scatter_about(seeds[14], (D,), 0.5, 3.0, ((0, 32),), jnp.float32)
    second_gain = jnp.clip(1.0 + 0.1 * jax.random.normal(seeds[15], (D,), jnp.float32), 0.5, 1.5)
    second_shift = scatter_about(seeds[16], (D,), 0.5, 3.0, ((0, 32),), jnp.float32)
    cotangent = noise_with(seeds[17], (TOKENS, D), 1.0, 6.0, ((0, 32),), (0, 1, 32, 2.75))
    return dict(tokens=tokens, segments=segments, query_proj=query_proj, query_bias=query_bias, key_proj=key_proj, value_proj=value_proj, value_bias=value_bias, merge_proj=merge_proj, merge_bias=merge_bias, first_gain=first_gain, first_shift=first_shift, expand_proj=expand_proj, expand_bias=expand_bias, shrink_proj=shrink_proj, shrink_bias=shrink_bias, second_gain=second_gain, second_shift=second_shift, cotangent=cotangent)


EPSILON = 1e-12
HIGH = lax.Precision.HIGHEST

@jax.custom_vjp
def low(v):
    return lax.optimization_barrier(v.astype(jnp.bfloat16)).astype(jnp.float32)

@jax.custom_vjp
def low_back(v):
    return v

def low_keep(v):
    return (low(v), None)

def low_pass(kept, grad):
    return (grad,)

def back_keep(v):
    return (v, None)

def back_low(kept, grad):
    return (low(grad),)
low.defvjp(low_keep, low_pass)
low_back.defvjp(back_keep, back_low)

def matmul(left, right):
    return jnp.dot(left, right, precision=HIGH, preferred_element_type=jnp.float32)

def normalize(values, gain, shift):
    centre = lax.optimization_barrier(jnp.mean(values, axis=-1, keepdims=True))
    centred = values - centre
    spread = lax.optimization_barrier(jnp.mean(centred * centred, axis=-1, keepdims=True))
    return centred * lax.rsqrt(spread + EPSILON) * gain + shift

def gelu_exact(values):
    return jax.nn.gelu(values, approximate=False)

def layer(tokens, params, seg_row):
    query_proj, query_bias, key_proj, value_proj, value_bias, merge_proj, merge_bias, first_gain, first_shift, expand_proj, expand_bias, shrink_proj, shrink_bias, second_gain, second_shift = params
    length = tokens.shape[0]
    query = low(low_back(matmul(tokens, query_proj)) + query_bias).reshape(length, HEADS, HD)
    keys = low(low_back(matmul(tokens, key_proj))).reshape(length, HEADS, HD)
    values = low(low_back(matmul(tokens, value_proj)) + value_bias).reshape(length, HEADS, HD)
    block = min(512, length)
    count = length // block
    scale = HD ** (-0.5)

    def attend(item):
        query_rows, seg_rows = item
        raw = low_back(jnp.einsum('qhd,khd->hqk', query_rows, keys, precision=HIGH))
        same = (seg_rows[:, None] == seg_row[None, :])[None]
        scores = jnp.where(same, raw * scale, -1e+30)
        peak = lax.optimization_barrier(jnp.max(scores, axis=2, keepdims=True))
        raised = jnp.exp(scores - peak)
        chance = raised / lax.optimization_barrier(jnp.sum(raised, axis=2, keepdims=True))
        return jnp.einsum('hqk,khd->qhd', low(chance), values, precision=HIGH)
    context = lax.map(jax.checkpoint(attend), (query.reshape(count, block, HEADS, HD), seg_row.reshape(count, block)))
    context = low_back(low(context.reshape(length, HEADS * HD)))
    mixed = tokens + low_back(matmul(context, merge_proj)) + merge_bias
    hidden = normalize(mixed, first_gain, first_shift)
    inner = low_back(matmul(low(hidden), expand_proj)) + expand_bias
    summed = hidden + low_back(matmul(low(gelu_exact(inner)), shrink_proj)) + shrink_bias
    return normalize(summed, second_gain, second_shift)

def reference(tokens, segments, query_proj, query_bias, key_proj, value_proj, value_bias, merge_proj, merge_bias, first_gain, first_shift, expand_proj, expand_bias, shrink_proj, shrink_bias, second_gain, second_shift, cotangent):
    params = tuple((value.astype(jnp.float32) for value in (query_proj, query_bias, key_proj, value_proj, value_bias, merge_proj, merge_bias, first_gain, first_shift, expand_proj, expand_bias, shrink_proj, shrink_bias, second_gain, second_shift)))
    inputs_all = tokens.astype(jnp.float32).reshape(N_DP, SEQ_LEN, D)
    grads_all = cotangent.astype(jnp.float32).reshape(N_DP, SEQ_LEN, D)

    def one(carry, item):
        rows, seg_row, grad_rows = item

        def forward(inputs, weights):
            return layer(inputs, weights, seg_row)
        result, pull = jax.vjp(forward, rows, params)
        grad_inputs, grad_weights = pull(grad_rows)
        carry = jax.tree.map(lambda total, extra: total + extra, carry, grad_weights)
        return (carry, (result.astype(jnp.bfloat16), grad_inputs.astype(jnp.bfloat16)))
    zeros = tuple((jnp.zeros_like(value) for value in params))
    grads, (results, grad_tokens) = lax.scan(one, zeros, (inputs_all, segments, grads_all))
    output = results.reshape(TOKENS, D)
    tokens_grad = grad_tokens.reshape(TOKENS, D)
    return (output, tokens_grad, grads[0], grads[1], grads[2], grads[3], grads[4], grads[5], grads[6], grads[7], grads[8], grads[9], grads[10], grads[11], grads[12], grads[13], grads[14])
```

```python
import jax, jax.numpy as jnp
from jax import lax
from jax.sharding import PartitionSpec as P
from jax.experimental import pallas as pl
from jax.experimental.pallas import tpu as pltpu

HD=64
BQ=256
BK=256
LOG2E=1.4426950408889634
NN=(((1,),(0,)),((),()))
NT=(((1,),(1,)),((),()))
TN=(((0,),(0,)),((),()))
f32=jnp.float32; bf16=jnp.bfloat16

def head_cols(h, heads):
    start=(h//2)*128
    stop=min(start+128, heads*HD)
    return start, stop

def padded(ref, h, heads, rows):
    start, stop = head_cols(h, heads)
    piece = ref[h*HD:(h+1)*HD, rows]
    if stop-start == HD: return piece
    zero = jnp.zeros_like(piece)
    return jnp.concatenate([piece, zero] if h%2==0 else [zero, piece], axis=0)

def fwd_kernel(lo_ref, hi_ref, flip_ref, q_ref, k_ref, v_ref, segc_ref, segr_ref, o_ref, lse_ref, s_ref):
    heads = q_ref.shape[0]//HD
    i = pl.program_id(0)
    lo = lo_ref[i]; hi = hi_ref[i]; flip = flip_ref[0]
    c = LOG2E * HD**-0.5
    qz = [padded(q_ref, h, heads, slice(None)) for h in range(heads)]
    segq = segr_ref[...]
    def one(kb, peaks):
        start = pl.multiple_of(jnp.bitwise_xor(kb, flip)*BK, BK)
        same = segc_ref[pl.ds(start,BK),:] == segq
        new=[]
        for h in range(heads):
            a,b = head_cols(h, heads)
            s = lax.dot_general(k_ref[pl.ds(start,BK), a:b], qz[h], NN, preferred_element_type=f32)
            s = jnp.where(same, s, -1e30)
            s_ref[h, kb-lo] = s
            new.append(jnp.maximum(peaks[h], jnp.max(s.reshape(BK//8,8,BQ),axis=0)))
        return tuple(new)
    peaks = lax.fori_loop(lo, hi, one, tuple(jnp.full((8,BQ),-1e30,f32) for _ in range(heads)))
    peaks = [jnp.max(p,axis=0,keepdims=True)*c for p in peaks]
    def two(kb, carry):
        sums, outs = carry
        start = pl.multiple_of(jnp.bitwise_xor(kb, flip)*BK, BK)
        ns=[];no=[]
        for h in range(heads):
            p = jnp.exp2(s_ref[h, kb-lo]*c - peaks[h])
            ns.append(sums[h]+jnp.sum(p.reshape(BK//8,8,BQ),axis=0))
            no.append(outs[h]+lax.dot_general(v_ref[h*HD:(h+1)*HD, pl.ds(start,BK)], p.astype(bf16), NN, preferred_element_type=f32))
        return tuple(ns),tuple(no)
    sums, outs = lax.fori_loop(lo, hi, two, (tuple(jnp.zeros((8,BQ),f32) for _ in range(heads)), tuple(jnp.zeros((HD,BQ),f32) for _ in range(heads))))
    for h in range(heads):
        total = jnp.sum(sums[h],axis=0,keepdims=True)
        o_ref[h*HD:(h+1)*HD,:] = (outs[h]/total).astype(bf16)
        lse_ref[h:h+1,:] = peaks[h]+jnp.log2(total)

def attn_fwd(qT,k,vT,segc,segr,lo,hi,flip):
    width,length=qT.shape
    heads=width//HD
    blocks=length//BQ
    return pl.pallas_call(
        fwd_kernel,
        out_shape=(jax.ShapeDtypeStruct((width,length),bf16), jax.ShapeDtypeStruct((heads,length),f32)),
        grid_spec=pltpu.PrefetchScalarGridSpec(num_scalar_prefetch=3, grid=(blocks,),
            in_specs=[pl.BlockSpec((width,BQ),lambda i,*_:(0,i)),
                      pl.BlockSpec((length,width),lambda i,*_:(0,0)),
                      pl.BlockSpec((width,length),lambda i,*_:(0,0)),
                      pl.BlockSpec((length,1),lambda i,*_:(0,0)),
                      pl.BlockSpec((1,BQ),lambda i,*_:(0,i))],
            out_specs=[pl.BlockSpec((width,BQ),lambda i,*_:(0,i)),pl.BlockSpec((heads,BQ),lambda i,*_:(0,i))],
            scratch_shapes=[pltpu.VMEM((heads,length//BK,BK,BQ),f32)]),
        compiler_params=pltpu.CompilerParams(dimension_semantics=("arbitrary",),vmem_limit_bytes=40<<20),
        cost_estimate=pl.CostEstimate(flops=4*length*length//2*width,bytes_accessed=8*length*width,transcendentals=heads*length*length//2),
        name="attention",
    )(lo,hi,flip,qT,k,vT,segc,segr)

def bwd_kernel(lo_ref, hi_ref, flip_ref, q_ref, k_ref, kT_ref, v_ref, do_ref, o_ref, lse_ref, segc_ref, segr_ref,
               dq_ref, dk_ref, dv_ref, qb_ref, vb_ref, dk_acc, dv_acc):
    heads = q_ref.shape[0]//HD
    width = q_ref.shape[0]
    i = pl.program_id(0)
    @pl.when(i==0)
    def _():
        dk_acc[...]=jnp.zeros_like(dk_acc); dv_acc[...]=jnp.zeros_like(dv_acc)
        qb_ref[...]=jnp.zeros_like(qb_ref)
    lo = lo_ref[i]; hi = hi_ref[i]; flip = flip_ref[0]
    scale = HD**-0.5
    c = LOG2E*scale
    qz = [padded(q_ref, h, heads, slice(None)) for h in range(heads)]
    dz = [padded(do_ref, h, heads, slice(None)) for h in range(heads)]
    deltas = [jnp.sum(do_ref[h*HD:(h+1)*HD,:].astype(f32)*o_ref[h*HD:(h+1)*HD,:].astype(f32),axis=0,keepdims=True) for h in range(heads)]
    segq = segr_ref[...]
    def one(kb, dqs):
        start = pl.multiple_of(jnp.bitwise_xor(kb, flip)*BK, BK)
        rows = pl.ds(start,BK)
        same = segc_ref[rows,:] == segq
        out=[]
        parts={}
        for h in range(heads):
            a,b = head_cols(h, heads)
            s = lax.dot_general(k_ref[rows, a:b], qz[h], NN, preferred_element_type=f32)
            p = jnp.exp2(jnp.where(same, s*c - lse_ref[h:h+1,:], -1e30))
            dp = lax.dot_general(v_ref[rows, a:b], dz[h], NN, preferred_element_type=f32)
            ds = (p*((dp-deltas[h])*scale)).astype(bf16)
            dvp = lax.dot_general(p.astype(bf16), dz[h], NT, preferred_element_type=f32)
            dkp = lax.dot_general(ds, qz[h], NT, preferred_element_type=f32)
            if (a,b) in parts: parts[a,b]=(parts[a,b][0]+dkp,parts[a,b][1]+dvp)
            else: parts[a,b]=(dkp,dvp)
            out.append(dqs[h]+lax.dot_general(kT_ref[h*HD:(h+1)*HD, rows], ds, NN, preferred_element_type=f32))
        for (a,b),(dkp,dvp) in parts.items():
            dk_acc[rows,a:b]+=dkp
            dv_acc[rows,a:b]+=dvp
        return tuple(out)
    dqs = lax.fori_loop(lo,hi,one,tuple(jnp.zeros((HD,BQ),f32) for _ in range(heads)))
    for h in range(heads):
        dq_ref[h*HD:(h+1)*HD,:]=dqs[h].astype(bf16)
        part = dqs[h][:,:128]
        for n in range(128,BQ,128): part=part+dqs[h][:,n:n+128]
        qb_ref[h*HD:(h+1)*HD,:]+=part
    @pl.when(i==pl.num_programs(0)-1)
    def _():
        dk_ref[...]=dk_acc[...].astype(bf16)
        dv_ref[...]=dv_acc[...].astype(bf16)
        vb_ref[...]=jnp.sum(dv_acc[...].reshape(dv_acc.shape[0]//8,8,width),axis=0)

def attn_bwd(qT,k,kT,v,doT,oT,lse,segc,segr,lo,hi,flip):
    width,length=qT.shape
    heads=width//HD
    blocks=length//BQ
    col=pl.BlockSpec((width,BQ),lambda i,*_:(0,i))
    row=pl.BlockSpec((length,width),lambda i,*_:(0,0))
    return pl.pallas_call(
        bwd_kernel,
        out_shape=(jax.ShapeDtypeStruct((width,length),bf16), jax.ShapeDtypeStruct((length,width),bf16), jax.ShapeDtypeStruct((length,width),bf16), jax.ShapeDtypeStruct((width,128),f32), jax.ShapeDtypeStruct((8,width),f32)),
        grid_spec=pltpu.PrefetchScalarGridSpec(num_scalar_prefetch=3, grid=(blocks,),
            in_specs=[col,row,pl.BlockSpec((width,length),lambda i,*_:(0,0)),row,col,col,
                      pl.BlockSpec((heads,BQ),lambda i,*_:(0,i)),
                      pl.BlockSpec((length,1),lambda i,*_:(0,0)),
                      pl.BlockSpec((1,BQ),lambda i,*_:(0,i))],
            out_specs=[col,row,row,pl.BlockSpec((width,128),lambda i,*_:(0,0)),pl.BlockSpec((8,width),lambda i,*_:(0,0))],
            scratch_shapes=[pltpu.VMEM((length,width),f32),pltpu.VMEM((length,width),f32)]),
        compiler_params=pltpu.CompilerParams(dimension_semantics=("arbitrary",),vmem_limit_bytes=40<<20),
        cost_estimate=pl.CostEstimate(flops=10*length*length//2*width,bytes_accessed=20*length*width,transcendentals=heads*length*length//2),
        name="attention_back",
    )(lo,hi,flip,qT,k,kT,v,doT,oT,lse,segc,segr)

def spans(seg_row):
    length=seg_row.shape[0]
    first=seg_row[::BQ]; last=seg_row[BQ-1::BQ]
    lo=jnp.sum(seg_row[None,:]<first[:,None],axis=1,dtype=jnp.int32)//BK
    hi=(jnp.sum(seg_row[None,:]<=last[:,None],axis=1,dtype=jnp.int32)+BK-1)//BK
    return lo,hi

EPSILON=1e-12
T=256
RC=32

def row_stats(values):
    centre=jnp.mean(values,axis=1,keepdims=True)
    centred=values-centre
    spread=jnp.mean(centred*centred,axis=1,keepdims=True)
    scale=lax.rsqrt(spread+EPSILON)
    return centred*scale, scale

def fold(values):
    return jnp.sum(values.reshape(values.shape[0]//8,8,values.shape[1]),axis=0)

def ffn_kernel(tok_ref, a0_ref, a1_ref, a2_ref, cot_ref, vec_ref, be_ref,
               e0,e1,e2,e3,
               out_ref, gm_ref, gml_ref, vg_ref, eb_ref, d0,d1,d2,d3,
               we, ws, hl, hlT, hid, xhat, rs1, act, gp, acc, sl, slT, gsum, il, de, dt, wsem, osem):
    es=(e0,e1,e2,e3); ds=(d0,d1,d2,d3)
    rows, width = tok_ref.shape
    blocks=len(es); units=we.shape[2]
    for r in range(blocks):
        pltpu.make_async_copy(es[r].at[:,0:units],we.at[r],wsem.at[0,r]).start()
        pltpu.make_async_copy(es[r].at[:,units:],ws.at[r],wsem.at[1,r]).start()
    mb=vec_ref[0:1,:]; g1=vec_ref[1:2,:]; b1=vec_ref[2:3,:]; sb=vec_ref[3:4,:]; g2=vec_ref[4:5,:]; b2=vec_ref[5:6,:]
    def first(i,_):
        at=pl.ds(pl.multiple_of(i*RC,RC),RC)
        mixed=tok_ref[at,:].astype(f32)+(a0_ref[at,:].astype(f32)+a1_ref[at,:].astype(f32)+a2_ref[at,:].astype(f32))+mb
        z,scale=row_stats(mixed)
        xhat[at,:]=z
        rs1[at,:]=jnp.broadcast_to(scale,(RC,128))
        h=z*g1+b1
        hid[at,:]=h
        hl[at,:]=h.astype(bf16)
        acc[at,:]=jnp.zeros((RC,width),f32)
        return 0
    lax.fori_loop(0,rows//RC,first,0)
    def turn(src,dst):
        def go(i,_):
            at=pl.multiple_of(i*T,T)
            dst[:,pl.ds(at,T)]=jnp.transpose(src[pl.ds(at,T),:].astype(f32)).astype(bf16)
            return 0
        lax.fori_loop(0,rows//T,go,0)
    turn(hl,hlT)
    per=units//T; mt=rows//T
    def forward(r,_):
        for k in range(blocks):
            @pl.when(r==k)
            def _():
                pltpu.make_async_copy(es[k].at[:,0:units],we.at[k],wsem.at[0,k]).wait()
        def tile(j,_):
            n=pl.multiple_of((j//mt)*T,T); m=pl.multiple_of((j%mt)*T,T)
            u=lax.dot_general(hl[pl.ds(m,T),:],we[r,:,pl.ds(n,T)],NN,preferred_element_type=f32)+be_ref[pl.ds(r,1),pl.ds(n,T)]
            cdf=0.5+0.5*lax.erf(u*(0.5**0.5))
            act[r,pl.ds(m,T),pl.ds(n,T)]=(u*cdf).astype(bf16)
            gp[r,pl.ds(m,T),pl.ds(n,T)]=cdf+u*(jnp.exp(-0.5*u*u)*0.3989422804014327)
            return 0
        lax.fori_loop(0,per*mt,tile,0)
        for k in range(blocks):
            @pl.when(r==k)
            def _():
                pltpu.make_async_copy(es[k].at[:,units:],ws.at[k],wsem.at[1,k]).wait()
        def shrink(j,_):
            n=pl.multiple_of((j//mt)*T,T); m=pl.multiple_of((j%mt)*T,T)
            acc[pl.ds(m,T),pl.ds(n,T)]+=lax.dot_general(act[r,pl.ds(m,T),:],ws[r,pl.ds(n,T),:],NT,preferred_element_type=f32)
            return 0
        lax.fori_loop(0,(width//T)*mt,shrink,0)
        return 0
    lax.fori_loop(0,blocks,forward,0)
    def second(i,sums):
        at=pl.ds(pl.multiple_of(i*RC,RC),RC)
        summed=hid[at,:]+acc[at,:]+sb
        z,scale=row_stats(summed)
        out_ref[at,:]=(z*g2+b2).astype(bf16)
        cot=cot_ref[at,:].astype(f32)
        e=cot*g2
        g=(e-jnp.mean(e,axis=1,keepdims=True)-z*jnp.mean(e*z,axis=1,keepdims=True))*scale
        gsum[at,:]=g
        sl[at,:]=g.astype(bf16)
        acc[at,:]=g
        return (sums[0]+fold(cot*z),sums[1]+fold(cot),sums[2]+fold(g))
    zero=jnp.zeros((8,width),f32)
    sg,sh,sbg=lax.fori_loop(0,rows//RC,second,(zero,zero,zero))
    turn(sl,slT)
    def sent(r,slot,k):
        return (pltpu.make_async_copy(de.at[slot],ds[k].at[:,0:units],osem.at[0,slot]),pltpu.make_async_copy(dt.at[slot],ds[k].at[:,units:],osem.at[1,slot]))
    def backward(r,_):
        slot=r%2
        def tile(j,_):
            n=pl.multiple_of((j//mt)*T,T); m=pl.multiple_of((j%mt)*T,T)
            ga=lax.dot_general(sl[pl.ds(m,T),:],ws[r,:,pl.ds(n,T)],NN,preferred_element_type=f32)
            gi=ga*gp[r,pl.ds(m,T),pl.ds(n,T)]
            il[pl.ds(m,T),pl.ds(n,T)]=gi.astype(bf16)
            part=fold(gi)
            eb_ref[r,:,pl.ds(n,T)]=jnp.where(m==0,part,eb_ref[r,:,pl.ds(n,T)]+part)
            return 0
        lax.fori_loop(0,per*mt,tile,0)
        def back(j,_):
            n=pl.multiple_of((j//mt)*T,T); m=pl.multiple_of((j%mt)*T,T)
            acc[pl.ds(m,T),pl.ds(n,T)]+=lax.dot_general(il[pl.ds(m,T),:],we[r,pl.ds(n,T),:],NT,preferred_element_type=f32)
            return 0
        lax.fori_loop(0,(width//T)*mt,back,0)
        for k in range(2,blocks):
            @pl.when(r==k)
            def _():
                for c in sent(r,k%2,k-2): c.wait()
        def grads(j,_):
            n=pl.multiple_of((j//(width//T))*T,T); m=pl.multiple_of((j%(width//T))*T,T)
            dt[slot,pl.ds(m,T),pl.ds(n,T)]=lax.dot_general(slT[pl.ds(m,T),:],act[r,:,pl.ds(n,T)],NN,preferred_element_type=f32).astype(bf16)
            de[slot,pl.ds(m,T),pl.ds(n,T)]=lax.dot_general(hlT[pl.ds(m,T),:],il[:,pl.ds(n,T)],NN,preferred_element_type=f32).astype(bf16)
            return 0
        lax.fori_loop(0,(width//T)*per,grads,0)
        for k in range(blocks):
            @pl.when(r==k)
            def _():
                for c in sent(r,k%2,k): c.start()
        return 0
    lax.fori_loop(0,blocks,backward,0)
    def last(i,sums):
        at=pl.ds(pl.multiple_of(i*RC,RC),RC)
        g=acc[at,:]
        z=xhat[at,:]
        e=g*g1
        gm=(e-jnp.mean(e,axis=1,keepdims=True)-z*jnp.mean(e*z,axis=1,keepdims=True))*rs1[at,0:1]
        gm_ref[at,:]=gm
        gml_ref[at,:]=gm.astype(bf16)
        return (sums[0]+fold(g*z),sums[1]+fold(g),sums[2]+fold(gm))
    fg,fs,mbg=lax.fori_loop(0,rows//RC,last,(zero,zero,zero))
    for n,v in enumerate((mbg,fg,fs,sbg,sg,sh)):
        vg_ref[n]=v
    for k in range(max(0,blocks-2),blocks):
        for c in sent(k,k%2,k): c.wait()

def ffn(tok,a0,a1,a2,cot,vec,be,es):
    rows,width=tok.shape; blocks=len(es); units=es[0].shape[1]//2
    v=pl.BlockSpec(memory_space=pltpu.VMEM); h=pl.BlockSpec(memory_space=pltpu.HBM)
    g=jax.ShapeDtypeStruct((width,2*units),bf16)
    V=pltpu.VMEM
    return pl.pallas_call(
        ffn_kernel,
        out_shape=(jax.ShapeDtypeStruct((rows,width),bf16),jax.ShapeDtypeStruct((rows,width),f32),jax.ShapeDtypeStruct((rows,width),bf16),
                   jax.ShapeDtypeStruct((6,8,width),f32),jax.ShapeDtypeStruct((blocks,8,units),f32))+(g,)*blocks,
        in_specs=[v]*7+[h]*blocks,
        out_specs=[v]*5+[h]*blocks,
        scratch_shapes=[V((blocks,width,units),bf16),V((blocks,width,units),bf16),
            V((rows,width),bf16),V((width,rows),bf16),V((rows,width),f32),V((rows,width),f32),V((rows,128),f32),
            V((blocks,rows,units),bf16),V((blocks,rows,units),f32),V((rows,width),f32),V((rows,width),bf16),V((width,rows),bf16),V((rows,width),f32),
            V((rows,units),bf16),V((2,width,units),bf16),V((2,width,units),bf16),
            pltpu.SemaphoreType.DMA((2,blocks)),pltpu.SemaphoreType.DMA((2,2))],
        compiler_params=pltpu.CompilerParams(vmem_limit_bytes=60<<20),
        cost_estimate=pl.CostEstimate(flops=12*rows*width*units*blocks,bytes_accessed=8*blocks*width*units,transcendentals=2*rows*units*blocks),
        name="feed_forward",
    )(tok,a0,a1,a2,cot,vec,be,*es)

def exchange(value, bit):
    return lax.ppermute(value, "tensor", [(i, i ^ bit) for i in range(4)])


def gather_rows(own):
    across = exchange(own, 2)
    return jnp.concatenate([own, exchange(own, 1), across, exchange(across, 1)], axis=0)


def scatter_rows(partial):
    rows = partial.shape[0] // 4
    low = partial.astype(bf16)
    piece = lambda r: low[r * rows : (r + 1) * rows]
    beside = exchange(jnp.concatenate([piece(1), piece(3)], axis=0), 1)
    ahead = (piece(2).astype(f32) + beside[rows:].astype(f32)).astype(bf16)
    return piece(0), beside[:rows], exchange(ahead, 2)


def on_device(
    tokens,
    segments,
    query_proj,
    query_bias,
    key_proj,
    value_proj,
    value_bias,
    merge_proj,
    merge_bias,
    first_gain,
    first_shift,
    expand_proj,
    expand_bias,
    shrink_proj,
    shrink_bias,
    second_gain,
    second_shift,
    cotangent,
):
    everyone = ("dp", "tensor")
    part = lax.axis_index("tensor")
    dp = lax.axis_size("dp")
    world = dp * 4
    width = query_proj.shape[1]
    units = expand_proj.shape[1]
    model = width * 4
    share = model // world
    unit_share = units * 4 // world

    shard = jnp.concatenate([query_proj, key_proj, value_proj, merge_proj.T], axis=1)
    attn_w = lax.all_gather(shard, "dp", axis=0, tiled=True)
    wide = jnp.concatenate([expand_proj, shrink_proj.T], axis=1)
    w0 = lax.all_gather(wide, "dp", axis=0, tiled=True)
    w2 = lax.all_gather(exchange(wide, 2), "dp", axis=0, tiled=True)
    w1 = exchange(w0, 1)
    w3 = exchange(w2, 1)
    own = jnp.concatenate(
        [query_bias, value_bias, merge_bias, first_gain, first_shift, shrink_bias, second_gain, second_shift, expand_bias]
    )
    slots = -(-own.shape[0] // 1024) * 8
    own = jnp.pad(own, (0, slots * 128 - own.shape[0])).reshape(1, slots, 128)
    vectors = lax.all_to_all(jnp.broadcast_to(own, (world, slots, 128)), everyone, 0, 0, tiled=True)
    vectors = vectors.reshape(world, slots * 128)
    whole = [vectors[:, n * share : (n + 1) * share].reshape(model) for n in range(8)]
    unit_bias = vectors[:, 8 * share : 8 * share + unit_share].reshape(4, units)
    flips = jnp.bitwise_xor(jnp.arange(4), part)
    unit_bias = jnp.take(unit_bias, flips, axis=0)
    query_b = lax.dynamic_slice_in_dim(whole[0], part * width, width)
    value_b = lax.dynamic_slice_in_dim(whole[1], part * width, width)
    rows_b = jnp.stack(whole[2:8])

    full = gather_rows(tokens)
    seg = gather_rows(segments.reshape(-1))
    segc, segr = seg[:, None], seg[None, :]
    lo, hi = spans(seg)
    flip = (part * (tokens.shape[0] // BK)).astype(jnp.int32).reshape(1)
    wq, wk, wv, wm = (attn_w[:, n * width : (n + 1) * width] for n in range(4))
    dot = lambda a, b, dims: lax.dot_general(a, b, dims, preferred_element_type=f32)
    query_t = (dot(wq, full, (((0,), (1,)), ((), ()))) + query_b[:, None]).astype(bf16)
    key_t = dot(wk, full, (((0,), (1,)), ((), ()))).astype(bf16)
    value_t = (dot(wv, full, (((0,), (1,)), ((), ()))) + value_b[:, None]).astype(bf16)
    keys = dot(full, wk, NN).astype(bf16)
    values = (dot(full, wv, NN) + value_b).astype(bf16)
    context_t, logsum = attn_fwd(query_t, keys, value_t, segc, segr, lo, hi, flip)
    a0, a1, a2 = scatter_rows(dot(context_t, wm, (((0,), (1,)), ((), ()))))

    out = ffn(tokens, a0, a1, a2, cotangent, rows_b, unit_bias, [w0, w1, w2, w3])
    output, grad_mixed, mixed_low, row_sums, unit_sums = out[:5]
    g0, g1, g2, g3 = out[5:]

    full_mixed = gather_rows(mixed_low)
    grad_context_t = dot(wm, full_mixed, (((0,), (1,)), ((), ()))).astype(bf16)
    dq_t, dk, dv, q_sums, v_sums = attn_bwd(
        query_t, keys, key_t, values, grad_context_t, context_t, logsum, segc, segr, lo, hi, flip
    )
    total = dot(dq_t, wq, (((0,), (1,)), ((), ()))) + dot(dk, wk, NT) + dot(dv, wv, NT)
    b0, b1, b2 = scatter_rows(total)
    tokens_grad = (grad_mixed + (b0.astype(f32) + b1.astype(f32) + b2.astype(f32))).astype(bf16)

    merge_local = dot(full_mixed, context_t, (((0,), (1,)), ((), ())))
    query_local = dot(full, dq_t, (((0,), (1,)), ((), ())))
    key_local = dot(full, dk, TN)
    value_local = dot(full, dv, TN)
    attn_local = jnp.concatenate([query_local, key_local, value_local, merge_local], axis=1).astype(bf16)
    swapped = lax.all_to_all(attn_local, "dp", 0, 0, tiled=True)
    attn_grad = jnp.sum(swapped.reshape(dp, -1, model).astype(f32), axis=0)
    querygrad, keygrad, valuegrad, mergegrad = (attn_grad[:, n * width : (n + 1) * width] for n in range(4))

    near = (g0.astype(f32) + exchange(g1, 1).astype(f32)).astype(bf16)
    far = (g2.astype(f32) + exchange(g3, 1).astype(f32)).astype(bf16)
    wide_local = (near.astype(f32) + exchange(far, 2).astype(f32)).astype(bf16)
    wide_grad = lax.psum_scatter(wide_local, "dp", scatter_dimension=0, tiled=True).astype(f32)
    expandgrad = wide_grad[:, :units]
    shrinkgrad = wide_grad[:, units:].T

    zero = jnp.zeros((4, width), f32)
    q_all = lax.dynamic_update_slice(zero, jnp.sum(q_sums, axis=1)[None], (part, 0)).reshape(world, share)
    v_all = lax.dynamic_update_slice(zero, jnp.sum(v_sums, axis=0)[None], (part, 0)).reshape(world, share)
    u_all = jnp.take(jnp.sum(unit_sums, axis=1), flips, axis=0).reshape(world, unit_share)
    row_all = [v.reshape(world, share) for v in jnp.sum(row_sums, axis=1)]
    send = jnp.concatenate([q_all, v_all] + row_all + [u_all], axis=1)
    send = jnp.pad(send, ((0, 0), (0, slots * 128 - send.shape[1]))).reshape(world, slots, 128)
    got = jnp.sum(lax.all_to_all(send, everyone, 0, 0, tiled=True).reshape(world, slots * 128), axis=0)
    small = [got[n * share : (n + 1) * share] for n in range(8)]
    qbiasgrad, vbiasgrad, mbiasgrad, fgaingrad, fshiftgrad, sbiasgrad, sgaingrad, sshiftgrad = small
    ebiasgrad = got[8 * share : 8 * share + unit_share]
    return (
        output,
        tokens_grad,
        querygrad,
        qbiasgrad,
        keygrad,
        valuegrad,
        vbiasgrad,
        mergegrad.T,
        mbiasgrad,
        fgaingrad,
        fshiftgrad,
        expandgrad,
        ebiasgrad,
        shrinkgrad,
        sbiasgrad,
        sgaingrad,
        sshiftgrad,
    )


def solution(mesh):
    return jax.shard_map(
        on_device,
        mesh=mesh,
        in_specs=(
            P(("dp", "tensor"), None),
            P("dp", "tensor"),
            P("dp", "tensor"),
            P(("dp", "tensor")),
            P("dp", "tensor"),
            P("dp", "tensor"),
            P(("dp", "tensor")),
            P("tensor", "dp"),
            P(("dp", "tensor")),
            P(("dp", "tensor")),
            P(("dp", "tensor")),
            P("dp", "tensor"),
            P(("dp", "tensor")),
            P("tensor", "dp"),
            P(("dp", "tensor")),
            P(("dp", "tensor")),
            P(("dp", "tensor")),
            P(("dp", "tensor"), None),
        ),
        out_specs=(
            P(("dp", "tensor"), None),
            P(("dp", "tensor"), None),
            P("dp", "tensor"),
            P(("dp", "tensor")),
            P("dp", "tensor"),
            P("dp", "tensor"),
            P(("dp", "tensor")),
            P("tensor", "dp"),
            P(("dp", "tensor")),
            P(("dp", "tensor")),
            P(("dp", "tensor")),
            P("dp", "tensor"),
            P(("dp", "tensor")),
            P("tensor", "dp"),
            P(("dp", "tensor")),
            P(("dp", "tensor")),
            P(("dp", "tensor")),
        ),
        check_vma=False,
    )
```

```python
import jax, jax.numpy as jnp
from jax import lax
from jax.sharding import PartitionSpec as P
from jax.experimental import pallas as pl
from jax.experimental.pallas import tpu as pltpu

HD=64
BQ=256
BK=256
LOG2E=1.4426950408889634
NN=(((1,),(0,)),((),()))
NT=(((1,),(1,)),((),()))
TN=(((0,),(0,)),((),()))
f32=jnp.float32; bf16=jnp.bfloat16

def head_cols(h, heads):
    start=(h//2)*128
    stop=min(start+128, heads*HD)
    return start, stop

def padded(ref, h, heads, rows):
    start, stop = head_cols(h, heads)
    piece = ref[h*HD:(h+1)*HD, rows]
    if stop-start == HD: return piece
    zero = jnp.zeros_like(piece)
    return jnp.concatenate([piece, zero] if h%2==0 else [zero, piece], axis=0)

def fwd_kernel(lo_ref, hi_ref, flip_ref, q_ref, k_ref, v_ref, segc_ref, segr_ref, o_ref, lse_ref, s_ref):
    heads = q_ref.shape[0]//HD
    i = pl.program_id(0)
    lo = lo_ref[i]; hi = hi_ref[i]; flip = flip_ref[0]
    c = LOG2E * HD**-0.5
    qz = [padded(q_ref, h, heads, slice(None)) for h in range(heads)]
    segq = segr_ref[...]
    def one(kb, peaks):
        start = pl.multiple_of(jnp.bitwise_xor(kb, flip)*BK, BK)
        same = segc_ref[pl.ds(start,BK),:] == segq
        new=[]
        for h in range(heads):
            a,b = head_cols(h, heads)
            s = lax.dot_general(k_ref[pl.ds(start,BK), a:b], qz[h], NN, preferred_element_type=f32)
            s = jnp.where(same, s, -1e30)
            s_ref[h, kb-lo] = s
            new.append(jnp.maximum(peaks[h], jnp.max(s.reshape(BK//8,8,BQ),axis=0)))
        return tuple(new)
    peaks = lax.fori_loop(lo, hi, one, tuple(jnp.full((8,BQ),-1e30,f32) for _ in range(heads)))
    peaks = [jnp.max(p,axis=0,keepdims=True)*c for p in peaks]
    def two(kb, carry):
        sums, outs = carry
        start = pl.multiple_of(jnp.bitwise_xor(kb, flip)*BK, BK)
        ns=[];no=[]
        for h in range(heads):
            p = jnp.exp2(s_ref[h, kb-lo]*c - peaks[h])
            ns.append(sums[h]+jnp.sum(p.reshape(BK//8,8,BQ),axis=0))
            no.append(outs[h]+lax.dot_general(v_ref[h*HD:(h+1)*HD, pl.ds(start,BK)], p.astype(bf16), NN, preferred_element_type=f32))
        return tuple(ns),tuple(no)
    sums, outs = lax.fori_loop(lo, hi, two, (tuple(jnp.zeros((8,BQ),f32) for _ in range(heads)), tuple(jnp.zeros((HD,BQ),f32) for _ in range(heads))))
    for h in range(heads):
        total = jnp.sum(sums[h],axis=0,keepdims=True)
        o_ref[h*HD:(h+1)*HD,:] = (outs[h]/total).astype(bf16)
        lse_ref[h:h+1,:] = peaks[h]+jnp.log2(total)

def attn_fwd(qT,k,vT,segc,segr,lo,hi,flip):
    width,length=qT.shape
    heads=width//HD
    blocks=length//BQ
    return pl.pallas_call(
        fwd_kernel,
        out_shape=(jax.ShapeDtypeStruct((width,length),bf16), jax.ShapeDtypeStruct((heads,length),f32)),
        grid_spec=pltpu.PrefetchScalarGridSpec(num_scalar_prefetch=3, grid=(blocks,),
            in_specs=[pl.BlockSpec((width,BQ),lambda i,*_:(0,i)),
                      pl.BlockSpec((length,width),lambda i,*_:(0,0)),
                      pl.BlockSpec((width,length),lambda i,*_:(0,0)),
                      pl.BlockSpec((length,1),lambda i,*_:(0,0)),
                      pl.BlockSpec((1,BQ),lambda i,*_:(0,i))],
            out_specs=[pl.BlockSpec((width,BQ),lambda i,*_:(0,i)),pl.BlockSpec((heads,BQ),lambda i,*_:(0,i))],
            scratch_shapes=[pltpu.VMEM((heads,length//BK,BK,BQ),f32)]),
        compiler_params=pltpu.CompilerParams(dimension_semantics=("arbitrary",),vmem_limit_bytes=60<<20),
        cost_estimate=pl.CostEstimate(flops=30*length*length*width,bytes_accessed=8*length*width,transcendentals=heads*length*length//2),
        name="attention",
    )(lo,hi,flip,qT,k,vT,segc,segr)

def bwd_kernel(lo_ref, hi_ref, flip_ref, q_ref, k_ref, kT_ref, v_ref, wT_ref, g0, g1, g2, g3, o_ref, lse_ref, segc_ref, segr_ref,
               dq_ref, dk_ref, dv_ref, qb_ref, vb_ref, dk_acc, dv_acc, do_ref):
    heads = q_ref.shape[0]//HD
    width = q_ref.shape[0]
    i = pl.program_id(0)
    @pl.when(i==0)
    def _():
        dk_acc[...]=jnp.zeros_like(dk_acc); dv_acc[...]=jnp.zeros_like(dv_acc)
        qb_ref[...]=jnp.zeros_like(qb_ref)
    lo = lo_ref[i]; hi = hi_ref[i]; flip = flip_ref[0]
    scale = HD**-0.5
    per = g0.shape[0]//BQ
    for n, g_ref in enumerate((g0, g1, g2, g3)):
        @pl.when(i//per==n)
        def _():
            at = pl.multiple_of((i%per)*BQ, BQ)
            do_ref[...] = lax.dot_general(wT_ref[3*width:,:], g_ref[pl.ds(at,BQ),:], NT, preferred_element_type=f32).astype(bf16)
    c = LOG2E*scale
    qz = [padded(q_ref, h, heads, slice(None)) for h in range(heads)]
    dz = [padded(do_ref, h, heads, slice(None)) for h in range(heads)]
    deltas = [jnp.sum(do_ref[h*HD:(h+1)*HD,:].astype(f32)*o_ref[h*HD:(h+1)*HD,:].astype(f32),axis=0,keepdims=True) for h in range(heads)]
    segq = segr_ref[...]
    def one(kb, dqs):
        start = pl.multiple_of(jnp.bitwise_xor(kb, flip)*BK, BK)
        rows = pl.ds(start,BK)
        same = segc_ref[rows,:] == segq
        out=[]
        parts={}
        for h in range(heads):
            a,b = head_cols(h, heads)
            s = lax.dot_general(k_ref[rows, a:b], qz[h], NN, preferred_element_type=f32)
            p = jnp.exp2(jnp.where(same, s*c - lse_ref[h:h+1,:], -1e30))
            dp = lax.dot_general(v_ref[rows, a:b], dz[h], NN, preferred_element_type=f32)
            ds = (p*((dp-deltas[h])*scale)).astype(bf16)
            dvp = lax.dot_general(p.astype(bf16), dz[h], NT, preferred_element_type=f32)
            dkp = lax.dot_general(ds, qz[h], NT, preferred_element_type=f32)
            if (a,b) in parts: parts[a,b]=(parts[a,b][0]+dkp,parts[a,b][1]+dvp)
            else: parts[a,b]=(dkp,dvp)
            out.append(dqs[h]+lax.dot_general(kT_ref[h*HD:(h+1)*HD, rows], ds, NN, preferred_element_type=f32))
        for (a,b),(dkp,dvp) in parts.items():
            dk_acc[rows,a:b]+=dkp
            dv_acc[rows,a:b]+=dvp
        return tuple(out)
    dqs = lax.fori_loop(lo,hi,one,tuple(jnp.zeros((HD,BQ),f32) for _ in range(heads)))
    for h in range(heads):
        dq_ref[h*HD:(h+1)*HD,:]=dqs[h].astype(bf16)
        part = dqs[h][:,:128]
        for n in range(128,BQ,128): part=part+dqs[h][:,n:n+128]
        qb_ref[h*HD:(h+1)*HD,:]+=part
    @pl.when(i==pl.num_programs(0)-1)
    def _():
        dk_ref[...]=dk_acc[...].astype(bf16)
        dv_ref[...]=dv_acc[...].astype(bf16)
        vb_ref[...]=jnp.sum(dv_acc[...].reshape(dv_acc.shape[0]//8,8,width),axis=0)

def attn_bwd(qT,k,kT,v,wT,grads,oT,lse,segc,segr,lo,hi,flip):
    width,length=qT.shape
    heads=width//HD
    blocks=length//BQ
    col=pl.BlockSpec((width,BQ),lambda i,*_:(0,i))
    row=pl.BlockSpec((length,width),lambda i,*_:(0,0))
    return pl.pallas_call(
        bwd_kernel,
        out_shape=(jax.ShapeDtypeStruct((width,length),bf16), jax.ShapeDtypeStruct((length,width),bf16), jax.ShapeDtypeStruct((length,width),bf16), jax.ShapeDtypeStruct((width,128),f32), jax.ShapeDtypeStruct((8,width),f32)),
        grid_spec=pltpu.PrefetchScalarGridSpec(num_scalar_prefetch=3, grid=(blocks,),
            in_specs=[col,row,pl.BlockSpec((width,length),lambda i,*_:(0,0)),row,pl.BlockSpec(wT.shape,lambda i,*_:(0,0))]+[pl.BlockSpec(g.shape,lambda i,*_:(0,0)) for g in grads]+[col,
                      pl.BlockSpec((heads,BQ),lambda i,*_:(0,i)),
                      pl.BlockSpec((length,1),lambda i,*_:(0,0)),
                      pl.BlockSpec((1,BQ),lambda i,*_:(0,i))],
            out_specs=[col,row,row,pl.BlockSpec((width,128),lambda i,*_:(0,0)),pl.BlockSpec((8,width),lambda i,*_:(0,0))],
            scratch_shapes=[pltpu.VMEM((length,width),f32),pltpu.VMEM((length,width),f32),pltpu.VMEM((width,BQ),bf16)]),
        compiler_params=pltpu.CompilerParams(dimension_semantics=("arbitrary",),vmem_limit_bytes=60<<20),
        cost_estimate=pl.CostEstimate(flops=60*length*length*width,bytes_accessed=20*length*width,transcendentals=heads*length*length//2),
        name="attention_back",
    )(lo,hi,flip,qT,k,kT,v,wT,*grads,oT,lse,segc,segr)

def spans(seg_row):
    length=seg_row.shape[0]
    first=seg_row[::BQ]; last=seg_row[BQ-1::BQ]
    lo=jnp.sum(seg_row[None,:]<first[:,None],axis=1,dtype=jnp.int32)//BK
    hi=(jnp.sum(seg_row[None,:]<=last[:,None],axis=1,dtype=jnp.int32)+BK-1)//BK
    return lo,hi

EPSILON=1e-12
T=256
RC=32

def row_stats(values):
    centre=jnp.mean(values,axis=1,keepdims=True)
    centred=values-centre
    spread=jnp.mean(centred*centred,axis=1,keepdims=True)
    scale=lax.rsqrt(spread+EPSILON)
    return centred*scale, scale

def fold(values):
    return jnp.sum(values.reshape(values.shape[0]//8,8,values.shape[1]),axis=0)

def ffn_kernel(tok_ref, a0_ref, a1_ref, a2_ref, cot_ref, vec_ref, be_ref,
               wa_ref,wb_ref,
               out_ref, gm_ref, gml_ref, vg_ref, eb_ref, ga_ref,gb_ref,
               we, ws, hl, hlT, hid, xhat, rs1, act, gp, acc, sl, slT, gsum, il, de, dt, wsem, osem):
    rows, width = tok_ref.shape
    blocks,_,units=we.shape
    es=[(wa_ref,wb_ref)[r%2].at[:,(r//2)*2*units:(r//2+1)*2*units] for r in range(blocks)]
    ds=[(ga_ref,gb_ref)[r%2].at[:,(r//2)*2*units:(r//2+1)*2*units] for r in range(blocks)]
    for r in range(blocks):
        pltpu.make_async_copy(es[r].at[:,0:units],we.at[r],wsem.at[0,r]).start()
        pltpu.make_async_copy(es[r].at[:,units:],ws.at[r],wsem.at[1,r]).start()
    mb=vec_ref[0:1,:]; g1=vec_ref[1:2,:]; b1=vec_ref[2:3,:]; sb=vec_ref[3:4,:]; g2=vec_ref[4:5,:]; b2=vec_ref[5:6,:]
    def first(i,_):
        at=pl.ds(pl.multiple_of(i*RC,RC),RC)
        mixed=tok_ref[at,:].astype(f32)+(a0_ref[at,:].astype(f32)+a1_ref[at,:].astype(f32)+a2_ref[at,:].astype(f32))+mb
        z,scale=row_stats(mixed)
        xhat[at,:]=z
        rs1[at,:]=jnp.broadcast_to(scale,(RC,128))
        h=z*g1+b1
        hid[at,:]=h
        hl[at,:]=h.astype(bf16)
        acc[at,:]=jnp.zeros((RC,width),f32)
        return 0
    lax.fori_loop(0,rows//RC,first,0,unroll=4)
    def turn(src,dst):
        def go(i,_):
            at=pl.multiple_of(i*T,T)
            dst[:,pl.ds(at,T)]=jnp.transpose(src[pl.ds(at,T),:].astype(f32)).astype(bf16)
            return 0
        lax.fori_loop(0,rows//T,go,0)
    turn(hl,hlT)
    TG=768; TM=min(512,rows); per=units//T; mt=rows//TM
    def forward(r,_):
        for k in range(blocks):
            @pl.when(r==k)
            def _():
                pltpu.make_async_copy(es[k].at[:,0:units],we.at[k],wsem.at[0,k]).wait()
        def tile(j,_):
            n=pl.multiple_of((j//mt)*T,T); m=pl.multiple_of((j%mt)*TM,TM)
            u=lax.dot_general(hl[pl.ds(m,TM),:],we[r,:,pl.ds(n,T)],NN,preferred_element_type=f32)+be_ref[pl.ds(r,1),pl.ds(n,T)]
            cdf=0.5+0.5*lax.erf(u*(0.5**0.5))
            act[r,pl.ds(m,TM),pl.ds(n,T)]=(u*cdf).astype(bf16)
            gp[r,pl.ds(m,TM),pl.ds(n,T)]=cdf+u*(jnp.exp(-0.5*u*u)*0.3989422804014327)
            return 0
        lax.fori_loop(0,per*mt,tile,0,unroll=3)
        for k in range(blocks):
            @pl.when(r==k)
            def _():
                pltpu.make_async_copy(es[k].at[:,units:],ws.at[k],wsem.at[1,k]).wait()
        def shrink(j,_):
            n=pl.multiple_of((j//mt)*T,T); m=pl.multiple_of((j%mt)*TM,TM)
            acc[pl.ds(m,TM),pl.ds(n,T)]+=lax.dot_general(act[r,pl.ds(m,TM),:],ws[r,pl.ds(n,T),:],NT,preferred_element_type=f32)
            return 0
        lax.fori_loop(0,(width//T)*mt,shrink,0,unroll=3)
        return 0
    lax.fori_loop(0,blocks,forward,0)
    def second(i,sums):
        at=pl.ds(pl.multiple_of(i*RC,RC),RC)
        summed=hid[at,:]+acc[at,:]+sb
        z,scale=row_stats(summed)
        out_ref[at,:]=(z*g2+b2).astype(bf16)
        cot=cot_ref[at,:].astype(f32)
        e=cot*g2
        g=(e-jnp.mean(e,axis=1,keepdims=True)-z*jnp.mean(e*z,axis=1,keepdims=True))*scale
        gsum[at,:]=g
        sl[at,:]=g.astype(bf16)
        acc[at,:]=g
        return (sums[0]+fold(cot*z),sums[1]+fold(cot),sums[2]+fold(g))
    zero=jnp.zeros((8,width),f32)
    sg,sh,sbg=lax.fori_loop(0,rows//RC,second,(zero,zero,zero),unroll=4)
    turn(sl,slT)
    def sent(r,slot,k):
        return (pltpu.make_async_copy(de.at[slot],ds[k].at[:,0:units],osem.at[0,slot]),pltpu.make_async_copy(dt.at[slot],ds[k].at[:,units:],osem.at[1,slot]))
    def backward(r,_):
        slot=r%2
        def tile(j,_):
            n=pl.multiple_of((j//mt)*T,T); m=pl.multiple_of((j%mt)*TM,TM)
            ga=lax.dot_general(sl[pl.ds(m,TM),:],ws[r,:,pl.ds(n,T)],NN,preferred_element_type=f32)
            gi=ga*gp[r,pl.ds(m,TM),pl.ds(n,T)]
            il[pl.ds(m,TM),pl.ds(n,T)]=gi.astype(bf16)
            part=fold(gi)
            eb_ref[r,:,pl.ds(n,T)]=jnp.where(m==0,part,eb_ref[r,:,pl.ds(n,T)]+part)
            return 0
        lax.fori_loop(0,per*mt,tile,0,unroll=3)
        def back(j,_):
            n=pl.multiple_of((j//mt)*T,T); m=pl.multiple_of((j%mt)*TM,TM)
            acc[pl.ds(m,TM),pl.ds(n,T)]+=lax.dot_general(il[pl.ds(m,TM),:],we[r,pl.ds(n,T),:],NT,preferred_element_type=f32)
            return 0
        lax.fori_loop(0,(width//T)*mt,back,0,unroll=3)
        for k in range(2,blocks):
            @pl.when(r==k)
            def _():
                for c in sent(r,k%2,k-2): c.wait()
        def grads(j,_):
            n=pl.multiple_of((j//(width//TG))*T,T); m=pl.multiple_of((j%(width//TG))*TG,TG)
            dt[slot,pl.ds(m,TG),pl.ds(n,T)]=lax.dot_general(slT[pl.ds(m,TG),:],act[r,:,pl.ds(n,T)],NN,preferred_element_type=f32).astype(bf16)
            de[slot,pl.ds(m,TG),pl.ds(n,T)]=lax.dot_general(hlT[pl.ds(m,TG),:],il[:,pl.ds(n,T)],NN,preferred_element_type=f32).astype(bf16)
            return 0
        lax.fori_loop(0,(width//TG)*per,grads,0,unroll=3)
        for k in range(blocks):
            @pl.when(r==k)
            def _():
                for c in sent(r,k%2,k): c.start()
        return 0
    lax.fori_loop(0,blocks,backward,0)
    def last(i,sums):
        at=pl.ds(pl.multiple_of(i*RC,RC),RC)
        g=acc[at,:]
        z=xhat[at,:]
        e=g*g1
        gm=(e-jnp.mean(e,axis=1,keepdims=True)-z*jnp.mean(e*z,axis=1,keepdims=True))*rs1[at,0:1]
        gm_ref[at,:]=gm
        gml_ref[at,:]=gm.astype(bf16)
        return (sums[0]+fold(g*z),sums[1]+fold(g),sums[2]+fold(gm))
    fg,fs,mbg=lax.fori_loop(0,rows//RC,last,(zero,zero,zero),unroll=4)
    for n,v in enumerate((mbg,fg,fs,sbg,sg,sh)):
        vg_ref[n]=v
    for k in range(max(0,blocks-2),blocks):
        for c in sent(k,k%2,k): c.wait()

def ffn(tok,a0,a1,a2,cot,vec,be,w_own,w_other):
    rows,width=tok.shape; blocks,units=be.shape
    v=pl.BlockSpec(memory_space=pltpu.VMEM); h=pl.BlockSpec(memory_space=pltpu.HBM)
    g=jax.ShapeDtypeStruct((width,blocks*units),bf16)
    V=pltpu.VMEM
    return pl.pallas_call(
        ffn_kernel,
        out_shape=(jax.ShapeDtypeStruct((rows,width),bf16),jax.ShapeDtypeStruct((rows,width),f32),jax.ShapeDtypeStruct((rows,width),bf16),
                   jax.ShapeDtypeStruct((6,8,width),f32),jax.ShapeDtypeStruct((blocks,8,units),f32))+(g,g),
        in_specs=[v]*7+[h]*2,
        out_specs=[v]*5+[h]*2,
        scratch_shapes=[V((blocks,width,units),bf16),V((blocks,width,units),bf16),
            V((rows,width),bf16),V((width,rows),bf16),V((rows,width),f32),V((rows,width),f32),V((rows,128),f32),
            V((blocks,rows,units),bf16),V((blocks,rows,units),f32),V((rows,width),f32),V((rows,width),bf16),V((width,rows),bf16),V((rows,width),f32),
            V((rows,units),bf16),V((2,width,units),bf16),V((2,width,units),bf16),
            pltpu.SemaphoreType.DMA((2,blocks)),pltpu.SemaphoreType.DMA((2,2))],
        compiler_params=pltpu.CompilerParams(vmem_limit_bytes=60<<20),
        cost_estimate=pl.CostEstimate(flops=30*rows*width*units*blocks,bytes_accessed=8*blocks*width*units,transcendentals=2*rows*units*blocks),
        name="feed_forward",
    )(tok,a0,a1,a2,cot,vec,be,w_own,w_other)


def proj_kernel(home_ref, x0, x1, x2, x3, wa_ref, wb_ref, bq_ref, bvc_ref, bvr_ref,
                q_ref, kT_ref, vT_ref, k_ref, v_ref, wT, w_ref, sem):
    model = w_ref.shape[0]
    count, rows = sem.shape[0], model // sem.shape[0]
    width = q_ref.shape[0]
    home = home_ref[0]
    def copy(r):
        src = (wa_ref, wb_ref)[r % 2].at[(r // 2) * rows : (r // 2 + 1) * rows]
        at = pl.multiple_of(jnp.bitwise_xor(home, r) * rows, rows)
        return pltpu.make_async_copy(src, w_ref.at[pl.ds(at, rows)], sem.at[r])
    if wa_ref.shape[0] == model:
        count = 1
        copy = lambda r: pltpu.make_async_copy(wa_ref, w_ref, sem.at[r])
    for r in range(count):
        copy(r).start()
    for r in range(count):
        copy(r).wait()
    def turn(i, _):
        at = pl.multiple_of(i * 256, 256)
        wT[:, pl.ds(at, 256)] = jnp.transpose(w_ref[pl.ds(at, 256), :].astype(f32)).astype(bf16)
        return 0
    lax.fori_loop(0, model // 256, turn, 0)
    for n, x_ref in enumerate((x0, x1, x2, x3)):
        size = x_ref.shape[0]
        def part(i, _):
            at = pl.multiple_of(i * 256, 256)
            to = pl.multiple_of(n * size + at, 256)
            x = x_ref[pl.ds(at, 256), :]
            kv = jnp.dot(x, w_ref[:, width : 3 * width], preferred_element_type=f32)
            k_ref[pl.ds(to, 256), :] = kv[:, 0:width].astype(bf16)
            v_ref[pl.ds(to, 256), :] = (kv[:, width:] + bvr_ref[...]).astype(bf16)
            t = lax.dot_general(wT[0 : 3 * width], x, NT, preferred_element_type=f32)
            q_ref[:, pl.ds(to, 256)] = (t[0:width] + bq_ref[...]).astype(bf16)
            kT_ref[:, pl.ds(to, 256)] = t[width : 2 * width].astype(bf16)
            vT_ref[:, pl.ds(to, 256)] = (t[2 * width :] + bvc_ref[...]).astype(bf16)
            return 0
        lax.fori_loop(0, size // 256, part, 0)


def project(home, tokens, wa, wb, count, bq, bv):
    length = 4 * tokens[0].shape[0]
    model = tokens[0].shape[1]
    width = bq.shape[0]
    v = pl.BlockSpec(memory_space=pltpu.VMEM)
    tall = jax.ShapeDtypeStruct((length, width), bf16)
    flat = jax.ShapeDtypeStruct((width, length), bf16)
    return pl.pallas_call(
        proj_kernel,
        out_shape=(flat, flat, flat, tall, tall, jax.ShapeDtypeStruct((model, model), bf16)),
        in_specs=[pl.BlockSpec(memory_space=pltpu.SMEM)] + [v] * 9,
        out_specs=[v] * 6,
        scratch_shapes=[pltpu.VMEM((model, model), bf16), pltpu.SemaphoreType.DMA((count,))],
        compiler_params=pltpu.CompilerParams(vmem_limit_bytes=60 << 20),
        cost_estimate=pl.CostEstimate(flops=30 * length * model * width, bytes_accessed=4 * length * model, transcendentals=0),
        name="projection",
    )(home, *tokens, wa, wb, bq[:, None], bv[:, None], bv[None, :])


def grads_kernel(x0, x1, x2, x3, g0, g1, g2, g3, c_ref, q_ref, k_ref, v_ref, o_ref, acc, xT, gT):
    width = q_ref.shape[0]
    model = x0.shape[1]
    for n, (x_ref, g_ref) in enumerate(zip((x0, x1, x2, x3), (g0, g1, g2, g3))):
        size = x_ref.shape[0]
        rows = slice(n * size, (n + 1) * size)
        def turn(i, _):
            at = pl.multiple_of(i * 256, 256)
            xT[:, pl.ds(at, 256)] = jnp.transpose(x_ref[pl.ds(at, 256), :].astype(f32)).astype(bf16)
            gT[:, pl.ds(at, 256)] = jnp.transpose(g_ref[pl.ds(at, 256), :].astype(f32)).astype(bf16)
            return 0
        lax.fori_loop(0, size // 256, turn, 0)
        def part(i, _):
            at = pl.ds(pl.multiple_of(i * 256, 256), 256)
            x = xT[at, :]
            pieces = (
                lax.dot_general(x, q_ref[:, rows], NT, preferred_element_type=f32),
                jnp.dot(x, k_ref[rows, :], preferred_element_type=f32),
                jnp.dot(x, v_ref[rows, :], preferred_element_type=f32),
                lax.dot_general(gT[at, :], c_ref[:, rows], NT, preferred_element_type=f32),
            )
            for m, piece in enumerate(pieces):
                total = piece if n == 0 else acc[m, at, :] + piece
                if n == 3:
                    o_ref[at, m * width : (m + 1) * width] = total.astype(bf16)
                else:
                    acc[m, at, :] = total
            return 0
        lax.fori_loop(0, model // 256, part, 0)


def attn_grads(tokens, grads, contextT, dqT, dk, dv):
    size, model = tokens[0].shape
    width = dqT.shape[0]
    v = pl.BlockSpec(memory_space=pltpu.VMEM)
    return pl.pallas_call(
        grads_kernel,
        out_shape=jax.ShapeDtypeStruct((model, 4 * width), bf16),
        in_specs=[v] * 12,
        out_specs=v,
        scratch_shapes=[pltpu.VMEM((4, model, width), f32), pltpu.VMEM((model, size), bf16), pltpu.VMEM((model, size), bf16)],
        compiler_params=pltpu.CompilerParams(vmem_limit_bytes=60 << 20),
        cost_estimate=pl.CostEstimate(flops=120 * size * model * width, bytes_accessed=24 * size * model, transcendentals=0),
        name="projection_grads",
    )(*tokens, *grads, contextT, dqT, dk, dv)


def hop(value, bit):
    count = lax.axis_size("dp")
    return lax.ppermute(value, "dp", [(i, i ^ bit) for i in range(count)])


def gather_shards(own):
    count = lax.axis_size("dp")
    if count != 8:
        every = lax.all_gather(own, "dp", axis=0, tiled=True)
        return every, every
    even = jnp.concatenate([own] + [hop(own, bit) for bit in (2, 4, 6)], axis=0)
    return even, hop(even, 1)


def later(value, *markers):
    anywhere = pl.BlockSpec(memory_space=pl.ANY)
    return pl.pallas_call(
        lambda *refs: None,
        out_shape=jax.ShapeDtypeStruct(value.shape, value.dtype),
        in_specs=[anywhere] * (1 + len(markers)),
        out_specs=anywhere,
        input_output_aliases={0: 0},
        cost_estimate=pl.CostEstimate(flops=0, bytes_accessed=0, transcendentals=0),
        name="later",
    )(value, *markers)


def exchange(value, bit):
    return lax.ppermute(value, "tensor", [(i, i ^ bit) for i in range(4)])


def row_blocks(own):
    across = exchange(own, 2)
    return [own, exchange(own, 1), across, exchange(across, 1)]


def gather_rows(own):
    return jnp.concatenate(row_blocks(own), axis=0)


def scatter_rows(partial):
    rows = partial.shape[0] // 4
    low = partial.astype(bf16)
    piece = lambda r: low[r * rows : (r + 1) * rows]
    beside = exchange(jnp.concatenate([piece(1), piece(3)], axis=0), 1)
    ahead = (piece(2).astype(f32) + beside[rows:].astype(f32)).astype(bf16)
    return (piece(0), beside[:rows], exchange(ahead, 2)), ahead


def on_device(
    tokens,
    segments,
    query_proj,
    query_bias,
    key_proj,
    value_proj,
    value_bias,
    merge_proj,
    merge_bias,
    first_gain,
    first_shift,
    expand_proj,
    expand_bias,
    shrink_proj,
    shrink_bias,
    second_gain,
    second_shift,
    cotangent,
):
    everyone = ("dp", "tensor")
    part = lax.axis_index("tensor")
    dp = lax.axis_size("dp")
    world = dp * 4
    width = query_proj.shape[1]
    units = expand_proj.shape[1]
    model = width * 4
    share = model // world
    unit_share = units * 4 // world

    shard = jnp.concatenate([query_proj, key_proj, value_proj, merge_proj.T], axis=1)
    shards = gather_shards(shard)
    wide = jnp.concatenate([expand_proj, shrink_proj.T], axis=1)
    wide = jnp.concatenate([wide, exchange(wide, 2)], axis=1)
    w_own = lax.all_gather(wide, "dp", axis=0, tiled=True)
    own = jnp.concatenate(
        [query_bias, value_bias, merge_bias, first_gain, first_shift, shrink_bias, second_gain, second_shift, expand_bias]
    )
    slots = -(-own.shape[0] // 1024) * 8
    own = jnp.pad(own, (0, slots * 128 - own.shape[0])).reshape(1, slots, 128)
    vectors = lax.all_to_all(jnp.broadcast_to(own, (world, slots, 128)), everyone, 0, 0, tiled=True)
    vectors = vectors.reshape(world, slots * 128)
    whole = [vectors[:, n * share : (n + 1) * share].reshape(model) for n in range(8)]
    unit_bias = vectors[:, 8 * share : 8 * share + unit_share].reshape(4, units)
    flips = jnp.bitwise_xor(jnp.arange(4), part)
    unit_bias = jnp.take(unit_bias, flips, axis=0)
    query_b = lax.dynamic_slice_in_dim(whole[0], part * width, width)
    value_b = lax.dynamic_slice_in_dim(whole[1], part * width, width)
    rows_b = jnp.stack(whole[2:8])

    blocks = row_blocks(tokens)
    seg = jnp.concatenate(row_blocks(segments.reshape(-1)), axis=0)
    segc, segr = seg[:, None], seg[None, :]
    lo, hi = spans(seg)
    flip = (part * (tokens.shape[0] // BK)).astype(jnp.int32).reshape(1)
    home = lax.axis_index("dp").astype(jnp.int32).reshape(1)
    query_t, key_t, value_t, keys, values, attn_wt = project(home, blocks, *shards, dp, query_b, value_b)
    wq, wk, wv, wm = (attn_wt[n * width : (n + 1) * width] for n in range(4))
    dot = lambda a, b, dims: lax.dot_general(a, b, dims, preferred_element_type=f32)
    context_t, logsum = attn_fwd(query_t, keys, value_t, segc, segr, lo, hi, flip)
    (a0, a1, a2), ahead = scatter_rows(dot(context_t, wm, TN))

    w_own = later(w_own, ahead)
    w_other = exchange(w_own, 1)
    out = ffn(tokens, a0, a1, a2, cotangent, rows_b, unit_bias, w_own, w_other)
    output, grad_mixed, mixed_low, row_sums, unit_sums = out[:5]
    g_own, g_other = out[5:]

    mixed_blocks = row_blocks(mixed_low)
    wide_local = (g_own.astype(f32) + exchange(g_other, 1).astype(f32)).astype(bf16)
    wide_local = lax.psum_scatter(wide_local, "dp", scatter_dimension=0, tiled=True)
    dq_t, dk, dv, q_sums, v_sums = attn_bwd(
        query_t, keys, key_t, values, attn_wt, mixed_blocks, context_t, logsum, segc, segr, lo, hi, flip
    )
    attn_local = attn_grads(blocks, mixed_blocks, context_t, dq_t, dk, dv)
    swapped = lax.all_to_all(attn_local, "dp", 0, 0, tiled=True)
    dq_late = later(dq_t, attn_local)
    total = dot(dq_late, wq, TN) + dot(dk, wk, NN) + dot(dv, wv, NN)
    (b0, b1, b2), _ = scatter_rows(total)
    tokens_grad = (grad_mixed + (b0.astype(f32) + b1.astype(f32) + b2.astype(f32))).astype(bf16)
    attn_grad = jnp.sum(swapped.reshape(dp, -1, model).astype(f32), axis=0)
    querygrad, keygrad, valuegrad, mergegrad = (attn_grad[:, n * width : (n + 1) * width] for n in range(4))
    wide_grad = wide_local[:, : 2 * units].astype(f32) + exchange(wide_local[:, 2 * units :], 2).astype(f32)
    expandgrad = wide_grad[:, :units]
    shrinkgrad = wide_grad[:, units:].T

    zero = jnp.zeros((4, width), f32)
    q_all = lax.dynamic_update_slice(zero, jnp.sum(q_sums, axis=1)[None], (part, 0)).reshape(world, share)
    v_all = lax.dynamic_update_slice(zero, jnp.sum(v_sums, axis=0)[None], (part, 0)).reshape(world, share)
    u_all = jnp.take(jnp.sum(unit_sums, axis=1), flips, axis=0).reshape(world, unit_share)
    row_all = [v.reshape(world, share) for v in jnp.sum(row_sums, axis=1)]
    send = jnp.concatenate([q_all, v_all] + row_all + [u_all], axis=1)
    send = jnp.pad(send, ((0, 0), (0, slots * 128 - send.shape[1]))).reshape(world, slots, 128)
    got = jnp.sum(lax.all_to_all(send, everyone, 0, 0, tiled=True).reshape(world, slots * 128), axis=0)
    small = [got[n * share : (n + 1) * share] for n in range(8)]
    qbiasgrad, vbiasgrad, mbiasgrad, fgaingrad, fshiftgrad, sbiasgrad, sgaingrad, sshiftgrad = small
    ebiasgrad = got[8 * share : 8 * share + unit_share]
    return (
        output,
        tokens_grad,
        querygrad,
        qbiasgrad,
        keygrad,
        valuegrad,
        vbiasgrad,
        mergegrad.T,
        mbiasgrad,
        fgaingrad,
        fshiftgrad,
        expandgrad,
        ebiasgrad,
        shrinkgrad,
        sbiasgrad,
        sgaingrad,
        sshiftgrad,
    )


def solution(mesh):
    return jax.shard_map(
        on_device,
        mesh=mesh,
        in_specs=(
            P(("dp", "tensor"), None),
            P("dp", "tensor"),
            P("dp", "tensor"),
            P(("dp", "tensor")),
            P("dp", "tensor"),
            P("dp", "tensor"),
            P(("dp", "tensor")),
            P("tensor", "dp"),
            P(("dp", "tensor")),
            P(("dp", "tensor")),
            P(("dp", "tensor")),
            P("dp", "tensor"),
            P(("dp", "tensor")),
            P("tensor", "dp"),
            P(("dp", "tensor")),
            P(("dp", "tensor")),
            P(("dp", "tensor")),
            P(("dp", "tensor"), None),
        ),
        out_specs=(
            P(("dp", "tensor"), None),
            P(("dp", "tensor"), None),
            P("dp", "tensor"),
            P(("dp", "tensor")),
            P("dp", "tensor"),
            P("dp", "tensor"),
            P(("dp", "tensor")),
            P("tensor", "dp"),
            P(("dp", "tensor")),
            P(("dp", "tensor")),
            P(("dp", "tensor")),
            P("dp", "tensor"),
            P(("dp", "tensor")),
            P("tensor", "dp"),
            P(("dp", "tensor")),
            P(("dp", "tensor")),
            P(("dp", "tensor")),
        ),
        check_vma=False,
    )
```

```python
import jax, jax.numpy as jnp
from jax import lax
from jax.sharding import PartitionSpec as P
from jax.experimental import pallas as pl
from jax.experimental.pallas import tpu as pltpu

HD=64
BQ=512
BK=512
LOG2E=1.4426950408889634
NN=(((1,),(0,)),((),()))
NT=(((1,),(1,)),((),()))
TN=(((0,),(0,)),((),()))
f32=jnp.float32; bf16=jnp.bfloat16

def head_cols(h, heads):
    start=(h//2)*128
    stop=min(start+128, heads*HD)
    return start, stop

def padded(ref, h, heads, rows):
    start, stop = head_cols(h, heads)
    piece = ref[h*HD:(h+1)*HD, rows]
    if stop-start == HD: return piece
    zero = jnp.zeros_like(piece)
    return jnp.concatenate([piece, zero] if h%2==0 else [zero, piece], axis=0)

def fwd_kernel(lo_ref, hi_ref, flip_ref, q_ref, k_ref, v_ref, w_ref, segc_ref, segr_ref, o_ref, lse_ref, near_ref, side_ref, far_ref, s_ref):
    heads = q_ref.shape[0]//HD
    i = pl.program_id(0)
    lo = lo_ref[i]; hi = hi_ref[i]; flip = flip_ref[0]
    c = LOG2E * HD**-0.5
    qz = [padded(q_ref, h, heads, slice(None)) for h in range(heads)]
    segq = segr_ref[...]
    def one(kb, peaks):
        start = pl.multiple_of(jnp.bitwise_xor(kb, flip)*BK, BK)
        same = segc_ref[pl.ds(start,BK),:] == segq
        new=[]
        for h in range(heads):
            a,b = head_cols(h, heads)
            s = lax.dot_general(k_ref[pl.ds(start,BK), a:b], qz[h], NN, preferred_element_type=f32)
            s = jnp.where(same, s, -1e30)
            s_ref[h, kb-lo] = s
            new.append(jnp.maximum(peaks[h], jnp.max(s.reshape(BK//8,8,BQ),axis=0)))
        return tuple(new)
    peaks = lax.fori_loop(lo, hi, one, tuple(jnp.full((8,BQ),-1e30,f32) for _ in range(heads)))
    peaks = [jnp.max(p,axis=0,keepdims=True)*c for p in peaks]
    def two(kb, carry):
        sums, outs = carry
        start = pl.multiple_of(jnp.bitwise_xor(kb, flip)*BK, BK)
        ns=[];no=[]
        for h in range(heads):
            p = jnp.exp2(s_ref[h, kb-lo]*c - peaks[h])
            ns.append(sums[h]+jnp.sum(p.reshape(BK//8,8,BQ),axis=0))
            no.append(outs[h]+lax.dot_general(v_ref[h*HD:(h+1)*HD, pl.ds(start,BK)], p.astype(bf16), NN, preferred_element_type=f32))
        return tuple(ns),tuple(no)
    sums, outs = lax.fori_loop(lo, hi, two, (tuple(jnp.zeros((8,BQ),f32) for _ in range(heads)), tuple(jnp.zeros((HD,BQ),f32) for _ in range(heads))))
    for h in range(heads):
        total = jnp.sum(sums[h],axis=0,keepdims=True)
        o_ref[h*HD:(h+1)*HD,:] = (outs[h]/total).astype(bf16)
        lse_ref[h:h+1,:] = peaks[h]+jnp.log2(total)
    context = jnp.transpose(o_ref[...].astype(f32)).astype(bf16)
    merged = jnp.dot(context, w_ref[...], preferred_element_type=f32).astype(bf16)
    size = near_ref.shape[0]
    per = size//BQ
    for n, ref in enumerate((near_ref, side_ref, far_ref, side_ref)):
        @pl.when(i//per==n)
        def _():
            at = pl.multiple_of((i%per)*BQ, BQ) + (size if n==3 else 0)
            ref[pl.ds(pl.multiple_of(at, BQ), BQ),:] = merged

def attn_fwd(qT,k,vT,wT,segc,segr,lo,hi,flip):
    width,length=qT.shape
    size,model=length//4,wT.shape[1]
    whole=lambda rows: pl.BlockSpec((rows,model),lambda i,*_:(0,0))
    heads=width//HD
    blocks=length//BQ
    return pl.pallas_call(
        fwd_kernel,
        out_shape=(jax.ShapeDtypeStruct((width,length),bf16), jax.ShapeDtypeStruct((heads,length),f32))+tuple(jax.ShapeDtypeStruct((n*size,model),bf16) for n in (1,2,1)),
        grid_spec=pltpu.PrefetchScalarGridSpec(num_scalar_prefetch=3, grid=(blocks,),
            in_specs=[pl.BlockSpec((width,BQ),lambda i,*_:(0,i)),
                      pl.BlockSpec((length,width),lambda i,*_:(0,0)),
                      pl.BlockSpec((width,length),lambda i,*_:(0,0)),
                      pl.BlockSpec((width,model),lambda i,*_:(model//width-1,0)),
                      pl.BlockSpec((length,1),lambda i,*_:(0,0)),
                      pl.BlockSpec((1,BQ),lambda i,*_:(0,i))],
            out_specs=[pl.BlockSpec((width,BQ),lambda i,*_:(0,i)),pl.BlockSpec((heads,BQ),lambda i,*_:(0,i)),whole(size),whole(2*size),whole(size)],
            scratch_shapes=[pltpu.VMEM((heads,length//BK,BK,BQ),f32)]),
        compiler_params=pltpu.CompilerParams(dimension_semantics=("arbitrary",),vmem_limit_bytes=60<<20),
        cost_estimate=pl.CostEstimate(flops=30*length*length*width,bytes_accessed=8*length*width,transcendentals=heads*length*length//2),
        name="attention",
    )(lo,hi,flip,qT,k,vT,wT,segc,segr)

def bwd_kernel(lo_ref, hi_ref, flip_ref, q_ref, k_ref, kT_ref, v_ref, wT_ref, g0, g1, g2, g3, o_ref, lse_ref, segc_ref, segr_ref,
               dq_ref, dk_ref, dv_ref, qb_ref, vb_ref, dk_acc, dv_acc, do_ref):
    heads = q_ref.shape[0]//HD
    width = q_ref.shape[0]
    i = pl.program_id(0)
    @pl.when(i==0)
    def _():
        dk_acc[...]=jnp.zeros_like(dk_acc); dv_acc[...]=jnp.zeros_like(dv_acc)
        qb_ref[...]=jnp.zeros_like(qb_ref)
    lo = lo_ref[i]; hi = hi_ref[i]; flip = flip_ref[0]
    scale = HD**-0.5
    per = g0.shape[0]//BQ
    for n, g_ref in enumerate((g0, g1, g2, g3)):
        @pl.when(i//per==n)
        def _():
            at = pl.multiple_of((i%per)*BQ, BQ)
            do_ref[...] = lax.dot_general(wT_ref[...], g_ref[pl.ds(at,BQ),:], NT, preferred_element_type=f32).astype(bf16)
    c = LOG2E*scale
    qz = [padded(q_ref, h, heads, slice(None)) for h in range(heads)]
    dz = [padded(do_ref, h, heads, slice(None)) for h in range(heads)]
    deltas = [jnp.sum(do_ref[h*HD:(h+1)*HD,:].astype(f32)*o_ref[h*HD:(h+1)*HD,:].astype(f32),axis=0,keepdims=True) for h in range(heads)]
    segq = segr_ref[...]
    def one(kb, dqs):
        start = pl.multiple_of(jnp.bitwise_xor(kb, flip)*BK, BK)
        rows = pl.ds(start,BK)
        same = segc_ref[rows,:] == segq
        out=[]
        parts={}
        for h in range(heads):
            a,b = head_cols(h, heads)
            s = lax.dot_general(k_ref[rows, a:b], qz[h], NN, preferred_element_type=f32)
            p = jnp.exp2(jnp.where(same, s*c - lse_ref[h:h+1,:], -1e30))
            dp = lax.dot_general(v_ref[rows, a:b], dz[h], NN, preferred_element_type=f32)
            ds = (p*((dp-deltas[h])*scale)).astype(bf16)
            dvp = lax.dot_general(p.astype(bf16), dz[h], NT, preferred_element_type=f32)
            dkp = lax.dot_general(ds, qz[h], NT, preferred_element_type=f32)
            if (a,b) in parts: parts[a,b]=(parts[a,b][0]+dkp,parts[a,b][1]+dvp)
            else: parts[a,b]=(dkp,dvp)
            out.append(dqs[h]+lax.dot_general(kT_ref[h*HD:(h+1)*HD, rows], ds, NN, preferred_element_type=f32))
        for (a,b),(dkp,dvp) in parts.items():
            dk_acc[rows,a:b]+=dkp
            dv_acc[rows,a:b]+=dvp
        return tuple(out)
    dqs = lax.fori_loop(lo,hi,one,tuple(jnp.zeros((HD,BQ),f32) for _ in range(heads)))
    for h in range(heads):
        dq_ref[h*HD:(h+1)*HD,:]=dqs[h].astype(bf16)
        part = dqs[h][:,:128]
        for n in range(128,BQ,128): part=part+dqs[h][:,n:n+128]
        qb_ref[h*HD:(h+1)*HD,:]+=part
    @pl.when(i==pl.num_programs(0)-1)
    def _():
        dk_ref[...]=dk_acc[...].astype(bf16)
        dv_ref[...]=dv_acc[...].astype(bf16)
        vb_ref[...]=jnp.sum(dv_acc[...].reshape(dv_acc.shape[0]//8,8,width),axis=0)

def attn_bwd(qT,k,kT,v,wT,grads,oT,lse,segc,segr,lo,hi,flip):
    width,length=qT.shape
    heads=width//HD
    blocks=length//BQ
    col=pl.BlockSpec((width,BQ),lambda i,*_:(0,i))
    row=pl.BlockSpec((length,width),lambda i,*_:(0,0))
    return pl.pallas_call(
        bwd_kernel,
        out_shape=(jax.ShapeDtypeStruct((width,length),bf16), jax.ShapeDtypeStruct((length,width),bf16), jax.ShapeDtypeStruct((length,width),bf16), jax.ShapeDtypeStruct((width,128),f32), jax.ShapeDtypeStruct((8,width),f32)),
        grid_spec=pltpu.PrefetchScalarGridSpec(num_scalar_prefetch=3, grid=(blocks,),
            in_specs=[col,row,pl.BlockSpec((width,length),lambda i,*_:(0,0)),row,pl.BlockSpec((width,wT.shape[1]),lambda i,*_:(wT.shape[1]//width-1,0))]+[pl.BlockSpec(g.shape,lambda i,*_:(0,0)) for g in grads]+[col,
                      pl.BlockSpec((heads,BQ),lambda i,*_:(0,i)),
                      pl.BlockSpec((length,1),lambda i,*_:(0,0)),
                      pl.BlockSpec((1,BQ),lambda i,*_:(0,i))],
            out_specs=[col,row,row,pl.BlockSpec((width,128),lambda i,*_:(0,0)),pl.BlockSpec((8,width),lambda i,*_:(0,0))],
            scratch_shapes=[pltpu.VMEM((length,width),f32),pltpu.VMEM((length,width),f32),pltpu.VMEM((width,BQ),bf16)]),
        compiler_params=pltpu.CompilerParams(dimension_semantics=("arbitrary",),vmem_limit_bytes=60<<20),
        cost_estimate=pl.CostEstimate(flops=38*length*length*width,bytes_accessed=20*length*width,transcendentals=heads*length*length//2),
        name="attention_back",
    )(lo,hi,flip,qT,k,kT,v,wT,*grads,oT,lse,segc,segr)

def spans(seg_row):
    length=seg_row.shape[0]
    first=seg_row[::BQ]; last=seg_row[BQ-1::BQ]
    lo=jnp.sum(seg_row[None,:]<first[:,None],axis=1,dtype=jnp.int32)//BK
    hi=(jnp.sum(seg_row[None,:]<=last[:,None],axis=1,dtype=jnp.int32)+BK-1)//BK
    return lo,hi

EPSILON=1e-12
T=256
RC=32

def row_stats(values):
    centre=jnp.mean(values,axis=1,keepdims=True)
    centred=values-centre
    spread=jnp.mean(centred*centred,axis=1,keepdims=True)
    scale=lax.rsqrt(spread+EPSILON)
    return centred*scale, scale

def fold(values):
    return jnp.sum(values.reshape(values.shape[0]//8,8,values.shape[1]),axis=0)

def ffn_kernel(tok_ref, a0_ref, a1_ref, a2_ref, cot_ref, vec_ref, be_ref,
               wa_ref,wb_ref,
               out_ref, gm_ref, gml_ref, vg_ref, eb_ref, ga_ref,gb_ref,
               we, ws, hl, hlT, hid, xhat, rs1, act, gp, acc, sl, slT, gsum, il, de, dt, wsem, osem):
    rows, width = tok_ref.shape
    blocks,_,units=we.shape
    es=[(wa_ref,wb_ref)[r%2].at[:,(r//2)*2*units:(r//2+1)*2*units] for r in range(blocks)]
    ds=[(ga_ref,gb_ref)[r%2].at[:,(r//2)*2*units:(r//2+1)*2*units] for r in range(blocks)]
    for r in range(blocks):
        pltpu.make_async_copy(es[r].at[:,0:units],we.at[r],wsem.at[0,r]).start()
        pltpu.make_async_copy(es[r].at[:,units:],ws.at[r],wsem.at[1,r]).start()
    mb=vec_ref[0:1,:]; g1=vec_ref[1:2,:]; b1=vec_ref[2:3,:]; sb=vec_ref[3:4,:]; g2=vec_ref[4:5,:]; b2=vec_ref[5:6,:]
    def first(i,_):
        at=pl.ds(pl.multiple_of(i*RC,RC),RC)
        mixed=tok_ref[at,:].astype(f32)+(a0_ref[at,:].astype(f32)+a1_ref[at,:].astype(f32)+a2_ref[at,:].astype(f32))+mb
        z,scale=row_stats(mixed)
        xhat[at,:]=z
        rs1[at,:]=jnp.broadcast_to(scale,(RC,128))
        h=z*g1+b1
        hid[at,:]=h
        hl[at,:]=h.astype(bf16)
        acc[at,:]=jnp.zeros((RC,width),f32)
        return 0
    lax.fori_loop(0,rows//RC,first,0,unroll=4)
    def turn(src,dst):
        def go(i,_):
            at=pl.multiple_of(i*T,T)
            dst[:,pl.ds(at,T)]=jnp.transpose(src[pl.ds(at,T),:].astype(f32)).astype(bf16)
            return 0
        lax.fori_loop(0,rows//T,go,0)
    turn(hl,hlT)
    TG=768; TM=min(512,rows); per=units//T; mt=rows//TM
    def forward(r,_):
        for k in range(blocks):
            @pl.when(r==k)
            def _():
                pltpu.make_async_copy(es[k].at[:,0:units],we.at[k],wsem.at[0,k]).wait()
        def tile(j,_):
            n=pl.multiple_of((j//mt)*T,T); m=pl.multiple_of((j%mt)*TM,TM)
            u=lax.dot_general(hl[pl.ds(m,TM),:],we[r,:,pl.ds(n,T)],NN,preferred_element_type=f32)+be_ref[pl.ds(r,1),pl.ds(n,T)]
            cdf=0.5+0.5*lax.erf(u*(0.5**0.5))
            act[r,pl.ds(m,TM),pl.ds(n,T)]=(u*cdf).astype(bf16)
            gp[r,pl.ds(m,TM),pl.ds(n,T)]=cdf+u*(jnp.exp(-0.5*u*u)*0.3989422804014327)
            return 0
        lax.fori_loop(0,per*mt,tile,0,unroll=3)
        for k in range(blocks):
            @pl.when(r==k)
            def _():
                pltpu.make_async_copy(es[k].at[:,units:],ws.at[k],wsem.at[1,k]).wait()
        def shrink(j,_):
            n=pl.multiple_of((j//mt)*T,T); m=pl.multiple_of((j%mt)*TM,TM)
            acc[pl.ds(m,TM),pl.ds(n,T)]+=lax.dot_general(act[r,pl.ds(m,TM),:],ws[r,pl.ds(n,T),:],NT,preferred_element_type=f32)
            return 0
        lax.fori_loop(0,(width//T)*mt,shrink,0,unroll=3)
        return 0
    lax.fori_loop(0,blocks,forward,0)
    def second(i,sums):
        at=pl.ds(pl.multiple_of(i*RC,RC),RC)
        summed=hid[at,:]+acc[at,:]+sb
        z,scale=row_stats(summed)
        out_ref[at,:]=(z*g2+b2).astype(bf16)
        cot=cot_ref[at,:].astype(f32)
        e=cot*g2
        g=(e-jnp.mean(e,axis=1,keepdims=True)-z*jnp.mean(e*z,axis=1,keepdims=True))*scale
        gsum[at,:]=g
        sl[at,:]=g.astype(bf16)
        acc[at,:]=g
        return (sums[0]+fold(cot*z),sums[1]+fold(cot),sums[2]+fold(g))
    zero=jnp.zeros((8,width),f32)
    sg,sh,sbg=lax.fori_loop(0,rows//RC,second,(zero,zero,zero),unroll=4)
    turn(sl,slT)
    def sent(r,slot,k):
        return (pltpu.make_async_copy(de.at[slot],ds[k].at[:,0:units],osem.at[0,slot]),pltpu.make_async_copy(dt.at[slot],ds[k].at[:,units:],osem.at[1,slot]))
    def backward(r,_):
        slot=r%2
        def tile(j,_):
            n=pl.multiple_of((j//mt)*T,T); m=pl.multiple_of((j%mt)*TM,TM)
            ga=lax.dot_general(sl[pl.ds(m,TM),:],ws[r,:,pl.ds(n,T)],NN,preferred_element_type=f32)
            gi=ga*gp[r,pl.ds(m,TM),pl.ds(n,T)]
            il[pl.ds(m,TM),pl.ds(n,T)]=gi.astype(bf16)
            part=fold(gi)
            eb_ref[r,:,pl.ds(n,T)]=jnp.where(m==0,part,eb_ref[r,:,pl.ds(n,T)]+part)
            return 0
        lax.fori_loop(0,per*mt,tile,0,unroll=3)
        def back(j,_):
            n=pl.multiple_of((j//mt)*T,T); m=pl.multiple_of((j%mt)*TM,TM)
            acc[pl.ds(m,TM),pl.ds(n,T)]+=lax.dot_general(il[pl.ds(m,TM),:],we[r,pl.ds(n,T),:],NT,preferred_element_type=f32)
            return 0
        lax.fori_loop(0,(width//T)*mt,back,0,unroll=3)
        for k in range(2,blocks):
            @pl.when(r==k)
            def _():
                for c in sent(r,k%2,k-2): c.wait()
        def grads(j,_):
            n=pl.multiple_of((j//(width//TG))*T,T); m=pl.multiple_of((j%(width//TG))*TG,TG)
            dt[slot,pl.ds(m,TG),pl.ds(n,T)]=lax.dot_general(slT[pl.ds(m,TG),:],act[r,:,pl.ds(n,T)],NN,preferred_element_type=f32).astype(bf16)
            de[slot,pl.ds(m,TG),pl.ds(n,T)]=lax.dot_general(hlT[pl.ds(m,TG),:],il[:,pl.ds(n,T)],NN,preferred_element_type=f32).astype(bf16)
            return 0
        lax.fori_loop(0,(width//TG)*per,grads,0,unroll=3)
        for k in range(blocks):
            @pl.when(r==k)
            def _():
                for c in sent(r,k%2,k): c.start()
        return 0
    lax.fori_loop(0,blocks,backward,0)
    def last(i,sums):
        at=pl.ds(pl.multiple_of(i*RC,RC),RC)
        g=acc[at,:]
        z=xhat[at,:]
        e=g*g1
        gm=(e-jnp.mean(e,axis=1,keepdims=True)-z*jnp.mean(e*z,axis=1,keepdims=True))*rs1[at,0:1]
        gm_ref[at,:]=gm
        gml_ref[at,:]=gm.astype(bf16)
        return (sums[0]+fold(g*z),sums[1]+fold(g),sums[2]+fold(gm))
    fg,fs,mbg=lax.fori_loop(0,rows//RC,last,(zero,zero,zero),unroll=4)
    for n,v in enumerate((mbg,fg,fs,sbg,sg,sh)):
        vg_ref[n]=v
    for k in range(max(0,blocks-2),blocks):
        for c in sent(k,k%2,k): c.wait()

def ffn(tok,a0,a1,a2,cot,vec,be,w_own,w_other):
    rows,width=tok.shape; blocks,units=be.shape
    v=pl.BlockSpec(memory_space=pltpu.VMEM); h=pl.BlockSpec(memory_space=pltpu.HBM)
    g=jax.ShapeDtypeStruct((width,blocks*units),bf16)
    V=pltpu.VMEM
    return pl.pallas_call(
        ffn_kernel,
        out_shape=(jax.ShapeDtypeStruct((rows,width),bf16),jax.ShapeDtypeStruct((rows,width),f32),jax.ShapeDtypeStruct((rows,width),bf16),
                   jax.ShapeDtypeStruct((6,8,width),f32),jax.ShapeDtypeStruct((blocks,8,units),f32))+(g,g),
        in_specs=[v]*7+[h]*2,
        out_specs=[v]*5+[h]*2,
        scratch_shapes=[V((blocks,width,units),bf16),V((blocks,width,units),bf16),
            V((rows,width),bf16),V((width,rows),bf16),V((rows,width),f32),V((rows,width),f32),V((rows,128),f32),
            V((blocks,rows,units),bf16),V((blocks,rows,units),f32),V((rows,width),f32),V((rows,width),bf16),V((width,rows),bf16),V((rows,width),f32),
            V((rows,units),bf16),V((2,width,units),bf16),V((2,width,units),bf16),
            pltpu.SemaphoreType.DMA((2,blocks)),pltpu.SemaphoreType.DMA((2,2))],
        compiler_params=pltpu.CompilerParams(vmem_limit_bytes=60<<20),
        cost_estimate=pl.CostEstimate(flops=30*rows*width*units*blocks,bytes_accessed=8*blocks*width*units,transcendentals=2*rows*units*blocks),
        name="feed_forward",
    )(tok,a0,a1,a2,cot,vec,be,w_own,w_other)


def proj_kernel(home_ref, x0, x1, x2, x3, wa_ref, wb_ref, bq_ref, bvc_ref, bvr_ref,
                q_ref, kT_ref, vT_ref, k_ref, v_ref, wT, w_ref, wk, wv, x_buf, sem, x_sem):
    model = w_ref.shape[0]
    count, rows = sem.shape[0], model // sem.shape[0]
    width = q_ref.shape[0]
    home = home_ref[0]
    step = pl.program_id(0)
    def copy(r):
        src = (wa_ref, wb_ref)[r % 2].at[(r // 2) * rows : (r // 2 + 1) * rows]
        at = pl.multiple_of(jnp.bitwise_xor(home, r) * rows, rows)
        return pltpu.make_async_copy(src, w_ref.at[pl.ds(at, rows)], sem.at[r])
    if wa_ref.shape[0] == model:
        count = 1
        copy = lambda r: pltpu.make_async_copy(wa_ref, w_ref, sem.at[r])
    fetch = [pltpu.make_async_copy(x, x_buf.at[n], x_sem.at[n]) for n, x in enumerate((x0, x1, x2, x3))]
    @pl.when(step == 0)
    def _():
        for r in range(count):
            copy(r).start()
        for x in fetch:
            x.start()
        for r in range(count):
            copy(r).wait()
        def turn(i, _):
            at = pl.multiple_of(i * 256, 256)
            wT[:, pl.ds(at, 256)] = jnp.transpose(w_ref[pl.ds(at, 256), :].astype(f32)).astype(bf16)
            return 0
        lax.fori_loop(0, model // 256, turn, 0)
        wk[...] = w_ref[:, width : 2 * width]
        wv[...] = w_ref[:, 2 * width : 3 * width]
    for n, x in enumerate(fetch):
        @pl.when(step == n)
        def _():
            x.wait()
    x = x_buf[step]
    k_ref[...] = jnp.dot(x, wk[...], preferred_element_type=f32).astype(bf16)
    v_ref[...] = (jnp.dot(x, wv[...], preferred_element_type=f32) + bvr_ref[...]).astype(bf16)
    q_ref[...] = (lax.dot_general(wT[0:width], x, NT, preferred_element_type=f32) + bq_ref[...]).astype(bf16)
    kT_ref[...] = lax.dot_general(wT[width : 2 * width], x, NT, preferred_element_type=f32).astype(bf16)
    vT_ref[...] = (lax.dot_general(wT[2 * width : 3 * width], x, NT, preferred_element_type=f32) + bvc_ref[...]).astype(bf16)


def project(home, tokens, wa, wb, count, bq, bv):
    size, model = tokens[0].shape
    length = 4 * size
    width = bq.shape[0]
    hbm = pl.BlockSpec(memory_space=pltpu.HBM)
    column = pl.BlockSpec((width, 1), lambda i: (0, 0))
    tall = jax.ShapeDtypeStruct((length, width), bf16)
    flat = jax.ShapeDtypeStruct((width, length), bf16)
    across = pl.BlockSpec((width, size), lambda i: (0, i))
    down = pl.BlockSpec((size, width), lambda i: (i, 0))
    return pl.pallas_call(
        proj_kernel,
        grid=(4,),
        out_shape=(flat, flat, flat, tall, tall, jax.ShapeDtypeStruct((model, model), bf16)),
        in_specs=[pl.BlockSpec(memory_space=pltpu.SMEM)] + [hbm] * 6 + [column, column, pl.BlockSpec((1, width), lambda i: (0, 0))],
        out_specs=[across, across, across, down, down, pl.BlockSpec((model, model), lambda i: (0, 0))],
        scratch_shapes=[pltpu.VMEM((model, model), bf16), pltpu.VMEM((model, width), bf16), pltpu.VMEM((model, width), bf16),
            pltpu.VMEM((4, size, model), bf16), pltpu.SemaphoreType.DMA((count,)), pltpu.SemaphoreType.DMA((4,))],
        compiler_params=pltpu.CompilerParams(dimension_semantics=("arbitrary",), vmem_limit_bytes=60 << 20),
        cost_estimate=pl.CostEstimate(flops=30 * length * model * width, bytes_accessed=4 * length * model, transcendentals=0),
        name="projection",
    )(home, *tokens, wa, wb, bq[:, None], bv[:, None], bv[None, :])


def grads_kernel(home_ref, x0, x1, x2, x3, g0, g1, g2, g3, c_ref, q_ref, k_ref, v_ref, *rest):
    *outs, acc, xT, gT = rest
    home = home_ref[0]
    width = q_ref.shape[0]
    model = x0.shape[1]
    for n, (x_ref, g_ref) in enumerate(zip((x0, x1, x2, x3), (g0, g1, g2, g3))):
        size = x_ref.shape[0]
        rows = slice(n * size, (n + 1) * size)
        def turn(i, _):
            at = pl.multiple_of(i * 256, 256)
            xT[:, pl.ds(at, 256)] = jnp.transpose(x_ref[pl.ds(at, 256), :].astype(f32)).astype(bf16)
            gT[:, pl.ds(at, 256)] = jnp.transpose(g_ref[pl.ds(at, 256), :].astype(f32)).astype(bf16)
            return 0
        lax.fori_loop(0, size // 256, turn, 0)
        def part(i, _):
            at = pl.ds(pl.multiple_of(i * 256, 256), 256)
            x = xT[at, :]
            pieces = (
                lax.dot_general(x, q_ref[:, rows], NT, preferred_element_type=f32),
                jnp.dot(x, k_ref[rows, :], preferred_element_type=f32),
                jnp.dot(x, v_ref[rows, :], preferred_element_type=f32),
                lax.dot_general(gT[at, :], c_ref[:, rows], NT, preferred_element_type=f32),
            )
            for m, piece in enumerate(pieces):
                acc[m, at, :] = piece if n == 0 else acc[m, at, :] + piece
            return 0
        lax.fori_loop(0, model // 256, part, 0)
    if len(outs) == 1:
        for m in range(4):
            outs[0][:, m * width : (m + 1) * width] = acc[m].astype(bf16)
        return
    rows = model // 8
    for r in range(8):
        at = pl.ds(pl.multiple_of(jnp.bitwise_xor(home, r) * rows, rows), rows)
        to = slice(r // 2 * rows, (r // 2 + 1) * rows)
        for m in range(4):
            outs[r % 2][to, m * width : (m + 1) * width] = acc[m, at, :].astype(bf16)


def attn_grads(home, count, tokens, grads, contextT, dqT, dk, dv):
    size, model = tokens[0].shape
    width = dqT.shape[0]
    v = pl.BlockSpec(memory_space=pltpu.VMEM)
    parts = 2 if count == 8 else 1
    return pl.pallas_call(
        grads_kernel,
        out_shape=[jax.ShapeDtypeStruct((model // parts, 4 * width), bf16)] * parts,
        in_specs=[pl.BlockSpec(memory_space=pltpu.SMEM)] + [v] * 12,
        out_specs=[v] * parts,
        scratch_shapes=[pltpu.VMEM((4, model, width), f32), pltpu.VMEM((model, size), bf16), pltpu.VMEM((model, size), bf16)],
        compiler_params=pltpu.CompilerParams(vmem_limit_bytes=60 << 20),
        cost_estimate=pl.CostEstimate(flops=120 * size * model * width, bytes_accessed=24 * size * model, transcendentals=0),
        name="projection_grads",
    )(home, *tokens, *grads, contextT, dqT, dk, dv)


def hop(value, bit):
    count = lax.axis_size("dp")
    return lax.ppermute(value, "dp", [(i, i ^ bit) for i in range(count)])


def gather_shards(own):
    count = lax.axis_size("dp")
    if count != 8:
        every = lax.all_gather(own, "dp", axis=0, tiled=True)
        return every, every
    even = jnp.concatenate([own] + [hop(own, bit) for bit in (2, 4, 6)], axis=0)
    return even, hop(even, 1)


def scatter_shards(parts):
    if len(parts) == 1:
        count = lax.axis_size("dp")
        swapped = lax.all_to_all(parts[0], "dp", 0, 0, tiled=True)
        return jnp.sum(swapped.reshape(count, -1, swapped.shape[1]).astype(f32), axis=0)
    even = (parts[0].astype(f32) + hop(parts[1], 1).astype(f32)).astype(bf16)
    even = even.reshape(4, -1, even.shape[1])
    return even[0].astype(f32) + sum(hop(even[n], 2 * n).astype(f32) for n in (1, 2, 3))


def later(value, *markers, flops=0):
    anywhere = pl.BlockSpec(memory_space=pl.ANY)
    return pl.pallas_call(
        lambda *refs: None,
        out_shape=jax.ShapeDtypeStruct(value.shape, value.dtype),
        in_specs=[anywhere] * (1 + len(markers)),
        out_specs=anywhere,
        input_output_aliases={0: 0},
        cost_estimate=pl.CostEstimate(flops=flops, bytes_accessed=0, transcendentals=0),
        name="later",
    )(value, *markers)


def exchange(value, bit):
    return lax.ppermute(value, "tensor", [(i, i ^ bit) for i in range(4)])


def row_blocks(own):
    across = exchange(own, 2)
    return [own, exchange(own, 1), across, exchange(across, 1)]


def gather_rows(own):
    return jnp.concatenate(row_blocks(own), axis=0)


def scatter_pieces(near, side, far):
    rows = near.shape[0]
    beside = exchange(side, 1)
    ahead = (far.astype(f32) + beside[rows:].astype(f32)).astype(bf16)
    return (near, beside[:rows], exchange(ahead, 2)), ahead


def scatter_rows(partial):
    rows = partial.shape[0] // 4
    low = partial.astype(bf16)
    piece = lambda r: low[r * rows : (r + 1) * rows]
    return scatter_pieces(piece(0), jnp.concatenate([piece(1), piece(3)], axis=0), piece(2))


def on_device(
    tokens,
    segments,
    query_proj,
    query_bias,
    key_proj,
    value_proj,
    value_bias,
    merge_proj,
    merge_bias,
    first_gain,
    first_shift,
    expand_proj,
    expand_bias,
    shrink_proj,
    shrink_bias,
    second_gain,
    second_shift,
    cotangent,
):
    everyone = ("dp", "tensor")
    part = lax.axis_index("tensor")
    dp = lax.axis_size("dp")
    world = dp * 4
    width = query_proj.shape[1]
    units = expand_proj.shape[1]
    model = width * 4
    share = model // world
    unit_share = units * 4 // world

    shard = jnp.concatenate([query_proj, key_proj, value_proj, merge_proj.T], axis=1)
    shards = gather_shards(shard)
    wide = jnp.concatenate([expand_proj, shrink_proj.T], axis=1)
    wide = jnp.concatenate([wide, exchange(wide, 2)], axis=1)
    w_own = lax.all_gather(wide, "dp", axis=0, tiled=True)
    own = jnp.concatenate(
        [query_bias, value_bias, merge_bias, first_gain, first_shift, shrink_bias, second_gain, second_shift, expand_bias]
    )
    rows = tokens.shape[0]
    count = own.shape[0]
    own = jnp.concatenate([own, segments.reshape(-1).astype(f32)])
    slots = -(-own.shape[0] // 1024) * 8
    own = jnp.pad(own, (0, slots * 128 - own.shape[0])).reshape(1, slots, 128)
    vectors = lax.all_to_all(jnp.broadcast_to(own, (world, slots, 128)), everyone, 0, 0, tiled=True)
    vectors = vectors.reshape(world, slots * 128)
    whole = [vectors[:, n * share : (n + 1) * share].reshape(model) for n in range(8)]
    unit_bias = vectors[:, 8 * share : 8 * share + unit_share].reshape(4, units)
    flips = jnp.bitwise_xor(jnp.arange(4), part)
    seg = lax.dynamic_slice(vectors, (lax.axis_index("dp") * 4, count), (4, rows))
    seg = jnp.take(seg, flips, axis=0).reshape(-1).astype(jnp.int32)
    unit_bias = jnp.take(unit_bias, flips, axis=0)
    query_b = lax.dynamic_slice_in_dim(whole[0], part * width, width)
    value_b = lax.dynamic_slice_in_dim(whole[1], part * width, width)
    rows_b = jnp.stack(whole[2:8])

    blocks = row_blocks(tokens)
    segc, segr = seg[:, None], seg[None, :]
    lo, hi = spans(seg)
    flip = (part * (tokens.shape[0] // BK)).astype(jnp.int32).reshape(1)
    home = lax.axis_index("dp").astype(jnp.int32).reshape(1)
    query_t, key_t, value_t, keys, values, attn_wt = project(home, blocks, *shards, dp, query_b, value_b)
    wq, wk, wv, _ = (attn_wt[n * width : (n + 1) * width] for n in range(4))
    dot = lambda a, b, dims: lax.dot_general(a, b, dims, preferred_element_type=f32)
    context_t, logsum, *pieces = attn_fwd(query_t, keys, value_t, attn_wt, segc, segr, lo, hi, flip)
    (a0, a1, a2), ahead = scatter_pieces(*pieces)

    w_other = exchange(w_own, 1)
    rows_b = later(rows_b, ahead, flops=7 * 10**10)
    out = ffn(tokens, a0, a1, a2, cotangent, rows_b, unit_bias, w_own, w_other)
    output, grad_mixed, mixed_low, row_sums, unit_sums = out[:5]
    g_own, g_other = out[5:]

    across = exchange(mixed_low, 2)
    beside = exchange(mixed_low, 1)
    wide_local = (g_own.astype(f32) + exchange(g_other, 1).astype(f32)).astype(bf16)
    mixed_blocks = [mixed_low, beside, across, exchange(across, 1)]
    wide_local = lax.psum_scatter(wide_local, "dp", scatter_dimension=0, tiled=True)
    dq_t, dk, dv, q_sums, v_sums = attn_bwd(
        query_t, keys, key_t, values, attn_wt, mixed_blocks, context_t, logsum, segc, segr, lo, hi, flip
    )
    attn_local = attn_grads(home, dp, blocks, mixed_blocks, context_t, dq_t, dk, dv)
    attn_grad = scatter_shards(attn_local)
    dq_late = later(dq_t, attn_local[0])
    total = dot(dq_late, wq, TN) + dot(dk, wk, NN) + dot(dv, wv, NN)
    (b0, b1, b2), _ = scatter_rows(total)
    tokens_grad = (grad_mixed + (b0.astype(f32) + b1.astype(f32) + b2.astype(f32))).astype(bf16)
    wide_far = exchange(wide_local[:, 2 * units :], 2)
    querygrad, keygrad, valuegrad, mergegrad = (attn_grad[:, n * width : (n + 1) * width] for n in range(4))
    wide_grad = wide_local[:, : 2 * units].astype(f32) + wide_far.astype(f32)
    expandgrad = wide_grad[:, :units]
    shrinkgrad = wide_grad[:, units:].T

    zero = jnp.zeros((4, width), f32)
    q_all = lax.dynamic_update_slice(zero, jnp.sum(q_sums, axis=1)[None], (part, 0)).reshape(world, share)
    v_all = lax.dynamic_update_slice(zero, jnp.sum(v_sums, axis=0)[None], (part, 0)).reshape(world, share)
    u_all = jnp.take(jnp.sum(unit_sums, axis=1), flips, axis=0).reshape(world, unit_share)
    row_all = [v.reshape(world, share) for v in jnp.sum(row_sums, axis=1)]
    send = jnp.concatenate([q_all, v_all] + row_all + [u_all], axis=1)
    send = jnp.pad(send, ((0, 0), (0, slots * 128 - send.shape[1]))).reshape(world, slots, 128)
    got = jnp.sum(lax.all_to_all(send, everyone, 0, 0, tiled=True).reshape(world, slots * 128), axis=0)
    small = [got[n * share : (n + 1) * share] for n in range(8)]
    qbiasgrad, vbiasgrad, mbiasgrad, fgaingrad, fshiftgrad, sbiasgrad, sgaingrad, sshiftgrad = small
    ebiasgrad = got[8 * share : 8 * share + unit_share]
    return (
        output,
        tokens_grad,
        querygrad,
        qbiasgrad,
        keygrad,
        valuegrad,
        vbiasgrad,
        mergegrad.T,
        mbiasgrad,
        fgaingrad,
        fshiftgrad,
        expandgrad,
        ebiasgrad,
        shrinkgrad,
        sbiasgrad,
        sgaingrad,
        sshiftgrad,
    )


def solution(mesh):
    return jax.shard_map(
        on_device,
        mesh=mesh,
        in_specs=(
            P(("dp", "tensor"), None),
            P("dp", "tensor"),
            P("dp", "tensor"),
            P(("dp", "tensor")),
            P("dp", "tensor"),
            P("dp", "tensor"),
            P(("dp", "tensor")),
            P("tensor", "dp"),
            P(("dp", "tensor")),
            P(("dp", "tensor")),
            P(("dp", "tensor")),
            P("dp", "tensor"),
            P(("dp", "tensor")),
            P("tensor", "dp"),
            P(("dp", "tensor")),
            P(("dp", "tensor")),
            P(("dp", "tensor")),
            P(("dp", "tensor"), None),
        ),
        out_specs=(
            P(("dp", "tensor"), None),
            P(("dp", "tensor"), None),
            P("dp", "tensor"),
            P(("dp", "tensor")),
            P("dp", "tensor"),
            P("dp", "tensor"),
            P(("dp", "tensor")),
            P("tensor", "dp"),
            P(("dp", "tensor")),
            P(("dp", "tensor")),
            P(("dp", "tensor")),
            P("dp", "tensor"),
            P(("dp", "tensor")),
            P("tensor", "dp"),
            P(("dp", "tensor")),
            P(("dp", "tensor")),
            P(("dp", "tensor")),
        ),
        check_vma=False,
    )
```

```python
import functools

import jax
import jax.numpy as jnp
from jax import lax
from jax.sharding import PartitionSpec as P
from jax.experimental import pallas as pl
from jax.experimental.pallas import tpu as pltpu

HD=64
BQ=512
BK=512
LOG2E=1.4426950408889634
NN=(((1,),(0,)),((),()))
NT=(((1,),(1,)),((),()))
TN=(((0,),(0,)),((),()))
f32=jnp.float32; bf16=jnp.bfloat16

def head_cols(h, heads):
    start=(h//2)*128
    stop=min(start+128, heads*HD)
    return start, stop

def padded(ref, h, heads, rows):
    start, stop = head_cols(h, heads)
    piece = ref[h*HD:(h+1)*HD, rows]
    if stop-start == HD: return piece
    zero = jnp.zeros_like(piece)
    return jnp.concatenate([piece, zero] if h%2==0 else [zero, piece], axis=0)

def fwd_kernel(start_at, lo_ref, hi_ref, flip_ref, q_ref, k_ref, v_ref, w_ref, segc_ref, segr_ref, o_ref, lse_ref, first_ref, second_ref, s_ref):
    heads = q_ref.shape[0]//HD
    i = pl.program_id(0)
    lo = lo_ref[start_at+i]; hi = hi_ref[start_at+i]; flip = flip_ref[0]
    c = LOG2E * HD**-0.5
    qz = [padded(q_ref, h, heads, slice(None)) for h in range(heads)]
    segq = segr_ref[...]
    def one(kb, peaks):
        start = pl.multiple_of(jnp.bitwise_xor(kb, flip)*BK, BK)
        same = segc_ref[pl.ds(start,BK),:] == segq
        new=[]
        for h in range(heads):
            a,b = head_cols(h, heads)
            s = lax.dot_general(k_ref[pl.ds(start,BK), a:b], qz[h], NN, preferred_element_type=f32)
            s = jnp.where(same, s, -1e30)
            s_ref[h, kb-lo] = s
            new.append(jnp.maximum(peaks[h], jnp.max(s.reshape(BK//8,8,BQ),axis=0)))
        return tuple(new)
    peaks = lax.fori_loop(lo, hi, one, tuple(jnp.full((8,BQ),-1e30,f32) for _ in range(heads)))
    peaks = [jnp.max(p,axis=0,keepdims=True)*c for p in peaks]
    def two(kb, carry):
        sums, outs = carry
        start = pl.multiple_of(jnp.bitwise_xor(kb, flip)*BK, BK)
        ns=[];no=[]
        for h in range(heads):
            p = jnp.exp2(s_ref[h, kb-lo]*c - peaks[h])
            ns.append(sums[h]+jnp.sum(p.reshape(BK//8,8,BQ),axis=0))
            no.append(outs[h]+lax.dot_general(v_ref[h*HD:(h+1)*HD, pl.ds(start,BK)], p.astype(bf16), NN, preferred_element_type=f32))
        return tuple(ns),tuple(no)
    sums, outs = lax.fori_loop(lo, hi, two, (tuple(jnp.zeros((8,BQ),f32) for _ in range(heads)), tuple(jnp.zeros((HD,BQ),f32) for _ in range(heads))))
    for h in range(heads):
        total = jnp.sum(sums[h],axis=0,keepdims=True)
        o_ref[h*HD:(h+1)*HD,:] = (outs[h]/total).astype(bf16)
        lse_ref[h:h+1,:] = peaks[h]+jnp.log2(total)
    context = jnp.transpose(o_ref[...].astype(f32)).astype(bf16)
    merged = jnp.dot(context, w_ref[...], preferred_element_type=f32).astype(bf16)
    per = first_ref.shape[0]//BQ
    for n, ref in enumerate((first_ref, second_ref)):
        @pl.when(i//per==n)
        def _():
            ref[pl.ds(pl.multiple_of((i%per)*BQ, BQ), BQ),:] = merged

def attn_fwd(second,qT,k,vT,wT,segc,segr,lo,hi,flip):
    width,length=qT.shape
    size,model=length//4,wT.shape[1]
    heads=width//HD
    blocks=length//BQ//2
    first=blocks*second
    col=pl.BlockSpec((width,BQ),lambda i,*_:(0,first+i))
    whole=pl.BlockSpec((size,model),lambda i,*_:(0,0))
    part=jax.ShapeDtypeStruct((size,model),bf16)
    return pl.pallas_call(
        functools.partial(fwd_kernel,first),
        out_shape=(jax.ShapeDtypeStruct((width,length//2),bf16), jax.ShapeDtypeStruct((8,length//2),f32), part, part),
        grid_spec=pltpu.PrefetchScalarGridSpec(num_scalar_prefetch=3, grid=(blocks,),
            in_specs=[col,
                      pl.BlockSpec((length,width),lambda i,*_:(0,0)),
                      pl.BlockSpec((width,length),lambda i,*_:(0,0)),
                      pl.BlockSpec((width,model),lambda i,*_:(model//width-1,0)),
                      pl.BlockSpec((length,1),lambda i,*_:(0,0)),
                      pl.BlockSpec((1,BQ),lambda i,*_:(0,first+i))],
            out_specs=[pl.BlockSpec((width,BQ),lambda i,*_:(0,i)),pl.BlockSpec((8,BQ),lambda i,*_:(0,i)),whole,whole],
            scratch_shapes=[pltpu.VMEM((heads,length//BK,BK,BQ),f32)]),
        compiler_params=pltpu.CompilerParams(dimension_semantics=("arbitrary",),vmem_limit_bytes=60<<20),
        cost_estimate=pl.CostEstimate(flops=25*length*length*width,bytes_accessed=4*length*width,transcendentals=heads*length*length//4),
        name="attention",
    )(lo,hi,flip,qT,k,vT,wT,segc,segr)

def bwd_kernel(start_at, lo_ref, hi_ref, flip_ref, q_ref, k_ref, kT_ref, v_ref, wT_ref, g0, g1, o_ref, lse_ref, segc_ref, segr_ref, *rest):
    if start_at:
        dk_old, dv_old, dq_ref, dk_ref, dv_ref, qb_ref, vb_ref, dk_acc, dv_acc, do_ref = rest
    else:
        dq_ref, dk_ref, dv_ref, qb_ref, dk_acc, dv_acc, do_ref = rest
    heads = q_ref.shape[0]//HD
    width = q_ref.shape[0]
    i = pl.program_id(0)
    @pl.when(i==0)
    def _():
        dk_acc[...]=jnp.zeros_like(dk_acc); dv_acc[...]=jnp.zeros_like(dv_acc)
        qb_ref[...]=jnp.zeros_like(qb_ref)
    lo = lo_ref[start_at+i]; hi = hi_ref[start_at+i]; flip = flip_ref[0]
    scale = HD**-0.5
    per = g0.shape[0]//BQ
    for n, g_ref in enumerate((g0, g1)):
        @pl.when(i//per==n)
        def _():
            at = pl.multiple_of((i%per)*BQ, BQ)
            do_ref[...] = lax.dot_general(wT_ref[...], g_ref[pl.ds(at,BQ),:], NT, preferred_element_type=f32).astype(bf16)
    c = LOG2E*scale
    qz = [padded(q_ref, h, heads, slice(None)) for h in range(heads)]
    dz = [padded(do_ref, h, heads, slice(None)) for h in range(heads)]
    deltas = [jnp.sum(do_ref[h*HD:(h+1)*HD,:].astype(f32)*o_ref[h*HD:(h+1)*HD,:].astype(f32),axis=0,keepdims=True) for h in range(heads)]
    segq = segr_ref[...]
    def one(kb, dqs):
        start = pl.multiple_of(jnp.bitwise_xor(kb, flip)*BK, BK)
        rows = pl.ds(start,BK)
        same = segc_ref[rows,:] == segq
        out=[]
        parts={}
        for h in range(heads):
            a,b = head_cols(h, heads)
            s = lax.dot_general(k_ref[rows, a:b], qz[h], NN, preferred_element_type=f32)
            p = jnp.exp2(jnp.where(same, s*c - lse_ref[h:h+1,:], -1e30))
            dp = lax.dot_general(v_ref[rows, a:b], dz[h], NN, preferred_element_type=f32)
            ds = (p*((dp-deltas[h])*scale)).astype(bf16)
            dvp = lax.dot_general(p.astype(bf16), dz[h], NT, preferred_element_type=f32)
            dkp = lax.dot_general(ds, qz[h], NT, preferred_element_type=f32)
            if (a,b) in parts: parts[a,b]=(parts[a,b][0]+dkp,parts[a,b][1]+dvp)
            else: parts[a,b]=(dkp,dvp)
            out.append(dqs[h]+lax.dot_general(kT_ref[h*HD:(h+1)*HD, rows], ds, NN, preferred_element_type=f32))
        for (a,b),(dkp,dvp) in parts.items():
            dk_acc[rows,a:b]+=dkp
            dv_acc[rows,a:b]+=dvp
        return tuple(out)
    dqs = lax.fori_loop(lo,hi,one,tuple(jnp.zeros((HD,BQ),f32) for _ in range(heads)))
    for h in range(heads):
        dq_ref[h*HD:(h+1)*HD,:]=dqs[h].astype(bf16)
        part = dqs[h][:,:128]
        for n in range(128,BQ,128): part=part+dqs[h][:,n:n+128]
        qb_ref[h*HD:(h+1)*HD,:]+=part
    @pl.when(i==pl.num_programs(0)-1)
    def _():
        if start_at:
            dk_ref[...]=(dk_acc[...]+dk_old[...]).astype(bf16)
            dv=dv_acc[...]+dv_old[...]
            dv_ref[...]=dv.astype(bf16)
            vb_ref[...]=jnp.sum(dv.reshape(dv.shape[0]//8,8,width),axis=0)
        else:
            dk_ref[...]=dk_acc[...]
            dv_ref[...]=dv_acc[...]

def attn_bwd(qT,k,kT,v,wT,grads,oT,lse,segc,segr,lo,hi,flip,sums=()):
    width,length=qT.shape
    heads=width//HD
    blocks=length//BQ//2
    first=blocks if sums else 0
    col=pl.BlockSpec((width,BQ),lambda i,*_:(0,first+i))
    row=pl.BlockSpec((length,width),lambda i,*_:(0,0))
    tall=jax.ShapeDtypeStruct((length,width),bf16 if sums else f32)
    eight=((jax.ShapeDtypeStruct((8,width),f32),),[pl.BlockSpec((8,width),lambda i,*_:(0,0))]) if sums else ((),[])
    return pl.pallas_call(
        functools.partial(bwd_kernel,first),
        out_shape=(jax.ShapeDtypeStruct((width,length//2),bf16), tall, tall, jax.ShapeDtypeStruct((width,128),f32))+eight[0],
        grid_spec=pltpu.PrefetchScalarGridSpec(num_scalar_prefetch=3, grid=(blocks,),
            in_specs=[col,row,pl.BlockSpec((width,length),lambda i,*_:(0,0)),row,pl.BlockSpec((width,wT.shape[1]),lambda i,*_:(wT.shape[1]//width-1,0))]+[pl.BlockSpec(g.shape,lambda i,*_:(0,0)) for g in grads]+[pl.BlockSpec((width,BQ),lambda i,*_:(0,i)),
                      pl.BlockSpec((8,BQ),lambda i,*_:(0,i)),
                      pl.BlockSpec((length,1),lambda i,*_:(0,0)),
                      pl.BlockSpec((1,BQ),lambda i,*_:(0,first+i))]+[row]*len(sums),
            out_specs=[pl.BlockSpec((width,BQ),lambda i,*_:(0,i)),row,row,pl.BlockSpec((width,128),lambda i,*_:(0,0))]+eight[1],
            scratch_shapes=[pltpu.VMEM((length,width),f32),pltpu.VMEM((length,width),f32),pltpu.VMEM((width,BQ),bf16)]),
        compiler_params=pltpu.CompilerParams(dimension_semantics=("arbitrary",),vmem_limit_bytes=60<<20),
        cost_estimate=pl.CostEstimate(flops=30*length*length*width,bytes_accessed=10*length*width,transcendentals=heads*length*length//4),
        name="attention_back",
    )(lo,hi,flip,qT,k,kT,v,wT,*grads,oT,lse,segc,segr,*sums)

def spans(seg_row):
    length=seg_row.shape[0]
    first=seg_row[::BQ]; last=seg_row[BQ-1::BQ]
    lo=jnp.sum(seg_row[None,:]<first[:,None],axis=1,dtype=jnp.int32)//BK
    hi=(jnp.sum(seg_row[None,:]<=last[:,None],axis=1,dtype=jnp.int32)+BK-1)//BK
    return lo,hi

EPSILON=1e-12
T=256
RC=32

def row_stats(values):
    centre=jnp.mean(values,axis=1,keepdims=True)
    centred=values-centre
    spread=jnp.mean(centred*centred,axis=1,keepdims=True)
    scale=lax.rsqrt(spread+EPSILON)
    return centred*scale, scale

def fold(values):
    return jnp.sum(values.reshape(values.shape[0]//8,8,values.shape[1]),axis=0)

def placements(count, model, blocks):
    if count != 8:
        return [[(r % 2, 0, r % 2, 0, None, model)] for r in range(blocks)]
    rows = model // 8
    every = []
    for r in range(blocks):
        core, beyond = r % 2, r // 2
        block = []
        for shard in range(8):
            odd, place = shard % 2, shard // 2
            if not beyond:
                source, first = odd, place
            elif not odd:
                source, first = 2, place
            else:
                source, first = (3, 0) if place == 0 else (4, place - 1)
            group = beyond and odd
            target = 0 if group else beyond * 2 + odd
            block.append((core * 5 + source, first * rows, core * 2 + group, (target * 4 + place) * rows, shard, rows))
        every.append(block)
    return every


def ffn_kernel(count, home_ref, tok_ref, a0_ref, a1_ref, a2_ref, cot_ref, vec_ref, be_ref, *refs):
    rows, width = tok_ref.shape
    blocks, units = be_ref.shape
    table = placements(count, width, blocks)
    n_in = 1 + max(item[0] for block in table for item in block)
    n_out = 1 + max(item[2] for block in table for item in block)
    pieces, refs = refs[:n_in], refs[n_in:]
    (out_ref, gm_ref, gml_ref, vg_ref, eb_ref), refs = refs[:5], refs[5:]
    grads, refs = refs[:n_out], refs[n_out:]
    we, ws, hl, hlT, hid, xhat, rs1, act, gp, acc, sl, slT, gsum, il, de, dt, wsem, osem = refs
    home = home_ref[0]
    def columns(ref, r, half):
        start = half * units + (r // 2 * 2 * units if len(table[0]) == 1 else 0)
        return ref.at[:, start : start + units]
    def spot(shard, size):
        return pl.ds(0 if shard is None else pl.multiple_of(jnp.bitwise_xor(home, shard) * size, size), size)
    def fetched(r, half):
        return [
            pltpu.make_async_copy(columns(pieces[p], r, half).at[first : first + size], (we, ws)[half].at[r, spot(shard, size)], wsem.at[half, r, k])
            for k, (p, first, _, _, shard, size) in enumerate(table[r])
        ]
    def sent(slot, r):
        return [
            pltpu.make_async_copy((de, dt)[half].at[slot, spot(shard, size)], columns(grads[g], r, half).at[first : first + size], osem.at[half, slot, k])
            for half in range(2)
            for k, (_, _, g, first, shard, size) in enumerate(table[r])
        ]
    for r in range(blocks):
        for half in range(2):
            for c in fetched(r, half):
                c.start()
    mb=vec_ref[0:1,:]; g1=vec_ref[1:2,:]; b1=vec_ref[2:3,:]; sb=vec_ref[3:4,:]; g2=vec_ref[4:5,:]; b2=vec_ref[5:6,:]
    def first(i,_):
        at=pl.ds(pl.multiple_of(i*RC,RC),RC)
        mixed=tok_ref[at,:].astype(f32)+(a0_ref[at,:].astype(f32)+a1_ref[at,:].astype(f32)+a2_ref[at,:].astype(f32))+mb
        z,scale=row_stats(mixed)
        xhat[at,:]=z
        rs1[at,:]=jnp.broadcast_to(scale,(RC,128))
        h=z*g1+b1
        hid[at,:]=h
        hl[at,:]=h.astype(bf16)
        acc[at,:]=jnp.zeros((RC,width),f32)
        return 0
    lax.fori_loop(0,rows//RC,first,0,unroll=4)
    def turn(src,dst):
        def go(i,_):
            at=pl.multiple_of(i*T,T)
            dst[:,pl.ds(at,T)]=jnp.transpose(src[pl.ds(at,T),:].astype(f32)).astype(bf16)
            return 0
        lax.fori_loop(0,rows//T,go,0)
    turn(hl,hlT)
    TG=768; TM=min(512,rows); per=units//T; mt=rows//TM
    def forward(r,_):
        for k in range(blocks):
            @pl.when(r==k)
            def _():
                for c in fetched(k, 0): c.wait()
        def tile(j,_):
            n=pl.multiple_of((j//mt)*T,T); m=pl.multiple_of((j%mt)*TM,TM)
            u=lax.dot_general(hl[pl.ds(m,TM),:],we[r,:,pl.ds(n,T)],NN,preferred_element_type=f32)+be_ref[pl.ds(r,1),pl.ds(n,T)]
            cdf=0.5+0.5*lax.erf(u*(0.5**0.5))
            act[r,pl.ds(m,TM),pl.ds(n,T)]=(u*cdf).astype(bf16)
            gp[r,pl.ds(m,TM),pl.ds(n,T)]=cdf+u*(jnp.exp(-0.5*u*u)*0.3989422804014327)
            return 0
        lax.fori_loop(0,per*mt,tile,0,unroll=3)
        for k in range(blocks):
            @pl.when(r==k)
            def _():
                for c in fetched(k, 1): c.wait()
        def shrink(j,_):
            n=pl.multiple_of((j//mt)*T,T); m=pl.multiple_of((j%mt)*TM,TM)
            acc[pl.ds(m,TM),pl.ds(n,T)]+=lax.dot_general(act[r,pl.ds(m,TM),:],ws[r,pl.ds(n,T),:],NT,preferred_element_type=f32)
            return 0
        lax.fori_loop(0,(width//T)*mt,shrink,0,unroll=3)
        return 0
    lax.fori_loop(0,blocks,forward,0)
    def second(i,sums):
        at=pl.ds(pl.multiple_of(i*RC,RC),RC)
        summed=hid[at,:]+acc[at,:]+sb
        z,scale=row_stats(summed)
        out_ref[at,:]=(z*g2+b2).astype(bf16)
        cot=cot_ref[at,:].astype(f32)
        e=cot*g2
        g=(e-jnp.mean(e,axis=1,keepdims=True)-z*jnp.mean(e*z,axis=1,keepdims=True))*scale
        gsum[at,:]=g
        sl[at,:]=g.astype(bf16)
        acc[at,:]=g
        return (sums[0]+fold(cot*z),sums[1]+fold(cot),sums[2]+fold(g))
    zero=jnp.zeros((8,width),f32)
    sg,sh,sbg=lax.fori_loop(0,rows//RC,second,(zero,zero,zero),unroll=4)
    turn(sl,slT)
    def backward(r,_):
        slot=r%2
        def tile(j,_):
            n=pl.multiple_of((j//mt)*T,T); m=pl.multiple_of((j%mt)*TM,TM)
            ga=lax.dot_general(sl[pl.ds(m,TM),:],ws[r,:,pl.ds(n,T)],NN,preferred_element_type=f32)
            gi=ga*gp[r,pl.ds(m,TM),pl.ds(n,T)]
            il[pl.ds(m,TM),pl.ds(n,T)]=gi.astype(bf16)
            part=fold(gi)
            eb_ref[r,:,pl.ds(n,T)]=jnp.where(m==0,part,eb_ref[r,:,pl.ds(n,T)]+part)
            return 0
        lax.fori_loop(0,per*mt,tile,0,unroll=3)
        def back(j,_):
            n=pl.multiple_of((j//mt)*T,T); m=pl.multiple_of((j%mt)*TM,TM)
            acc[pl.ds(m,TM),pl.ds(n,T)]+=lax.dot_general(il[pl.ds(m,TM),:],we[r,pl.ds(n,T),:],NT,preferred_element_type=f32)
            return 0
        lax.fori_loop(0,(width//T)*mt,back,0,unroll=3)
        for k in range(2,blocks):
            @pl.when(r==k)
            def _():
                for c in sent(k%2,k-2): c.wait()
        def grads(j,_):
            n=pl.multiple_of((j//(width//TG))*T,T); m=pl.multiple_of((j%(width//TG))*TG,TG)
            dt[slot,pl.ds(m,TG),pl.ds(n,T)]=lax.dot_general(slT[pl.ds(m,TG),:],act[r,:,pl.ds(n,T)],NN,preferred_element_type=f32).astype(bf16)
            de[slot,pl.ds(m,TG),pl.ds(n,T)]=lax.dot_general(hlT[pl.ds(m,TG),:],il[:,pl.ds(n,T)],NN,preferred_element_type=f32).astype(bf16)
            return 0
        lax.fori_loop(0,(width//TG)*per,grads,0,unroll=3)
        for k in range(blocks):
            @pl.when(r==k)
            def _():
                for c in sent(k%2,k): c.start()
        return 0
    lax.fori_loop(0,blocks,backward,0)
    def last(i,sums):
        at=pl.ds(pl.multiple_of(i*RC,RC),RC)
        g=acc[at,:]
        z=xhat[at,:]
        e=g*g1
        gm=(e-jnp.mean(e,axis=1,keepdims=True)-z*jnp.mean(e*z,axis=1,keepdims=True))*rs1[at,0:1]
        gm_ref[at,:]=gm
        gml_ref[at,:]=gm.astype(bf16)
        return (sums[0]+fold(g*z),sums[1]+fold(g),sums[2]+fold(gm))
    fg,fs,mbg=lax.fori_loop(0,rows//RC,last,(zero,zero,zero),unroll=4)
    for n,v in enumerate((mbg,fg,fs,sbg,sg,sh)):
        vg_ref[n]=v
    for k in range(max(0,blocks-2),blocks):
        for c in sent(k%2,k): c.wait()

def ffn(home, count, tok, a0, a1, a2, cot, vec, be, pieces):
    rows, width = tok.shape
    blocks, units = be.shape
    table = placements(count, width, blocks)
    n_out = 1 + max(item[2] for block in table for item in block)
    each = len(table[0])
    sizes = [(width * 3 // 2, 2 * units), (width // 2, 2 * units)] * 2 if each > 1 else [(width, blocks * units)] * 2
    grads = tuple(jax.ShapeDtypeStruct(size, bf16) for size in sizes)
    v = pl.BlockSpec(memory_space=pltpu.VMEM)
    h = pl.BlockSpec(memory_space=pltpu.HBM)
    V = pltpu.VMEM
    return pl.pallas_call(
        functools.partial(ffn_kernel, count),
        out_shape=(jax.ShapeDtypeStruct((rows, width), bf16), jax.ShapeDtypeStruct((rows, width), f32), jax.ShapeDtypeStruct((rows, width), bf16),
            jax.ShapeDtypeStruct((6, 8, width), f32), jax.ShapeDtypeStruct((blocks, 8, units), f32)) + grads,
        in_specs=[pl.BlockSpec(memory_space=pltpu.SMEM)] + [v] * 7 + [h] * len(pieces),
        out_specs=[v] * 5 + [h] * n_out,
        scratch_shapes=[V((blocks, width, units), bf16), V((blocks, width, units), bf16),
            V((rows, width), bf16), V((width, rows), bf16), V((rows, width), f32), V((rows, width), f32), V((rows, 128), f32),
            V((blocks, rows, units), bf16), V((blocks, rows, units), f32), V((rows, width), f32), V((rows, width), bf16), V((width, rows), bf16), V((rows, width), f32),
            V((rows, units), bf16), V((2, width, units), bf16), V((2, width, units), bf16),
            pltpu.SemaphoreType.DMA((2, blocks, each)), pltpu.SemaphoreType.DMA((2, 2, each))],
        compiler_params=pltpu.CompilerParams(vmem_limit_bytes=60 << 20),
        cost_estimate=pl.CostEstimate(flops=30 * rows * width * units * blocks, bytes_accessed=8 * blocks * width * units, transcendentals=2 * rows * units * blocks),
        name="feed_forward",
    )(home, tok, a0, a1, a2, cot, vec, be, *pieces)


def proj_kernel(home_ref, x0, x1, x2, x3, wa_ref, wb_ref, bq_ref, bvc_ref, bvr_ref,
                q_ref, kT_ref, vT_ref, k_ref, v_ref, wT, w_ref, wk, wv, x_buf, sem, x_sem):
    model = w_ref.shape[0]
    count, rows = sem.shape[0], model // sem.shape[0]
    width = q_ref.shape[0]
    home = home_ref[0]
    step = pl.program_id(0)
    def copy(r):
        src = (wa_ref, wb_ref)[r % 2].at[(r // 2) * rows : (r // 2 + 1) * rows]
        at = pl.multiple_of(jnp.bitwise_xor(home, r) * rows, rows)
        return pltpu.make_async_copy(src, w_ref.at[pl.ds(at, rows)], sem.at[r])
    if wa_ref.shape[0] == model:
        count = 1
        copy = lambda r: pltpu.make_async_copy(wa_ref, w_ref, sem.at[r])
    fetch = [pltpu.make_async_copy(x, x_buf.at[n], x_sem.at[n]) for n, x in enumerate((x0, x1, x2, x3))]
    @pl.when(step == 0)
    def _():
        for r in range(count):
            copy(r).start()
        for x in fetch:
            x.start()
        for r in range(count):
            copy(r).wait()
        def turn(i, _):
            at = pl.multiple_of(i * 256, 256)
            wT[:, pl.ds(at, 256)] = jnp.transpose(w_ref[pl.ds(at, 256), :].astype(f32)).astype(bf16)
            return 0
        lax.fori_loop(0, model // 256, turn, 0)
        wk[...] = w_ref[:, width : 2 * width]
        wv[...] = w_ref[:, 2 * width : 3 * width]
    for n, x in enumerate(fetch):
        @pl.when(step == n)
        def _():
            x.wait()
    x = x_buf[step]
    k_ref[...] = jnp.dot(x, wk[...], preferred_element_type=f32).astype(bf16)
    v_ref[...] = (jnp.dot(x, wv[...], preferred_element_type=f32) + bvr_ref[...]).astype(bf16)
    q_ref[...] = (lax.dot_general(wT[0:width], x, NT, preferred_element_type=f32) + bq_ref[...]).astype(bf16)
    kT_ref[...] = lax.dot_general(wT[width : 2 * width], x, NT, preferred_element_type=f32).astype(bf16)
    vT_ref[...] = (lax.dot_general(wT[2 * width : 3 * width], x, NT, preferred_element_type=f32) + bvc_ref[...]).astype(bf16)


def project(home, tokens, wa, wb, count, bq, bv):
    size, model = tokens[0].shape
    length = 4 * size
    width = bq.shape[0]
    hbm = pl.BlockSpec(memory_space=pltpu.HBM)
    column = pl.BlockSpec((width, 1), lambda i: (0, 0))
    tall = jax.ShapeDtypeStruct((length, width), bf16)
    flat = jax.ShapeDtypeStruct((width, length), bf16)
    across = pl.BlockSpec((width, size), lambda i: (0, i))
    down = pl.BlockSpec((size, width), lambda i: (i, 0))
    return pl.pallas_call(
        proj_kernel,
        grid=(4,),
        out_shape=(flat, flat, flat, tall, tall, jax.ShapeDtypeStruct((model, model), bf16)),
        in_specs=[pl.BlockSpec(memory_space=pltpu.SMEM)] + [hbm] * 6 + [column, column, pl.BlockSpec((1, width), lambda i: (0, 0))],
        out_specs=[across, across, across, down, down, pl.BlockSpec((model, model), lambda i: (0, 0))],
        scratch_shapes=[pltpu.VMEM((model, model), bf16), pltpu.VMEM((model, width), bf16), pltpu.VMEM((model, width), bf16),
            pltpu.VMEM((4, size, model), bf16), pltpu.SemaphoreType.DMA((count,)), pltpu.SemaphoreType.DMA((4,))],
        compiler_params=pltpu.CompilerParams(dimension_semantics=("arbitrary",), vmem_limit_bytes=60 << 20),
        cost_estimate=pl.CostEstimate(flops=30 * length * model * width, bytes_accessed=4 * length * model, transcendentals=0),
        name="projection",
    )(home, *tokens, wa, wb, bq[:, None], bv[:, None], bv[None, :])


def grads_kernel(home_ref, x0, x1, x2, x3, g0, g1, g2, g3, ca_ref, cb_ref, qa_ref, qb_ref, k_ref, v_ref, *rest):
    *outs, acc, x_buf, g_buf, xT, gT, sem = rest
    home = home_ref[0]
    step = pl.program_id(0)
    size, model = xT.shape[1], xT.shape[0]
    width = k_ref.shape[1]
    fetch = [
        (pltpu.make_async_copy(x, x_buf.at[n], sem.at[0, n]), pltpu.make_async_copy(g, g_buf.at[n], sem.at[1, n]))
        for n, (x, g) in enumerate(zip((x0, x1, x2, x3), (g0, g1, g2, g3)))
    ]
    @pl.when(step == 0)
    def _():
        for x, g in fetch:
            x.start()
            g.start()
    for n, (x, g) in enumerate(fetch):
        @pl.when(step == n)
        def _():
            x.wait()
            g.wait()
    for i in range(0, size, 256):
        xT[:, i : i + 256] = jnp.transpose(x_buf[step, i : i + 256, :].astype(f32)).astype(bf16)
        gT[:, i : i + 256] = jnp.transpose(g_buf[step, i : i + 256, :].astype(f32)).astype(bf16)
    q = jnp.where(step < 2, qa_ref[...], qb_ref[...])
    c = jnp.where(step < 2, ca_ref[...], cb_ref[...])
    pieces = (
        lax.dot_general(xT[...], q, NT, preferred_element_type=f32),
        jnp.dot(xT[...], k_ref[...], preferred_element_type=f32),
        jnp.dot(xT[...], v_ref[...], preferred_element_type=f32),
        lax.dot_general(gT[...], c, NT, preferred_element_type=f32),
    )
    @pl.when(step == 0)
    def _():
        for m, piece in enumerate(pieces):
            acc[m] = piece
    @pl.when(step > 0)
    def _():
        for m, piece in enumerate(pieces):
            acc[m] += piece
    @pl.when(step == 3)
    def _():
        if len(outs) == 1:
            for m in range(4):
                outs[0][:, m * width : (m + 1) * width] = acc[m].astype(bf16)
            return
        rows = model // 8
        for r in range(8):
            at = pl.ds(pl.multiple_of(jnp.bitwise_xor(home, r) * rows, rows), rows)
            to = slice(r // 2 * rows, (r // 2 + 1) * rows)
            for m in range(4):
                outs[r % 2][to, m * width : (m + 1) * width] = acc[m, at, :].astype(bf16)


def halves(width, size):
    return [pl.BlockSpec((width, size), lambda i: (0, jnp.minimum(i, 1))), pl.BlockSpec((width, size), lambda i: (0, jnp.maximum(i, 2) - 2))]


def attn_grads(home, count, tokens, grads, contextT, dqT, dk, dv):
    size, model = tokens[0].shape
    width = dk.shape[1]
    hbm = pl.BlockSpec(memory_space=pltpu.HBM)
    down = pl.BlockSpec((size, width), lambda i: (i, 0))
    parts = 2 if count == 8 else 1
    V = pltpu.VMEM
    return pl.pallas_call(
        grads_kernel,
        grid=(4,),
        out_shape=[jax.ShapeDtypeStruct((model // parts, 4 * width), bf16)] * parts,
        in_specs=[pl.BlockSpec(memory_space=pltpu.SMEM)] + [hbm] * 8 + halves(width, size) * 2 + [down, down],
        out_specs=[pl.BlockSpec((model // parts, 4 * width), lambda i: (0, 0))] * parts,
        scratch_shapes=[V((4, model, width), f32), V((4, size, model), bf16), V((4, size, model), bf16), V((model, size), bf16), V((model, size), bf16),
            pltpu.SemaphoreType.DMA((2, 4))],
        compiler_params=pltpu.CompilerParams(dimension_semantics=("arbitrary",), vmem_limit_bytes=60 << 20),
        cost_estimate=pl.CostEstimate(flops=8 * size * model * width, bytes_accessed=24 * size * model, transcendentals=0),
        name="projection_grads",
    )(home, *tokens, *grads, *contextT, *dqT, dk, dv)


def back_kernel(qa_ref, qb_ref, k_ref, v_ref, wq_ref, wk_ref, wv_ref, near_ref, side_ref, far_ref):
    i = pl.program_id(0)
    size = near_ref.shape[0]
    def block(q_ref):
        q = jnp.transpose(q_ref[...].astype(f32)).astype(bf16)
        total = jnp.dot(q, wq_ref[...], preferred_element_type=f32)
        total = total + jnp.dot(k_ref[...], wk_ref[...], preferred_element_type=f32)
        return (total + jnp.dot(v_ref[...], wv_ref[...], preferred_element_type=f32)).astype(bf16)
    for n, ref in enumerate((near_ref, side_ref, far_ref, side_ref)):
        @pl.when(i == n)
        def _():
            ref[size if n == 3 else 0 : 2 * size if n == 3 else size, :] = block((qa_ref, qb_ref)[n // 2])


def project_back(dqT, dk, dv, wT):
    length, width = dk.shape
    size, model = length // 4, wT.shape[1]
    down = pl.BlockSpec((size, width), lambda i: (i, 0))
    weight = [pl.BlockSpec((width, model), functools.partial(lambda n, i: (n, 0), n)) for n in range(3)]
    return pl.pallas_call(
        back_kernel,
        grid=(4,),
        out_shape=[jax.ShapeDtypeStruct((n * size, model), bf16) for n in (1, 2, 1)],
        in_specs=halves(width, size) + [down, down] + weight,
        out_specs=[pl.BlockSpec((n * size, model), lambda i: (0, 0)) for n in (1, 2, 1)],
        compiler_params=pltpu.CompilerParams(dimension_semantics=("arbitrary",), vmem_limit_bytes=60 << 20),
        cost_estimate=pl.CostEstimate(flops=70 * length * model * width, bytes_accessed=8 * length * model, transcendentals=0),
        name="projection_back",
    )(*dqT, dk, dv, wT, wT, wT)


def hop(value, bit):
    count = lax.axis_size("dp")
    return lax.ppermute(value, "dp", [(i, i ^ bit) for i in range(count)])


def gather_shards(own):
    count = lax.axis_size("dp")
    if count != 8:
        every = lax.all_gather(own, "dp", axis=0, tiled=True)
        return every, every
    even = jnp.concatenate([own] + [hop(own, bit) for bit in (2, 4, 6)], axis=0)
    return even, hop(even, 1)


def later(value, *markers, flops=0):
    anywhere = pl.BlockSpec(memory_space=pl.ANY)
    return pl.pallas_call(
        lambda *refs: None,
        out_shape=jax.ShapeDtypeStruct(value.shape, value.dtype),
        in_specs=[anywhere] * (1 + len(markers)),
        out_specs=anywhere,
        input_output_aliases={0: 0},
        cost_estimate=pl.CostEstimate(flops=flops, bytes_accessed=0, transcendentals=0),
        name="later",
    )(value, *markers)


def exchange(value, bit):
    return lax.ppermute(value, "tensor", [(i, i ^ bit) for i in range(4)])


def row_blocks(own):
    across = exchange(own, 2)
    return [own, exchange(own, 1), across, exchange(across, 1)]


def gather_rows(own):
    return jnp.concatenate(row_blocks(own), axis=0)


def scatter_pieces(near, side, far):
    rows = near.shape[0]
    beside = exchange(side, 1)
    ahead = (far.astype(f32) + beside[rows:].astype(f32)).astype(bf16)
    return (near, beside[:rows], exchange(ahead, 2)), ahead


def gather_blocks(own):
    if lax.axis_size("dp") != 8:
        return [lax.all_gather(jnp.concatenate([own, exchange(own, 2)], axis=1), "dp", axis=0, tiled=True)]
    even = jnp.concatenate([own] + [hop(own, bit) for bit in (2, 4, 6)], axis=0)
    return [even, hop(even, 1), exchange(even, 2)]


def last_blocks(pieces, *markers):
    if len(pieces) == 1:
        return []
    _, odd, beyond = pieces
    cut = odd.shape[0] // 4
    return [later(exchange(odd[:cut], 2), *markers), later(hop(beyond[cut:], 1), *markers)]


def total(*terms):
    result = terms[0].astype(f32)
    for term in terms[1:]:
        result = result + term.astype(f32)
    return result


def fold_both(own, got):
    cut = own.shape[0] // 4
    return total(own[:cut], got[:cut]).astype(bf16), total(own[cut:], got[cut:]).astype(bf16)


def fold_rest(own, got, across, along):
    rows = own.shape[0] // 3
    cut = rows // 4
    part = lambda n: total(own[n * rows : (n + 1) * rows], got[n * rows : (n + 1) * rows])
    odd, beyond = part(1), part(2)
    odd = jnp.concatenate([odd[:cut] + across.astype(f32), odd[cut:]], axis=0).astype(bf16)
    beyond = jnp.concatenate([beyond[:cut], beyond[cut:] + along.astype(f32)], axis=0).astype(bf16)
    return odd, beyond


def fold_even(own, got, odd, beyond):
    rows = own.shape[0] // 3
    return total(own[:rows], got[:rows], odd, beyond).astype(bf16).reshape(4, rows // 4, -1)


def on_device(
    tokens,
    segments,
    query_proj,
    query_bias,
    key_proj,
    value_proj,
    value_bias,
    merge_proj,
    merge_bias,
    first_gain,
    first_shift,
    expand_proj,
    expand_bias,
    shrink_proj,
    shrink_bias,
    second_gain,
    second_shift,
    cotangent,
):
    everyone = ("dp", "tensor")
    part = lax.axis_index("tensor")
    dp = lax.axis_size("dp")
    world = dp * 4
    width = query_proj.shape[1]
    units = expand_proj.shape[1]
    model = width * 4
    share = model // world
    unit_share = units * 4 // world

    shard = jnp.concatenate([query_proj, key_proj, value_proj, merge_proj.T], axis=1)
    shards = gather_shards(shard)
    wide = jnp.concatenate([expand_proj, shrink_proj.T], axis=1)
    pieces = gather_blocks(wide)
    own = jnp.concatenate(
        [query_bias, value_bias, merge_bias, first_gain, first_shift, shrink_bias, second_gain, second_shift, expand_bias]
    )
    rows = tokens.shape[0]
    count = own.shape[0]
    own = jnp.concatenate([own, segments.reshape(-1).astype(f32)])
    slots = -(-own.shape[0] // 1024) * 8
    own = jnp.pad(own, (0, slots * 128 - own.shape[0])).reshape(1, slots, 128)
    vectors = lax.all_to_all(jnp.broadcast_to(own, (world, slots, 128)), everyone, 0, 0, tiled=True)
    vectors = vectors.reshape(world, slots * 128)
    whole = vectors[:, : 8 * share].reshape(world, 8, share).transpose(1, 0, 2).reshape(8, model)
    unit_bias = vectors[:, 8 * share : 8 * share + unit_share].reshape(4, units)
    flips = jnp.bitwise_xor(jnp.arange(4), part)
    seg = lax.dynamic_slice(vectors, (lax.axis_index("dp") * 4, count), (4, rows))
    seg = jnp.take(seg, flips, axis=0).reshape(-1).astype(jnp.int32)
    unit_bias = jnp.take(unit_bias, flips, axis=0)
    query_b = lax.dynamic_slice_in_dim(whole[0], part * width, width)
    value_b = lax.dynamic_slice_in_dim(whole[1], part * width, width)
    rows_b = whole[2:8]

    blocks = row_blocks(tokens)
    segc, segr = seg[:, None], seg[None, :]
    lo, hi = spans(seg)
    flip = (part * (tokens.shape[0] // BK)).astype(jnp.int32).reshape(1)
    home = lax.axis_index("dp").astype(jnp.int32).reshape(1)
    query_t, key_t, value_t, keys, values, attn_wt = project(home, blocks, *shards, dp, query_b, value_b)
    ahead = functools.partial(attn_fwd, 1, query_t, keys, value_t, attn_wt, segc, segr)
    behind = functools.partial(attn_fwd, 0, query_t, keys, value_t, attn_wt, segc, segr)
    context_b, logsum_b, far, side = ahead(later(lo, pieces[0]), hi, flip)
    beside = exchange(side, 1)
    far = (far.astype(f32) + beside.astype(f32)).astype(bf16)
    swapped = [exchange(pieces[0], 1)]
    context_a, logsum_a, a0, side = behind(later(lo, far, swapped[0], *pieces[1:]), hi, flip)
    a1 = exchange(side, 1)
    a2 = later(exchange(far, 2), context_a)

    swapped = swapped + [later(exchange(piece, 1), context_a) for piece in pieces[1:]]
    last = last_blocks(pieces, context_a, a2)
    pieces = pieces + last + swapped + [exchange(piece, 1) for piece in last]
    out = ffn(home, dp, tokens, a0, a1, a2, cotangent, rows_b, unit_bias, pieces)
    output, grad_mixed, mixed_low, row_sums, unit_sums = out[:5]
    beside = exchange(mixed_low, 1)
    across = exchange(mixed_low, 2)
    grads = out[5:]
    local = len(grads) // 2
    swapped = [exchange(grad, 1) for grad in grads[local:]]
    back = functools.partial(attn_bwd, query_t, keys, key_t, values, attn_wt)
    waits = []
    if local == 2:
        waits = fold_both(grads[1], swapped[1])
    dq_a, dk_a, dv_a, q_sums_a = back((mixed_low, beside), context_a, logsum_a, segc, segr, later(lo, *waits), hi, flip)
    across = later(across, q_sums_a)
    mixed_blocks = [mixed_low, beside, across, exchange(across, 1)]
    if local == 2:
        waits = fold_rest(grads[0], swapped[0], later(exchange(waits[0], 2), q_sums_a), later(hop(waits[1], 1), q_sums_a))
    dq_b, dk, dv, q_sums_b, v_sums = back(
        mixed_blocks[2:], context_b, logsum_b, segc, segr, later(lo, *waits), hi, flip, sums=(dk_a, dv_a)
    )
    attn_local = attn_grads(home, dp, blocks, mixed_blocks, (context_a, context_b), (dq_a, dq_b), dk, dv)
    if local == 2:
        waits = [fold_even(grads[0], swapped[0], later(hop(waits[0], 1), attn_local[0]), later(exchange(waits[1], 2), attn_local[0]))]
    even = waits[0] if local == 2 else attn_local[0]
    b0, side, far = project_back((later(dq_a, even), dq_b), dk, dv, attn_wt)

    if local == 2:
        wide_grad = even[0].astype(f32) + sum(later(hop(even[n], 2 * n), b0).astype(f32) for n in (1, 2, 3))
        rows = attn_local[0].shape[0] // 4
        even = total(attn_local[0], later(hop(attn_local[1], 1), wide_grad)).astype(bf16).reshape(4, rows, -1)
        attn_grad = even[0].astype(f32) + sum(hop(even[n], 2 * n).astype(f32) for n in (1, 2, 3))
    else:
        mine = lax.psum_scatter(total(grads[0], swapped[0]).astype(bf16), "dp", scatter_dimension=0, tiled=True)
        wide_grad = total(mine[:, : 2 * units], exchange(mine[:, 2 * units :], 2))
        attn_grad = lax.all_to_all(attn_local[0], "dp", 0, 0, tiled=True)
        attn_grad = jnp.sum(attn_grad.reshape(dp, -1, model).astype(f32), axis=0)
    q_sums = later(q_sums_a + q_sums_b, wide_grad)
    v_sums = later(v_sums, wide_grad)
    mine = (jnp.arange(4) == part).astype(f32)[:, None]
    q_all = (mine * jnp.sum(q_sums, axis=1)[None]).reshape(1, model)
    v_all = (mine * jnp.sum(v_sums, axis=0)[None]).reshape(1, model)
    early = jnp.sum(row_sums, axis=1).reshape(6, world, share).transpose(1, 0, 2).reshape(world, 6 * share)
    late = jnp.concatenate([q_all, v_all], axis=0).reshape(2, world, share).transpose(1, 0, 2).reshape(world, 2 * share)
    u_all = jnp.take(jnp.sum(unit_sums, axis=1), flips, axis=0).reshape(world, unit_share)
    send = jnp.concatenate([late, early, u_all], axis=1)
    send = jnp.pad(send, ((0, 0), (0, slots * 128 - send.shape[1]))).reshape(world, slots, 128)
    got = jnp.sum(lax.all_to_all(send, everyone, 0, 0, tiled=True).reshape(world, slots * 128), axis=0)
    small = [got[n * share : (n + 1) * share] for n in range(8)]

    (b0, b1, b2), _ = scatter_pieces(b0, side, far)
    tokens_grad = (grad_mixed + (b0.astype(f32) + b1.astype(f32) + b2.astype(f32))).astype(bf16)
    querygrad, keygrad, valuegrad, mergegrad = (attn_grad[:, n * width : (n + 1) * width] for n in range(4))
    expandgrad = wide_grad[:, :units]
    shrinkgrad = wide_grad[:, units:].T

    qbiasgrad, vbiasgrad, mbiasgrad, fgaingrad, fshiftgrad, sbiasgrad, sgaingrad, sshiftgrad = small
    ebiasgrad = got[8 * share : 8 * share + unit_share]
    return (
        output,
        tokens_grad,
        querygrad,
        qbiasgrad,
        keygrad,
        valuegrad,
        vbiasgrad,
        mergegrad.T,
        mbiasgrad,
        fgaingrad,
        fshiftgrad,
        expandgrad,
        ebiasgrad,
        shrinkgrad,
        sbiasgrad,
        sgaingrad,
        sshiftgrad,
    )


def solution(mesh):
    return jax.shard_map(
        on_device,
        mesh=mesh,
        in_specs=(
            P(("dp", "tensor"), None),
            P("dp", "tensor"),
            P("dp", "tensor"),
            P(("dp", "tensor")),
            P("dp", "tensor"),
            P("dp", "tensor"),
            P(("dp", "tensor")),
            P("tensor", "dp"),
            P(("dp", "tensor")),
            P(("dp", "tensor")),
            P(("dp", "tensor")),
            P("dp", "tensor"),
            P(("dp", "tensor")),
            P("tensor", "dp"),
            P(("dp", "tensor")),
            P(("dp", "tensor")),
            P(("dp", "tensor")),
            P(("dp", "tensor"), None),
        ),
        out_specs=(
            P(("dp", "tensor"), None),
            P(("dp", "tensor"), None),
            P("dp", "tensor"),
            P(("dp", "tensor")),
            P("dp", "tensor"),
            P("dp", "tensor"),
            P(("dp", "tensor")),
            P("tensor", "dp"),
            P(("dp", "tensor")),
            P(("dp", "tensor")),
            P(("dp", "tensor")),
            P("dp", "tensor"),
            P(("dp", "tensor")),
            P("tensor", "dp"),
            P(("dp", "tensor")),
            P(("dp", "tensor")),
            P(("dp", "tensor")),
        ),
        check_vma=False,
    )
```

```python
import functools

import jax
import jax.numpy as jnp
from jax import lax
from jax.sharding import PartitionSpec as P
from jax.experimental import pallas as pl
from jax.experimental.pallas import tpu as pltpu

HD=64
BQ=512
BK=512
LOG2E=1.4426950408889634
NN=(((1,),(0,)),((),()))
NT=(((1,),(1,)),((),()))
TN=(((0,),(0,)),((),()))
f32=jnp.float32; bf16=jnp.bfloat16

def head_cols(h, heads):
    start=(h//2)*128
    stop=min(start+128, heads*HD)
    return start, stop

def padded(ref, h, heads, rows):
    start, stop = head_cols(h, heads)
    piece = ref[h*HD:(h+1)*HD, rows]
    if stop-start == HD: return piece
    zero = jnp.zeros_like(piece)
    return jnp.concatenate([piece, zero] if h%2==0 else [zero, piece], axis=0)

def fwd_kernel(start_at, lo_ref, hi_ref, flip_ref, q_ref, k_ref, v_ref, w_ref, segc_ref, segr_ref, o_ref, lse_ref, first_ref, second_ref, s_ref):
    heads = q_ref.shape[0]//HD
    i = pl.program_id(0)
    lo = lo_ref[start_at+i]; hi = hi_ref[start_at+i]; flip = flip_ref[0]
    c = LOG2E * HD**-0.5
    qz = [padded(q_ref, h, heads, slice(None)) for h in range(heads)]
    segq = segr_ref[...]
    def one(kb, peaks):
        start = pl.multiple_of(jnp.bitwise_xor(kb, flip)*BK, BK)
        same = segc_ref[pl.ds(start,BK),:] == segq
        new=[]
        for h in range(heads):
            a,b = head_cols(h, heads)
            s = lax.dot_general(k_ref[pl.ds(start,BK), a:b], qz[h], NN, preferred_element_type=f32)
            s = jnp.where(same, s, -1e30)
            s_ref[h, kb-lo] = s
            new.append(jnp.maximum(peaks[h], jnp.max(s.reshape(BK//8,8,BQ),axis=0)))
        return tuple(new)
    peaks = lax.fori_loop(lo, hi, one, tuple(jnp.full((8,BQ),-1e30,f32) for _ in range(heads)))
    peaks = [jnp.max(p,axis=0,keepdims=True)*c for p in peaks]
    def two(kb, carry):
        sums, outs = carry
        start = pl.multiple_of(jnp.bitwise_xor(kb, flip)*BK, BK)
        ns=[];no=[]
        for h in range(heads):
            p = jnp.exp2(s_ref[h, kb-lo]*c - peaks[h])
            ns.append(sums[h]+jnp.sum(p.reshape(BK//8,8,BQ),axis=0))
            no.append(outs[h]+lax.dot_general(v_ref[h*HD:(h+1)*HD, pl.ds(start,BK)], p.astype(bf16), NN, preferred_element_type=f32))
        return tuple(ns),tuple(no)
    sums, outs = lax.fori_loop(lo, hi, two, (tuple(jnp.zeros((8,BQ),f32) for _ in range(heads)), tuple(jnp.zeros((HD,BQ),f32) for _ in range(heads))))
    for h in range(heads):
        total = jnp.sum(sums[h],axis=0,keepdims=True)
        o_ref[h*HD:(h+1)*HD,:] = (outs[h]/total).astype(bf16)
        lse_ref[h:h+1,:] = peaks[h]+jnp.log2(total)
    context = jnp.transpose(o_ref[...].astype(f32)).astype(bf16)
    merged = jnp.dot(context, w_ref[...], preferred_element_type=f32).astype(bf16)
    per = first_ref.shape[0]//BQ
    for n, ref in enumerate((first_ref, second_ref)):
        @pl.when(i//per==n)
        def _():
            ref[pl.ds(pl.multiple_of((i%per)*BQ, BQ), BQ),:] = merged

def attn_fwd(second,qT,k,vT,wT,segc,segr,lo,hi,flip):
    width,length=qT.shape
    size,model=length//4,wT.shape[1]
    heads=width//HD
    blocks=length//BQ//2
    first=blocks*second
    col=pl.BlockSpec((width,BQ),lambda i,*_:(0,first+i))
    whole=pl.BlockSpec((size,model),lambda i,*_:(0,0))
    part=jax.ShapeDtypeStruct((size,model),bf16)
    return pl.pallas_call(
        functools.partial(fwd_kernel,first),
        out_shape=(jax.ShapeDtypeStruct((width,length//2),bf16), jax.ShapeDtypeStruct((8,length//2),f32), part, part),
        grid_spec=pltpu.PrefetchScalarGridSpec(num_scalar_prefetch=3, grid=(blocks,),
            in_specs=[col,
                      pl.BlockSpec((length,width),lambda i,*_:(0,0)),
                      pl.BlockSpec((width,length),lambda i,*_:(0,0)),
                      pl.BlockSpec((width,model),lambda i,*_:(model//width-1,0)),
                      pl.BlockSpec((length,1),lambda i,*_:(0,0)),
                      pl.BlockSpec((1,BQ),lambda i,*_:(0,first+i))],
            out_specs=[pl.BlockSpec((width,BQ),lambda i,*_:(0,i)),pl.BlockSpec((8,BQ),lambda i,*_:(0,i)),whole,whole],
            scratch_shapes=[pltpu.VMEM((heads,length//BK,BK,BQ),f32)]),
        compiler_params=pltpu.CompilerParams(dimension_semantics=("arbitrary",),vmem_limit_bytes=60<<20),
        cost_estimate=pl.CostEstimate(flops=25*length*length*width,bytes_accessed=4*length*width,transcendentals=heads*length*length//4),
        name="attention",
    )(lo,hi,flip,qT,k,vT,wT,segc,segr)

def bwd_kernel(start_at, lo_ref, hi_ref, flip_ref, q_ref, k_ref, kT_ref, v_ref, wT_ref, g0, g1, o_ref, lse_ref, segc_ref, segr_ref, *rest):
    if start_at:
        dk_old, dv_old, dq_ref, dk_ref, dv_ref, qb_ref, vb_ref, dk_acc, dv_acc, do_ref = rest
    else:
        dq_ref, dk_ref, dv_ref, qb_ref, dk_acc, dv_acc, do_ref = rest
    heads = q_ref.shape[0]//HD
    width = q_ref.shape[0]
    i = pl.program_id(0)
    @pl.when(i==0)
    def _():
        dk_acc[...]=jnp.zeros_like(dk_acc); dv_acc[...]=jnp.zeros_like(dv_acc)
        qb_ref[...]=jnp.zeros_like(qb_ref)
    lo = lo_ref[start_at+i]; hi = hi_ref[start_at+i]; flip = flip_ref[0]
    scale = HD**-0.5
    per = g0.shape[0]//BQ
    for n, g_ref in enumerate((g0, g1)):
        @pl.when(i//per==n)
        def _():
            at = pl.multiple_of((i%per)*BQ, BQ)
            do_ref[...] = lax.dot_general(wT_ref[...], g_ref[pl.ds(at,BQ),:], NT, preferred_element_type=f32).astype(bf16)
    c = LOG2E*scale
    qz = [padded(q_ref, h, heads, slice(None)) for h in range(heads)]
    dz = [padded(do_ref, h, heads, slice(None)) for h in range(heads)]
    deltas = [jnp.sum(do_ref[h*HD:(h+1)*HD,:].astype(f32)*o_ref[h*HD:(h+1)*HD,:].astype(f32),axis=0,keepdims=True) for h in range(heads)]
    segq = segr_ref[...]
    def one(kb, dqs):
        start = pl.multiple_of(jnp.bitwise_xor(kb, flip)*BK, BK)
        rows = pl.ds(start,BK)
        same = segc_ref[rows,:] == segq
        out=[]
        parts={}
        for h in range(heads):
            a,b = head_cols(h, heads)
            s = lax.dot_general(k_ref[rows, a:b], qz[h], NN, preferred_element_type=f32)
            p = jnp.exp2(jnp.where(same, s*c - lse_ref[h:h+1,:], -1e30))
            dp = lax.dot_general(v_ref[rows, a:b], dz[h], NN, preferred_element_type=f32)
            ds = (p*((dp-deltas[h])*scale)).astype(bf16)
            dvp = lax.dot_general(p.astype(bf16), dz[h], NT, preferred_element_type=f32)
            dkp = lax.dot_general(ds, qz[h], NT, preferred_element_type=f32)
            if (a,b) in parts: parts[a,b]=(parts[a,b][0]+dkp,parts[a,b][1]+dvp)
            else: parts[a,b]=(dkp,dvp)
            out.append(dqs[h]+lax.dot_general(kT_ref[h*HD:(h+1)*HD, rows], ds, NN, preferred_element_type=f32))
        for (a,b),(dkp,dvp) in parts.items():
            dk_acc[rows,a:b]+=dkp
            dv_acc[rows,a:b]+=dvp
        return tuple(out)
    dqs = lax.fori_loop(lo,hi,one,tuple(jnp.zeros((HD,BQ),f32) for _ in range(heads)))
    for h in range(heads):
        dq_ref[h*HD:(h+1)*HD,:]=dqs[h].astype(bf16)
        part = dqs[h][:,:128]
        for n in range(128,BQ,128): part=part+dqs[h][:,n:n+128]
        qb_ref[h*HD:(h+1)*HD,:]+=part
    @pl.when(i==pl.num_programs(0)-1)
    def _():
        if start_at:
            dk_ref[...]=(dk_acc[...]+dk_old[...]).astype(bf16)
            dv=dv_acc[...]+dv_old[...]
            dv_ref[...]=dv.astype(bf16)
            vb_ref[...]=jnp.sum(dv.reshape(dv.shape[0]//8,8,width),axis=0)
        else:
            dk_ref[...]=dk_acc[...]
            dv_ref[...]=dv_acc[...]

def attn_bwd(qT,k,kT,v,wT,grads,oT,lse,segc,segr,lo,hi,flip,sums=()):
    width,length=qT.shape
    heads=width//HD
    blocks=length//BQ//2
    first=blocks if sums else 0
    col=pl.BlockSpec((width,BQ),lambda i,*_:(0,first+i))
    row=pl.BlockSpec((length,width),lambda i,*_:(0,0))
    tall=jax.ShapeDtypeStruct((length,width),bf16 if sums else f32)
    eight=((jax.ShapeDtypeStruct((8,width),f32),),[pl.BlockSpec((8,width),lambda i,*_:(0,0))]) if sums else ((),[])
    return pl.pallas_call(
        functools.partial(bwd_kernel,first),
        out_shape=(jax.ShapeDtypeStruct((width,length//2),bf16), tall, tall, jax.ShapeDtypeStruct((width,128),f32))+eight[0],
        grid_spec=pltpu.PrefetchScalarGridSpec(num_scalar_prefetch=3, grid=(blocks,),
            in_specs=[col,row,pl.BlockSpec((width,length),lambda i,*_:(0,0)),row,pl.BlockSpec((width,wT.shape[1]),lambda i,*_:(wT.shape[1]//width-1,0))]+[pl.BlockSpec(g.shape,lambda i,*_:(0,0)) for g in grads]+[pl.BlockSpec((width,BQ),lambda i,*_:(0,i)),
                      pl.BlockSpec((8,BQ),lambda i,*_:(0,i)),
                      pl.BlockSpec((length,1),lambda i,*_:(0,0)),
                      pl.BlockSpec((1,BQ),lambda i,*_:(0,first+i))]+[row]*len(sums),
            out_specs=[pl.BlockSpec((width,BQ),lambda i,*_:(0,i)),row,row,pl.BlockSpec((width,128),lambda i,*_:(0,0))]+eight[1],
            scratch_shapes=[pltpu.VMEM((length,width),f32),pltpu.VMEM((length,width),f32),pltpu.VMEM((width,BQ),bf16)]),
        compiler_params=pltpu.CompilerParams(dimension_semantics=("arbitrary",),vmem_limit_bytes=60<<20),
        cost_estimate=pl.CostEstimate(flops=30*length*length*width,bytes_accessed=10*length*width,transcendentals=heads*length*length//4),
        name="attention_back",
    )(lo,hi,flip,qT,k,kT,v,wT,*grads,oT,lse,segc,segr,*sums)

def spans(seg_row):
    length=seg_row.shape[0]
    first=seg_row[::BQ]; last=seg_row[BQ-1::BQ]
    lo=jnp.sum(seg_row[None,:]<first[:,None],axis=1,dtype=jnp.int32)//BK
    hi=(jnp.sum(seg_row[None,:]<=last[:,None],axis=1,dtype=jnp.int32)+BK-1)//BK
    return lo,hi

EPSILON=1e-12
T=256
RC=128

def row_stats(values):
    centre=jnp.mean(values,axis=1,keepdims=True)
    centred=values-centre
    spread=jnp.mean(centred*centred,axis=1,keepdims=True)
    scale=lax.rsqrt(spread+EPSILON)
    return centred*scale, scale

def fold(values):
    return jnp.sum(values.reshape(values.shape[0]//8,8,values.shape[1]),axis=0)

def placements(count, model, blocks):
    if count != 8:
        return [[(r % 2, 0, r % 2, 0, None, model)] for r in range(blocks)]
    rows = model // 8
    every = []
    for r in range(blocks):
        core, beyond = r % 2, r // 2
        block = []
        for shard in range(8):
            odd, place = shard % 2, shard // 2
            if not beyond:
                source, first = odd, place
            elif not odd:
                source, first = 2, place
            else:
                source, first = (3, 0) if place == 0 else (4, place - 1)
            group = beyond and odd
            target = 0 if group else beyond * 2 + odd
            block.append((core * 5 + source, first * rows, core * 2 + group, (target * 4 + place) * rows, shard, rows))
        every.append(block)
    return every


def ffn_kernel(count, home_ref, tok_ref, a0_ref, a1_ref, a2_ref, cot_ref, vec_ref, be_ref, *refs):
    rows, width = tok_ref.shape
    blocks, units = be_ref.shape
    table = placements(count, width, blocks)
    n_in = 1 + max(item[0] for block in table for item in block)
    n_out = 1 + max(item[2] for block in table for item in block)
    pieces, refs = refs[:n_in], refs[n_in:]
    (out_ref, gm_ref, gml_ref, vg_ref, eb_ref), refs = refs[:5], refs[5:]
    grads, refs = refs[:n_out], refs[n_out:]
    we, ws, hl, hlT, hid, xhat, rs1, act, gp, acc, sl, slT, gsum, il, de, dt, wsem, osem = refs
    home = home_ref[0]
    def columns(ref, r, half):
        start = half * units + (r // 2 * 2 * units if len(table[0]) == 1 else 0)
        return ref.at[:, start : start + units]
    def spot(shard, size):
        return pl.ds(0 if shard is None else pl.multiple_of(jnp.bitwise_xor(home, shard) * size, size), size)
    def fetched(r, half):
        return [
            pltpu.make_async_copy(columns(pieces[p], r, half).at[first : first + size], (we, ws)[half].at[r, spot(shard, size)], wsem.at[half, r, k])
            for k, (p, first, _, _, shard, size) in enumerate(table[r])
        ]
    def sent(slot, r):
        return [
            pltpu.make_async_copy((de, dt)[half].at[slot, spot(shard, size)], columns(grads[g], r, half).at[first : first + size], osem.at[half, slot, k])
            for half in range(2)
            for k, (_, _, g, first, shard, size) in enumerate(table[r])
        ]
    for r in range(blocks):
        for half in range(2):
            for c in fetched(r, half):
                c.start()
    mb=vec_ref[0:1,:]; g1=vec_ref[1:2,:]; b1=vec_ref[2:3,:]; sb=vec_ref[3:4,:]; g2=vec_ref[4:5,:]; b2=vec_ref[5:6,:]
    def first(i,_):
        at=pl.ds(pl.multiple_of(i*RC,RC),RC)
        mixed=tok_ref[at,:].astype(f32)+(a0_ref[at,:].astype(f32)+a1_ref[at,:].astype(f32)+a2_ref[at,:].astype(f32))+mb
        z,scale=row_stats(mixed)
        xhat[at,:]=z
        rs1[at,:]=jnp.broadcast_to(scale,(RC,128))
        h=z*g1+b1
        hid[at,:]=h
        hl[at,:]=h.astype(bf16)
        acc[at,:]=jnp.zeros((RC,width),f32)
        return 0
    lax.fori_loop(0,rows//RC,first,0,unroll=2)
    def turn(src,dst):
        def go(i,_):
            at=pl.multiple_of(i*T,T)
            dst[:,pl.ds(at,T)]=jnp.transpose(src[pl.ds(at,T),:].astype(f32)).astype(bf16)
            return 0
        lax.fori_loop(0,rows//T,go,0)
    turn(hl,hlT)
    TG=768; TM=min(512,rows); per=units//T; mt=rows//TM
    def forward(r,_):
        for k in range(blocks):
            @pl.when(r==k)
            def _():
                for c in fetched(k, 0): c.wait()
        def tile(j,_):
            n=pl.multiple_of((j//mt)*T,T); m=pl.multiple_of((j%mt)*TM,TM)
            u=lax.dot_general(hl[pl.ds(m,TM),:],we[r,:,pl.ds(n,T)],NN,preferred_element_type=f32)+be_ref[pl.ds(r,1),pl.ds(n,T)]
            cdf=0.5+0.5*lax.erf(u*(0.5**0.5))
            act[r,pl.ds(m,TM),pl.ds(n,T)]=(u*cdf).astype(bf16)
            gp[r,pl.ds(m,TM),pl.ds(n,T)]=cdf+u*(jnp.exp(-0.5*u*u)*0.3989422804014327)
            return 0
        lax.fori_loop(0,per*mt,tile,0,unroll=3)
        for k in range(blocks):
            @pl.when(r==k)
            def _():
                for c in fetched(k, 1): c.wait()
        def shrink(j,_):
            n=pl.multiple_of((j//mt)*T,T); m=pl.multiple_of((j%mt)*TM,TM)
            acc[pl.ds(m,TM),pl.ds(n,T)]+=lax.dot_general(act[r,pl.ds(m,TM),:],ws[r,pl.ds(n,T),:],NT,preferred_element_type=f32)
            return 0
        lax.fori_loop(0,(width//T)*mt,shrink,0,unroll=3)
        return 0
    lax.fori_loop(0,blocks,forward,0)
    def second(i,sums):
        at=pl.ds(pl.multiple_of(i*RC,RC),RC)
        summed=hid[at,:]+acc[at,:]+sb
        z,scale=row_stats(summed)
        out_ref[at,:]=(z*g2+b2).astype(bf16)
        cot=cot_ref[at,:].astype(f32)
        e=cot*g2
        g=(e-jnp.mean(e,axis=1,keepdims=True)-z*jnp.mean(e*z,axis=1,keepdims=True))*scale
        gsum[at,:]=g
        sl[at,:]=g.astype(bf16)
        acc[at,:]=g
        return (sums[0]+fold(cot*z),sums[1]+fold(cot),sums[2]+fold(g))
    zero=jnp.zeros((8,width),f32)
    sg,sh,sbg=lax.fori_loop(0,rows//RC,second,(zero,zero,zero),unroll=2)
    turn(sl,slT)
    def backward(r,_):
        slot=r%2
        def tile(j,_):
            n=pl.multiple_of((j//mt)*T,T); m=pl.multiple_of((j%mt)*TM,TM)
            ga=lax.dot_general(sl[pl.ds(m,TM),:],ws[r,:,pl.ds(n,T)],NN,preferred_element_type=f32)
            gi=ga*gp[r,pl.ds(m,TM),pl.ds(n,T)]
            il[pl.ds(m,TM),pl.ds(n,T)]=gi.astype(bf16)
            part=fold(gi)
            eb_ref[r,:,pl.ds(n,T)]=jnp.where(m==0,part,eb_ref[r,:,pl.ds(n,T)]+part)
            return 0
        lax.fori_loop(0,per*mt,tile,0,unroll=3)
        def back(j,_):
            n=pl.multiple_of((j//mt)*T,T); m=pl.multiple_of((j%mt)*TM,TM)
            acc[pl.ds(m,TM),pl.ds(n,T)]+=lax.dot_general(il[pl.ds(m,TM),:],we[r,pl.ds(n,T),:],NT,preferred_element_type=f32)
            return 0
        lax.fori_loop(0,(width//T)*mt,back,0,unroll=3)
        for k in range(2,blocks):
            @pl.when(r==k)
            def _():
                for c in sent(k%2,k-2): c.wait()
        def grads(j,_):
            n=pl.multiple_of((j//(width//TG))*T,T); m=pl.multiple_of((j%(width//TG))*TG,TG)
            dt[slot,pl.ds(m,TG),pl.ds(n,T)]=lax.dot_general(slT[pl.ds(m,TG),:],act[r,:,pl.ds(n,T)],NN,preferred_element_type=f32).astype(bf16)
            de[slot,pl.ds(m,TG),pl.ds(n,T)]=lax.dot_general(hlT[pl.ds(m,TG),:],il[:,pl.ds(n,T)],NN,preferred_element_type=f32).astype(bf16)
            return 0
        lax.fori_loop(0,(width//TG)*per,grads,0,unroll=3)
        for k in range(blocks):
            @pl.when(r==k)
            def _():
                for c in sent(k%2,k): c.start()
        return 0
    lax.fori_loop(0,blocks,backward,0)
    def last(i,sums):
        at=pl.ds(pl.multiple_of(i*RC,RC),RC)
        g=acc[at,:]
        z=xhat[at,:]
        e=g*g1
        gm=(e-jnp.mean(e,axis=1,keepdims=True)-z*jnp.mean(e*z,axis=1,keepdims=True))*rs1[at,0:1]
        gm_ref[at,:]=gm
        gml_ref[at,:]=gm.astype(bf16)
        return (sums[0]+fold(g*z),sums[1]+fold(g),sums[2]+fold(gm))
    fg,fs,mbg=lax.fori_loop(0,rows//RC,last,(zero,zero,zero),unroll=2)
    for n,v in enumerate((mbg,fg,fs,sbg,sg,sh)):
        vg_ref[n]=v
    for k in range(max(0,blocks-2),blocks):
        for c in sent(k%2,k): c.wait()

def ffn(home, count, tok, a0, a1, a2, cot, vec, be, pieces):
    rows, width = tok.shape
    blocks, units = be.shape
    table = placements(count, width, blocks)
    n_out = 1 + max(item[2] for block in table for item in block)
    each = len(table[0])
    sizes = [(width * 3 // 2, 2 * units), (width // 2, 2 * units)] * 2 if each > 1 else [(width, blocks * units)] * 2
    grads = tuple(jax.ShapeDtypeStruct(size, bf16) for size in sizes)
    v = pl.BlockSpec(memory_space=pltpu.VMEM)
    h = pl.BlockSpec(memory_space=pltpu.HBM)
    V = pltpu.VMEM
    return pl.pallas_call(
        functools.partial(ffn_kernel, count),
        out_shape=(jax.ShapeDtypeStruct((rows, width), bf16), jax.ShapeDtypeStruct((rows, width), f32), jax.ShapeDtypeStruct((rows, width), bf16),
            jax.ShapeDtypeStruct((6, 8, width), f32), jax.ShapeDtypeStruct((blocks, 8, units), f32)) + grads,
        in_specs=[pl.BlockSpec(memory_space=pltpu.SMEM)] + [v] * 7 + [h] * len(pieces),
        out_specs=[v] * 5 + [h] * n_out,
        scratch_shapes=[V((blocks, width, units), bf16), V((blocks, width, units), bf16),
            V((rows, width), bf16), V((width, rows), bf16), V((rows, width), f32), V((rows, width), f32), V((rows, 128), f32),
            V((blocks, rows, units), bf16), V((blocks, rows, units), f32), V((rows, width), f32), V((rows, width), bf16), V((width, rows), bf16), V((rows, width), f32),
            V((rows, units), bf16), V((2, width, units), bf16), V((2, width, units), bf16),
            pltpu.SemaphoreType.DMA((2, blocks, each)), pltpu.SemaphoreType.DMA((2, 2, each))],
        compiler_params=pltpu.CompilerParams(vmem_limit_bytes=60 << 20),
        cost_estimate=pl.CostEstimate(flops=30 * rows * width * units * blocks, bytes_accessed=8 * blocks * width * units, transcendentals=2 * rows * units * blocks),
        name="feed_forward",
    )(home, tok, a0, a1, a2, cot, vec, be, *pieces)


def proj_kernel(home_ref, x0, x1, x2, x3, wa_ref, wb_ref, bq_ref, bvc_ref, bvr_ref,
                q_ref, kT_ref, vT_ref, k_ref, v_ref, wT, w_ref, wk, wv, x_buf, sem, x_sem):
    model = w_ref.shape[0]
    count, rows = sem.shape[0], model // sem.shape[0]
    width = q_ref.shape[0]
    home = home_ref[0]
    step = pl.program_id(0)
    def copy(r):
        src = (wa_ref, wb_ref)[r % 2].at[(r // 2) * rows : (r // 2 + 1) * rows]
        at = pl.multiple_of(jnp.bitwise_xor(home, r) * rows, rows)
        return pltpu.make_async_copy(src, w_ref.at[pl.ds(at, rows)], sem.at[r])
    if wa_ref.shape[0] == model:
        count = 1
        copy = lambda r: pltpu.make_async_copy(wa_ref, w_ref, sem.at[r])
    fetch = [pltpu.make_async_copy(x, x_buf.at[n], x_sem.at[n]) for n, x in enumerate((x0, x1, x2, x3))]
    @pl.when(step == 0)
    def _():
        for r in range(count):
            copy(r).start()
        for x in fetch:
            x.start()
        for r in range(count):
            copy(r).wait()
        def turn(i, _):
            at = pl.multiple_of(i * 256, 256)
            wT[:, pl.ds(at, 256)] = jnp.transpose(w_ref[pl.ds(at, 256), :].astype(f32)).astype(bf16)
            return 0
        lax.fori_loop(0, model // 256, turn, 0)
        wk[...] = w_ref[:, width : 2 * width]
        wv[...] = w_ref[:, 2 * width : 3 * width]
    for n, x in enumerate(fetch):
        @pl.when(step == n)
        def _():
            x.wait()
    x = x_buf[step]
    k_ref[...] = jnp.dot(x, wk[...], preferred_element_type=f32).astype(bf16)
    v_ref[...] = (jnp.dot(x, wv[...], preferred_element_type=f32) + bvr_ref[...]).astype(bf16)
    q_ref[...] = (lax.dot_general(wT[0:width], x, NT, preferred_element_type=f32) + bq_ref[...]).astype(bf16)
    kT_ref[...] = lax.dot_general(wT[width : 2 * width], x, NT, preferred_element_type=f32).astype(bf16)
    vT_ref[...] = (lax.dot_general(wT[2 * width : 3 * width], x, NT, preferred_element_type=f32) + bvc_ref[...]).astype(bf16)


def project(home, tokens, wa, wb, count, bq, bv):
    size, model = tokens[0].shape
    length = 4 * size
    width = bq.shape[0]
    hbm = pl.BlockSpec(memory_space=pltpu.HBM)
    column = pl.BlockSpec((width, 1), lambda i: (0, 0))
    tall = jax.ShapeDtypeStruct((length, width), bf16)
    flat = jax.ShapeDtypeStruct((width, length), bf16)
    across = pl.BlockSpec((width, size), lambda i: (0, i))
    down = pl.BlockSpec((size, width), lambda i: (i, 0))
    return pl.pallas_call(
        proj_kernel,
        grid=(4,),
        out_shape=(flat, flat, flat, tall, tall, jax.ShapeDtypeStruct((model, model), bf16)),
        in_specs=[pl.BlockSpec(memory_space=pltpu.SMEM)] + [hbm] * 6 + [column, column, pl.BlockSpec((1, width), lambda i: (0, 0))],
        out_specs=[across, across, across, down, down, pl.BlockSpec((model, model), lambda i: (0, 0))],
        scratch_shapes=[pltpu.VMEM((model, model), bf16), pltpu.VMEM((model, width), bf16), pltpu.VMEM((model, width), bf16),
            pltpu.VMEM((4, size, model), bf16), pltpu.SemaphoreType.DMA((count,)), pltpu.SemaphoreType.DMA((4,))],
        compiler_params=pltpu.CompilerParams(dimension_semantics=("arbitrary",), vmem_limit_bytes=60 << 20),
        cost_estimate=pl.CostEstimate(flops=30 * length * model * width, bytes_accessed=4 * length * model, transcendentals=0),
        name="projection",
    )(home, *tokens, wa, wb, bq[:, None], bv[:, None], bv[None, :])


def grads_kernel(home_ref, x0, x1, x2, x3, g0, g1, g2, g3, ca_ref, cb_ref, qa_ref, qb_ref, k_ref, v_ref, *rest):
    *outs, acc, x_buf, g_buf, xT, gT, sem = rest
    home = home_ref[0]
    step = pl.program_id(0)
    size, model = xT.shape[1], xT.shape[0]
    width = k_ref.shape[1]
    fetch = [
        (pltpu.make_async_copy(x, x_buf.at[n], sem.at[0, n]), pltpu.make_async_copy(g, g_buf.at[n], sem.at[1, n]))
        for n, (x, g) in enumerate(zip((x0, x1, x2, x3), (g0, g1, g2, g3)))
    ]
    @pl.when(step == 0)
    def _():
        for x, g in fetch:
            x.start()
            g.start()
    for n, (x, g) in enumerate(fetch):
        @pl.when(step == n)
        def _():
            x.wait()
            g.wait()
    for i in range(0, size, 256):
        xT[:, i : i + 256] = jnp.transpose(x_buf[step, i : i + 256, :].astype(f32)).astype(bf16)
        gT[:, i : i + 256] = jnp.transpose(g_buf[step, i : i + 256, :].astype(f32)).astype(bf16)
    q = jnp.where(step < 2, qa_ref[...], qb_ref[...])
    c = jnp.where(step < 2, ca_ref[...], cb_ref[...])
    pieces = (
        lax.dot_general(xT[...], q, NT, preferred_element_type=f32),
        jnp.dot(xT[...], k_ref[...], preferred_element_type=f32),
        jnp.dot(xT[...], v_ref[...], preferred_element_type=f32),
        lax.dot_general(gT[...], c, NT, preferred_element_type=f32),
    )
    @pl.when(step == 0)
    def _():
        for m, piece in enumerate(pieces):
            acc[m] = piece
    @pl.when(step > 0)
    def _():
        for m, piece in enumerate(pieces):
            acc[m] += piece
    @pl.when(step == 3)
    def _():
        if len(outs) == 1:
            for m in range(4):
                outs[0][:, m * width : (m + 1) * width] = acc[m].astype(bf16)
            return
        rows = model // 8
        for r in range(8):
            at = pl.ds(pl.multiple_of(jnp.bitwise_xor(home, r) * rows, rows), rows)
            to = slice(r // 2 * rows, (r // 2 + 1) * rows)
            for m in range(4):
                outs[r % 2][to, m * width : (m + 1) * width] = acc[m, at, :].astype(bf16)


def halves(width, size):
    return [pl.BlockSpec((width, size), lambda i: (0, jnp.minimum(i, 1))), pl.BlockSpec((width, size), lambda i: (0, jnp.maximum(i, 2) - 2))]


def attn_grads(home, count, tokens, grads, contextT, dqT, dk, dv):
    size, model = tokens[0].shape
    width = dk.shape[1]
    hbm = pl.BlockSpec(memory_space=pltpu.HBM)
    down = pl.BlockSpec((size, width), lambda i: (i, 0))
    parts = 2 if count == 8 else 1
    V = pltpu.VMEM
    return pl.pallas_call(
        grads_kernel,
        grid=(4,),
        out_shape=[jax.ShapeDtypeStruct((model // parts, 4 * width), bf16)] * parts,
        in_specs=[pl.BlockSpec(memory_space=pltpu.SMEM)] + [hbm] * 8 + halves(width, size) * 2 + [down, down],
        out_specs=[pl.BlockSpec((model // parts, 4 * width), lambda i: (0, 0))] * parts,
        scratch_shapes=[V((4, model, width), f32), V((4, size, model), bf16), V((4, size, model), bf16), V((model, size), bf16), V((model, size), bf16),
            pltpu.SemaphoreType.DMA((2, 4))],
        compiler_params=pltpu.CompilerParams(dimension_semantics=("arbitrary",), vmem_limit_bytes=60 << 20),
        cost_estimate=pl.CostEstimate(flops=8 * size * model * width, bytes_accessed=24 * size * model, transcendentals=0),
        name="projection_grads",
    )(home, *tokens, *grads, *contextT, *dqT, dk, dv)


def back_kernel(qa_ref, qb_ref, k_ref, v_ref, wq_ref, wk_ref, wv_ref, near_ref, side_ref, far_ref):
    i = pl.program_id(0)
    size = near_ref.shape[0]
    def block(q_ref):
        q = jnp.transpose(q_ref[...].astype(f32)).astype(bf16)
        total = jnp.dot(q, wq_ref[...], preferred_element_type=f32)
        total = total + jnp.dot(k_ref[...], wk_ref[...], preferred_element_type=f32)
        return (total + jnp.dot(v_ref[...], wv_ref[...], preferred_element_type=f32)).astype(bf16)
    for n, ref in enumerate((near_ref, side_ref, far_ref, side_ref)):
        @pl.when(i == n)
        def _():
            ref[size if n == 3 else 0 : 2 * size if n == 3 else size, :] = block((qa_ref, qb_ref)[n // 2])


def project_back(dqT, dk, dv, wT):
    length, width = dk.shape
    size, model = length // 4, wT.shape[1]
    down = pl.BlockSpec((size, width), lambda i: (i, 0))
    weight = [pl.BlockSpec((width, model), functools.partial(lambda n, i: (n, 0), n)) for n in range(3)]
    return pl.pallas_call(
        back_kernel,
        grid=(4,),
        out_shape=[jax.ShapeDtypeStruct((n * size, model), bf16) for n in (1, 2, 1)],
        in_specs=halves(width, size) + [down, down] + weight,
        out_specs=[pl.BlockSpec((n * size, model), lambda i: (0, 0)) for n in (1, 2, 1)],
        compiler_params=pltpu.CompilerParams(dimension_semantics=("arbitrary",), vmem_limit_bytes=60 << 20),
        cost_estimate=pl.CostEstimate(flops=70 * length * model * width, bytes_accessed=8 * length * model, transcendentals=0),
        name="projection_back",
    )(*dqT, dk, dv, wT, wT, wT)


def hop(value, bit):
    count = lax.axis_size("dp")
    return lax.ppermute(value, "dp", [(i, i ^ bit) for i in range(count)])


def gather_shards(own):
    count = lax.axis_size("dp")
    if count != 8:
        every = lax.all_gather(own, "dp", axis=0, tiled=True)
        return every, every
    even = jnp.concatenate([own] + [hop(own, bit) for bit in (2, 4, 6)], axis=0)
    return even, hop(even, 1)


def later(value, *markers, flops=0):
    anywhere = pl.BlockSpec(memory_space=pl.ANY)
    return pl.pallas_call(
        lambda *refs: None,
        out_shape=jax.ShapeDtypeStruct(value.shape, value.dtype),
        in_specs=[anywhere] * (1 + len(markers)),
        out_specs=anywhere,
        input_output_aliases={0: 0},
        cost_estimate=pl.CostEstimate(flops=flops, bytes_accessed=0, transcendentals=0),
        name="later",
    )(value, *markers)


def exchange(value, bit):
    return lax.ppermute(value, "tensor", [(i, i ^ bit) for i in range(4)])


def row_blocks(own):
    across = exchange(own, 2)
    return [own, exchange(own, 1), across, exchange(across, 1)]


def gather_rows(own):
    return jnp.concatenate(row_blocks(own), axis=0)


def scatter_pieces(near, side, far):
    rows = near.shape[0]
    beside = exchange(side, 1)
    ahead = (far.astype(f32) + beside[rows:].astype(f32)).astype(bf16)
    return (near, beside[:rows], exchange(ahead, 2)), ahead


def gather_blocks(own):
    if lax.axis_size("dp") != 8:
        return [lax.all_gather(jnp.concatenate([own, exchange(own, 2)], axis=1), "dp", axis=0, tiled=True)]
    even = jnp.concatenate([own] + [hop(own, bit) for bit in (2, 4, 6)], axis=0)
    return [even, hop(even, 1), exchange(even, 2)]


def last_blocks(pieces, *markers):
    if len(pieces) == 1:
        return []
    _, odd, beyond = pieces
    cut = odd.shape[0] // 4
    return [later(exchange(odd[:cut], 2), *markers), later(hop(beyond[cut:], 1), *markers)]


def total(*terms):
    result = terms[0].astype(f32)
    for term in terms[1:]:
        result = result + term.astype(f32)
    return result


def fold_both(own, got):
    cut = own.shape[0] // 4
    return total(own[:cut], got[:cut]).astype(bf16), total(own[cut:], got[cut:]).astype(bf16)


def fold_rest(own, got, across, along):
    rows = own.shape[0] // 3
    cut = rows // 4
    part = lambda n: total(own[n * rows : (n + 1) * rows], got[n * rows : (n + 1) * rows])
    odd, beyond = part(1), part(2)
    odd = jnp.concatenate([odd[:cut] + across.astype(f32), odd[cut:]], axis=0).astype(bf16)
    beyond = jnp.concatenate([beyond[:cut], beyond[cut:] + along.astype(f32)], axis=0).astype(bf16)
    return odd, beyond


def fold_even(own, got, odd, beyond):
    rows = own.shape[0] // 3
    return total(own[:rows], got[:rows], odd, beyond).astype(bf16).reshape(4, rows // 4, -1)


def on_device(
    tokens,
    segments,
    query_proj,
    query_bias,
    key_proj,
    value_proj,
    value_bias,
    merge_proj,
    merge_bias,
    first_gain,
    first_shift,
    expand_proj,
    expand_bias,
    shrink_proj,
    shrink_bias,
    second_gain,
    second_shift,
    cotangent,
):
    everyone = ("dp", "tensor")
    part = lax.axis_index("tensor")
    dp = lax.axis_size("dp")
    world = dp * 4
    width = query_proj.shape[1]
    units = expand_proj.shape[1]
    model = width * 4
    share = model // world
    unit_share = units * 4 // world

    shard = jnp.concatenate([query_proj, key_proj, value_proj, merge_proj.T], axis=1)
    shards = gather_shards(shard)
    wide = jnp.concatenate([expand_proj, shrink_proj.T], axis=1)
    pieces = gather_blocks(wide)
    own = jnp.concatenate(
        [query_bias, value_bias, merge_bias, first_gain, first_shift, shrink_bias, second_gain, second_shift, expand_bias]
    )
    rows = tokens.shape[0]
    count = own.shape[0]
    own = jnp.concatenate([own, segments.reshape(-1).astype(f32)])
    slots = -(-own.shape[0] // 1024) * 8
    own = jnp.pad(own, (0, slots * 128 - own.shape[0])).reshape(1, slots, 128)
    vectors = lax.all_to_all(jnp.broadcast_to(own, (world, slots, 128)), everyone, 0, 0, tiled=True)
    vectors = vectors.reshape(world, slots * 128)
    whole = vectors[:, : 8 * share].reshape(world, 8, share).transpose(1, 0, 2).reshape(8, model)
    unit_bias = vectors[:, 8 * share : 8 * share + unit_share].reshape(4, units)
    flips = jnp.bitwise_xor(jnp.arange(4), part)
    seg = lax.dynamic_slice(vectors, (lax.axis_index("dp") * 4, count), (4, rows))
    seg = jnp.take(seg, flips, axis=0).reshape(-1).astype(jnp.int32)
    unit_bias = jnp.take(unit_bias, flips, axis=0)
    query_b = lax.dynamic_slice_in_dim(whole[0], part * width, width)
    value_b = lax.dynamic_slice_in_dim(whole[1], part * width, width)
    rows_b = whole[2:8]

    blocks = row_blocks(tokens)
    segc, segr = seg[:, None], seg[None, :]
    lo, hi = spans(seg)
    flip = (part * (tokens.shape[0] // BK)).astype(jnp.int32).reshape(1)
    home = lax.axis_index("dp").astype(jnp.int32).reshape(1)
    query_t, key_t, value_t, keys, values, attn_wt = project(home, blocks, *shards, dp, query_b, value_b)
    ahead = functools.partial(attn_fwd, 1, query_t, keys, value_t, attn_wt, segc, segr)
    behind = functools.partial(attn_fwd, 0, query_t, keys, value_t, attn_wt, segc, segr)
    context_b, logsum_b, far, side = ahead(later(lo, pieces[0]), hi, flip)
    beside = exchange(side, 1)
    far = (far.astype(f32) + beside.astype(f32)).astype(bf16)
    swapped = [exchange(pieces[0], 1)]
    context_a, logsum_a, a0, side = behind(later(lo, far, swapped[0], *pieces[1:]), hi, flip)
    a1 = exchange(side, 1)
    a2 = later(exchange(far, 2), context_a)

    swapped = swapped + [later(exchange(piece, 1), context_a) for piece in pieces[1:]]
    last = last_blocks(pieces, context_a, a2)
    pieces = pieces + last + swapped + [exchange(piece, 1) for piece in last]
    out = ffn(home, dp, tokens, a0, a1, a2, cotangent, rows_b, unit_bias, pieces)
    output, grad_mixed, mixed_low, row_sums, unit_sums = out[:5]
    beside = exchange(mixed_low, 1)
    across = exchange(mixed_low, 2)
    grads = out[5:]
    local = len(grads) // 2
    swapped = [exchange(grad, 1) for grad in grads[local:]]
    back = functools.partial(attn_bwd, query_t, keys, key_t, values, attn_wt)
    waits = []
    if local == 2:
        waits = fold_both(grads[1], swapped[1])
    dq_a, dk_a, dv_a, q_sums_a = back((mixed_low, beside), context_a, logsum_a, segc, segr, later(lo, *waits), hi, flip)
    across = later(across, q_sums_a)
    mixed_blocks = [mixed_low, beside, across, exchange(across, 1)]
    if local == 2:
        waits = fold_rest(grads[0], swapped[0], later(exchange(waits[0], 2), q_sums_a), later(hop(waits[1], 1), q_sums_a))
    dq_b, dk, dv, q_sums_b, v_sums = back(
        mixed_blocks[2:], context_b, logsum_b, segc, segr, later(lo, *waits), hi, flip, sums=(dk_a, dv_a)
    )
    attn_local = attn_grads(home, dp, blocks, mixed_blocks, (context_a, context_b), (dq_a, dq_b), dk, dv)
    if local == 2:
        waits = [fold_even(grads[0], swapped[0], later(hop(waits[0], 1), attn_local[0]), later(exchange(waits[1], 2), attn_local[0]))]
    even = waits[0] if local == 2 else attn_local[0]
    b0, side, far = project_back((later(dq_a, even), dq_b), dk, dv, attn_wt)

    if local == 2:
        wide_grad = even[0].astype(f32) + sum(later(hop(even[n], 2 * n), b0).astype(f32) for n in (1, 2, 3))
        rows = attn_local[0].shape[0] // 4
        even = total(attn_local[0], later(hop(attn_local[1], 1), wide_grad)).astype(bf16).reshape(4, rows, -1)
        attn_grad = even[0].astype(f32) + sum(hop(even[n], 2 * n).astype(f32) for n in (1, 2, 3))
    else:
        mine = lax.psum_scatter(total(grads[0], swapped[0]).astype(bf16), "dp", scatter_dimension=0, tiled=True)
        wide_grad = total(mine[:, : 2 * units], exchange(mine[:, 2 * units :], 2))
        attn_grad = lax.all_to_all(attn_local[0], "dp", 0, 0, tiled=True)
        attn_grad = jnp.sum(attn_grad.reshape(dp, -1, model).astype(f32), axis=0)
    q_sums = later(q_sums_a, wide_grad) + later(q_sums_b, wide_grad)
    v_sums = later(v_sums, wide_grad)
    mine = (jnp.arange(4) == part).astype(f32)[:, None]
    q_all = (mine * jnp.sum(q_sums, axis=1)[None]).reshape(1, model)
    v_all = (mine * jnp.sum(v_sums, axis=0)[None]).reshape(1, model)
    early = jnp.sum(row_sums, axis=1).reshape(6, world, share).transpose(1, 0, 2).reshape(world, 6 * share)
    late = jnp.concatenate([q_all, v_all], axis=0).reshape(2, world, share).transpose(1, 0, 2).reshape(world, 2 * share)
    u_all = jnp.take(jnp.sum(unit_sums, axis=1), flips, axis=0).reshape(world, unit_share)
    send = jnp.concatenate([late, early, u_all], axis=1)
    send = jnp.pad(send, ((0, 0), (0, slots * 128 - send.shape[1]))).reshape(world, slots, 128)
    got = jnp.sum(lax.all_to_all(send, everyone, 0, 0, tiled=True).reshape(world, slots * 128), axis=0)
    small = [got[n * share : (n + 1) * share] for n in range(8)]

    (b0, b1, b2), _ = scatter_pieces(b0, side, far)
    tokens_grad = (grad_mixed + (b0.astype(f32) + b1.astype(f32) + b2.astype(f32))).astype(bf16)
    querygrad, keygrad, valuegrad, mergegrad = (attn_grad[:, n * width : (n + 1) * width] for n in range(4))
    expandgrad = wide_grad[:, :units]
    shrinkgrad = wide_grad[:, units:].T

    qbiasgrad, vbiasgrad, mbiasgrad, fgaingrad, fshiftgrad, sbiasgrad, sgaingrad, sshiftgrad = small
    ebiasgrad = got[8 * share : 8 * share + unit_share]
    return (
        output,
        tokens_grad,
        querygrad,
        qbiasgrad,
        keygrad,
        valuegrad,
        vbiasgrad,
        mergegrad.T,
        mbiasgrad,
        fgaingrad,
        fshiftgrad,
        expandgrad,
        ebiasgrad,
        shrinkgrad,
        sbiasgrad,
        sgaingrad,
        sshiftgrad,
    )


def solution(mesh):
    return jax.shard_map(
        on_device,
        mesh=mesh,
        in_specs=(
            P(("dp", "tensor"), None),
            P("dp", "tensor"),
            P("dp", "tensor"),
            P(("dp", "tensor")),
            P("dp", "tensor"),
            P("dp", "tensor"),
            P(("dp", "tensor")),
            P("tensor", "dp"),
            P(("dp", "tensor")),
            P(("dp", "tensor")),
            P(("dp", "tensor")),
            P("dp", "tensor"),
            P(("dp", "tensor")),
            P("tensor", "dp"),
            P(("dp", "tensor")),
            P(("dp", "tensor")),
            P(("dp", "tensor")),
            P(("dp", "tensor"), None),
        ),
        out_specs=(
            P(("dp", "tensor"), None),
            P(("dp", "tensor"), None),
            P("dp", "tensor"),
            P(("dp", "tensor")),
            P("dp", "tensor"),
            P("dp", "tensor"),
            P(("dp", "tensor")),
            P("tensor", "dp"),
            P(("dp", "tensor")),
            P(("dp", "tensor")),
            P(("dp", "tensor")),
            P("dp", "tensor"),
            P(("dp", "tensor")),
            P("tensor", "dp"),
            P(("dp", "tensor")),
            P(("dp", "tensor")),
            P(("dp", "tensor")),
        ),
        check_vma=False,
    )
```

```python
import functools

import jax
import jax.numpy as jnp
from jax import lax
from jax.sharding import PartitionSpec as P
from jax.experimental import pallas as pl
from jax.experimental.pallas import tpu as pltpu

HD=64
BQ=512
BK=512
LOG2E=1.4426950408889634
NN=(((1,),(0,)),((),()))
NT=(((1,),(1,)),((),()))
TN=(((0,),(0,)),((),()))
f32=jnp.float32; bf16=jnp.bfloat16

def head_cols(h, heads):
    start=(h//2)*128
    stop=min(start+128, heads*HD)
    return start, stop

def padded(ref, h, heads, rows):
    start, stop = head_cols(h, heads)
    piece = ref[h*HD:(h+1)*HD, rows]
    if stop-start == HD: return piece
    zero = jnp.zeros_like(piece)
    return jnp.concatenate([piece, zero] if h%2==0 else [zero, piece], axis=0)

def fwd_kernel(start_at, lo_ref, hi_ref, flip_ref, q_ref, k_ref, v_ref, w_ref, segc_ref, segr_ref, o_ref, lse_ref, first_ref, second_ref, s_ref):
    heads = q_ref.shape[0]//HD
    i = pl.program_id(0)
    lo = lo_ref[start_at+i]; hi = hi_ref[start_at+i]; flip = flip_ref[0]
    c = LOG2E * HD**-0.5
    qz = [padded(q_ref, h, heads, slice(None)) for h in range(heads)]
    segq = segr_ref[...]
    def one(kb, peaks):
        start = pl.multiple_of(jnp.bitwise_xor(kb, flip)*BK, BK)
        same = segc_ref[pl.ds(start,BK),:] == segq
        new=[]
        for h in range(heads):
            a,b = head_cols(h, heads)
            s = lax.dot_general(k_ref[pl.ds(start,BK), a:b], qz[h], NN, preferred_element_type=f32)
            s = jnp.where(same, s, -1e30)
            s_ref[h, kb-lo] = s
            new.append(jnp.maximum(peaks[h], jnp.max(s.reshape(BK//8,8,BQ),axis=0)))
        return tuple(new)
    peaks = lax.fori_loop(lo, hi, one, tuple(jnp.full((8,BQ),-1e30,f32) for _ in range(heads)))
    peaks = [jnp.max(p,axis=0,keepdims=True)*c for p in peaks]
    def two(kb, carry):
        sums, outs = carry
        start = pl.multiple_of(jnp.bitwise_xor(kb, flip)*BK, BK)
        ns=[];no=[]
        for h in range(heads):
            p = jnp.exp2(s_ref[h, kb-lo]*c - peaks[h])
            ns.append(sums[h]+jnp.sum(p.reshape(BK//8,8,BQ),axis=0))
            no.append(outs[h]+lax.dot_general(v_ref[h*HD:(h+1)*HD, pl.ds(start,BK)], p.astype(bf16), NN, preferred_element_type=f32))
        return tuple(ns),tuple(no)
    sums, outs = lax.fori_loop(lo, hi, two, (tuple(jnp.zeros((8,BQ),f32) for _ in range(heads)), tuple(jnp.zeros((HD,BQ),f32) for _ in range(heads))))
    for h in range(heads):
        total = jnp.sum(sums[h],axis=0,keepdims=True)
        o_ref[h*HD:(h+1)*HD,:] = (outs[h]/total).astype(bf16)
        lse_ref[h:h+1,:] = peaks[h]+jnp.log2(total)
    context = jnp.transpose(o_ref[...].astype(f32)).astype(bf16)
    merged = jnp.dot(context, w_ref[...], preferred_element_type=f32).astype(bf16)
    per = first_ref.shape[0]//BQ
    for n, ref in enumerate((first_ref, second_ref)):
        @pl.when(i//per==n)
        def _():
            ref[pl.ds(pl.multiple_of((i%per)*BQ, BQ), BQ),:] = merged

def attn_fwd(second,qT,k,vT,wT,segc,segr,lo,hi,flip):
    width,length=qT.shape
    size,model=length//4,wT.shape[1]
    heads=width//HD
    blocks=length//BQ//2
    first=blocks*second
    col=pl.BlockSpec((width,BQ),lambda i,*_:(0,first+i))
    whole=pl.BlockSpec((size,model),lambda i,*_:(0,0))
    part=jax.ShapeDtypeStruct((size,model),bf16)
    return pl.pallas_call(
        functools.partial(fwd_kernel,first),
        out_shape=(jax.ShapeDtypeStruct((width,length//2),bf16), jax.ShapeDtypeStruct((8,length//2),f32), part, part),
        grid_spec=pltpu.PrefetchScalarGridSpec(num_scalar_prefetch=3, grid=(blocks,),
            in_specs=[col,
                      pl.BlockSpec((length,width),lambda i,*_:(0,0)),
                      pl.BlockSpec((width,length),lambda i,*_:(0,0)),
                      pl.BlockSpec((width,model),lambda i,*_:(model//width-1,0)),
                      pl.BlockSpec((length,1),lambda i,*_:(0,0)),
                      pl.BlockSpec((1,BQ),lambda i,*_:(0,first+i))],
            out_specs=[pl.BlockSpec((width,BQ),lambda i,*_:(0,i)),pl.BlockSpec((8,BQ),lambda i,*_:(0,i)),whole,whole],
            scratch_shapes=[pltpu.VMEM((heads,length//BK,BK,BQ),f32)]),
        compiler_params=pltpu.CompilerParams(dimension_semantics=("arbitrary",),vmem_limit_bytes=60<<20),
        cost_estimate=pl.CostEstimate(flops=25*length*length*width,bytes_accessed=4*length*width,transcendentals=heads*length*length//4),
        name="attention",
    )(lo,hi,flip,qT,k,vT,wT,segc,segr)

def bwd_kernel(start_at, lo_ref, hi_ref, flip_ref, q_ref, k_ref, kT_ref, v_ref, wT_ref, g0, g1, o_ref, lse_ref, segc_ref, segr_ref, *rest):
    if start_at:
        dk_old, dv_old, dq_ref, dk_ref, dv_ref, qb_ref, vb_ref, dk_acc, dv_acc, do_ref = rest
    else:
        dq_ref, dk_ref, dv_ref, qb_ref, dk_acc, dv_acc, do_ref = rest
    heads = q_ref.shape[0]//HD
    width = q_ref.shape[0]
    i = pl.program_id(0)
    @pl.when(i==0)
    def _():
        dk_acc[...]=jnp.zeros_like(dk_acc); dv_acc[...]=jnp.zeros_like(dv_acc)
        qb_ref[...]=jnp.zeros_like(qb_ref)
    lo = lo_ref[start_at+i]; hi = hi_ref[start_at+i]; flip = flip_ref[0]
    scale = HD**-0.5
    per = g0.shape[0]//BQ
    for n, g_ref in enumerate((g0, g1)):
        @pl.when(i//per==n)
        def _():
            at = pl.multiple_of((i%per)*BQ, BQ)
            do_ref[...] = lax.dot_general(wT_ref[...], g_ref[pl.ds(at,BQ),:], NT, preferred_element_type=f32).astype(bf16)
    c = LOG2E*scale
    qz = [padded(q_ref, h, heads, slice(None)) for h in range(heads)]
    dz = [padded(do_ref, h, heads, slice(None)) for h in range(heads)]
    deltas = [jnp.sum(do_ref[h*HD:(h+1)*HD,:].astype(f32)*o_ref[h*HD:(h+1)*HD,:].astype(f32),axis=0,keepdims=True) for h in range(heads)]
    segq = segr_ref[...]
    def one(kb, dqs):
        start = pl.multiple_of(jnp.bitwise_xor(kb, flip)*BK, BK)
        rows = pl.ds(start,BK)
        same = segc_ref[rows,:] == segq
        out=[]
        parts={}
        for h in range(heads):
            a,b = head_cols(h, heads)
            s = lax.dot_general(k_ref[rows, a:b], qz[h], NN, preferred_element_type=f32)
            p = jnp.exp2(jnp.where(same, s*c - lse_ref[h:h+1,:], -1e30))
            dp = lax.dot_general(v_ref[rows, a:b], dz[h], NN, preferred_element_type=f32)
            ds = (p*((dp-deltas[h])*scale)).astype(bf16)
            dvp = lax.dot_general(p.astype(bf16), dz[h], NT, preferred_element_type=f32)
            dkp = lax.dot_general(ds, qz[h], NT, preferred_element_type=f32)
            if (a,b) in parts: parts[a,b]=(parts[a,b][0]+dkp,parts[a,b][1]+dvp)
            else: parts[a,b]=(dkp,dvp)
            out.append(dqs[h]+lax.dot_general(kT_ref[h*HD:(h+1)*HD, rows], ds, NN, preferred_element_type=f32))
        for (a,b),(dkp,dvp) in parts.items():
            dk_acc[rows,a:b]+=dkp
            dv_acc[rows,a:b]+=dvp
        return tuple(out)
    dqs = lax.fori_loop(lo,hi,one,tuple(jnp.zeros((HD,BQ),f32) for _ in range(heads)))
    for h in range(heads):
        dq_ref[h*HD:(h+1)*HD,:]=dqs[h].astype(bf16)
        part = dqs[h][:,:128]
        for n in range(128,BQ,128): part=part+dqs[h][:,n:n+128]
        qb_ref[h*HD:(h+1)*HD,:]+=part
    @pl.when(i==pl.num_programs(0)-1)
    def _():
        if start_at:
            dk_ref[...]=(dk_acc[...]+dk_old[...]).astype(bf16)
            dv=dv_acc[...]+dv_old[...]
            dv_ref[...]=dv.astype(bf16)
            vb_ref[...]=jnp.sum(dv.reshape(dv.shape[0]//8,8,width),axis=0)
        else:
            dk_ref[...]=dk_acc[...]
            dv_ref[...]=dv_acc[...]

def attn_bwd(qT,k,kT,v,wT,grads,oT,lse,segc,segr,lo,hi,flip,sums=()):
    width,length=qT.shape
    heads=width//HD
    blocks=length//BQ//2
    first=blocks if sums else 0
    col=pl.BlockSpec((width,BQ),lambda i,*_:(0,first+i))
    row=pl.BlockSpec((length,width),lambda i,*_:(0,0))
    tall=jax.ShapeDtypeStruct((length,width),bf16 if sums else f32)
    eight=((jax.ShapeDtypeStruct((8,width),f32),),[pl.BlockSpec((8,width),lambda i,*_:(0,0))]) if sums else ((),[])
    return pl.pallas_call(
        functools.partial(bwd_kernel,first),
        out_shape=(jax.ShapeDtypeStruct((width,length//2),bf16), tall, tall, jax.ShapeDtypeStruct((width,128),f32))+eight[0],
        grid_spec=pltpu.PrefetchScalarGridSpec(num_scalar_prefetch=3, grid=(blocks,),
            in_specs=[col,row,pl.BlockSpec((width,length),lambda i,*_:(0,0)),row,pl.BlockSpec((width,wT.shape[1]),lambda i,*_:(wT.shape[1]//width-1,0))]+[pl.BlockSpec(g.shape,lambda i,*_:(0,0)) for g in grads]+[pl.BlockSpec((width,BQ),lambda i,*_:(0,i)),
                      pl.BlockSpec((8,BQ),lambda i,*_:(0,i)),
                      pl.BlockSpec((length,1),lambda i,*_:(0,0)),
                      pl.BlockSpec((1,BQ),lambda i,*_:(0,first+i))]+[row]*len(sums),
            out_specs=[pl.BlockSpec((width,BQ),lambda i,*_:(0,i)),row,row,pl.BlockSpec((width,128),lambda i,*_:(0,0))]+eight[1],
            scratch_shapes=[pltpu.VMEM((length,width),f32),pltpu.VMEM((length,width),f32),pltpu.VMEM((width,BQ),bf16)]),
        compiler_params=pltpu.CompilerParams(dimension_semantics=("arbitrary",),vmem_limit_bytes=60<<20),
        cost_estimate=pl.CostEstimate(flops=30*length*length*width,bytes_accessed=10*length*width,transcendentals=heads*length*length//4),
        name="attention_back",
    )(lo,hi,flip,qT,k,kT,v,wT,*grads,oT,lse,segc,segr,*sums)

def spans(seg_row):
    length=seg_row.shape[0]
    first=seg_row[::BQ]; last=seg_row[BQ-1::BQ]
    lo=jnp.sum(seg_row[None,:]<first[:,None],axis=1,dtype=jnp.int32)//BK
    hi=(jnp.sum(seg_row[None,:]<=last[:,None],axis=1,dtype=jnp.int32)+BK-1)//BK
    return lo,hi

EPSILON=1e-12
T=256
RC=128

def row_stats(values):
    centre=jnp.mean(values,axis=1,keepdims=True)
    centred=values-centre
    spread=jnp.mean(centred*centred,axis=1,keepdims=True)
    scale=lax.rsqrt(spread+EPSILON)
    return centred*scale, scale

def fold(values):
    return jnp.sum(values.reshape(values.shape[0]//8,8,values.shape[1]),axis=0)

def placements(count, model, blocks):
    if count != 8:
        return [[(r % 2, 0, r % 2, 0, None, model)] for r in range(blocks)]
    rows = model // 8
    every = []
    for r in range(blocks):
        core, beyond = r % 2, r // 2
        block = []
        for shard in range(8):
            odd, place = shard % 2, shard // 2
            if not beyond:
                source, first = odd, place
            elif not odd:
                source, first = 2, place
            else:
                source, first = (3, 0) if place == 0 else (4, place - 1)
            group = beyond and odd
            target = 0 if group else beyond * 2 + odd
            block.append((core * 5 + source, first * rows, core * 2 + group, (target * 4 + place) * rows, shard, rows))
        every.append(block)
    return every


def ffn_kernel(count, home_ref, tok_ref, a0_ref, a1_ref, a2_ref, cot_ref, vec_ref, be_ref, *refs):
    rows, width = tok_ref.shape
    blocks, units = be_ref.shape
    table = placements(count, width, blocks)
    n_in = 1 + max(item[0] for block in table for item in block)
    n_out = 1 + max(item[2] for block in table for item in block)
    pieces, refs = refs[:n_in], refs[n_in:]
    (out_ref, gm_ref, gml_ref, vg_ref, eb_ref), refs = refs[:5], refs[5:]
    grads, refs = refs[:n_out], refs[n_out:]
    we, ws, hl, hlT, hid, xhat, rs1, act, gp, acc, sl, slT, gsum, il, de, dt, wsem, osem = refs
    home = home_ref[0]
    def columns(ref, r, half):
        start = half * units + (r // 2 * 2 * units if len(table[0]) == 1 else 0)
        return ref.at[:, start : start + units]
    def spot(shard, size):
        return pl.ds(0 if shard is None else pl.multiple_of(jnp.bitwise_xor(home, shard) * size, size), size)
    def fetched(r, half):
        return [
            pltpu.make_async_copy(columns(pieces[p], r, half).at[first : first + size], (we, ws)[half].at[r, spot(shard, size)], wsem.at[half, r, k])
            for k, (p, first, _, _, shard, size) in enumerate(table[r])
        ]
    def sent(slot, r):
        return [
            pltpu.make_async_copy((de, dt)[half].at[slot, spot(shard, size)], columns(grads[g], r, half).at[first : first + size], osem.at[half, slot, k])
            for half in range(2)
            for k, (_, _, g, first, shard, size) in enumerate(table[r])
        ]
    for r in range(blocks):
        for half in range(2):
            for c in fetched(r, half):
                c.start()
    mb=vec_ref[0:1,:]; g1=vec_ref[1:2,:]; b1=vec_ref[2:3,:]; sb=vec_ref[3:4,:]; g2=vec_ref[4:5,:]; b2=vec_ref[5:6,:]
    def first(i,_):
        at=pl.ds(pl.multiple_of(i*RC,RC),RC)
        mixed=tok_ref[at,:].astype(f32)+(a0_ref[at,:].astype(f32)+a1_ref[at,:].astype(f32)+a2_ref[at,:].astype(f32))+mb
        z,scale=row_stats(mixed)
        xhat[at,:]=z
        rs1[at,:]=jnp.broadcast_to(scale,(RC,128))
        h=z*g1+b1
        hid[at,:]=h
        hl[at,:]=h.astype(bf16)
        acc[at,:]=jnp.zeros((RC,width),f32)
        return 0
    lax.fori_loop(0,rows//RC,first,0,unroll=2)
    def turn(src,dst):
        def go(i,_):
            at=pl.multiple_of(i*T,T)
            dst[:,pl.ds(at,T)]=jnp.transpose(src[pl.ds(at,T),:].astype(f32)).astype(bf16)
            return 0
        lax.fori_loop(0,rows//T,go,0)
    turn(hl,hlT)
    TG=768; TM=min(512,rows); per=units//T; mt=rows//TM
    def forward(r,_):
        for k in range(blocks):
            @pl.when(r==k)
            def _():
                for c in fetched(k, 0): c.wait()
        def tile(j,_):
            n=pl.multiple_of((j//mt)*T,T); m=pl.multiple_of((j%mt)*TM,TM)
            u=lax.dot_general(hl[pl.ds(m,TM),:],we[r,:,pl.ds(n,T)],NN,preferred_element_type=f32)+be_ref[pl.ds(r,1),pl.ds(n,T)]
            cdf=0.5+0.5*lax.erf(u*(0.5**0.5))
            act[r,pl.ds(m,TM),pl.ds(n,T)]=(u*cdf).astype(bf16)
            gp[r,pl.ds(m,TM),pl.ds(n,T)]=cdf+u*(jnp.exp(-0.5*u*u)*0.3989422804014327)
            return 0
        lax.fori_loop(0,per*mt,tile,0,unroll=3)
        for k in range(blocks):
            @pl.when(r==k)
            def _():
                for c in fetched(k, 1): c.wait()
        def shrink(j,_):
            n=pl.multiple_of((j//mt)*T,T); m=pl.multiple_of((j%mt)*TM,TM)
            acc[pl.ds(m,TM),pl.ds(n,T)]+=lax.dot_general(act[r,pl.ds(m,TM),:],ws[r,pl.ds(n,T),:],NT,preferred_element_type=f32)
            return 0
        lax.fori_loop(0,(width//T)*mt,shrink,0,unroll=3)
        return 0
    lax.fori_loop(0,blocks,forward,0)
    def second(i,sums):
        at=pl.ds(pl.multiple_of(i*RC,RC),RC)
        summed=hid[at,:]+acc[at,:]+sb
        z,scale=row_stats(summed)
        out_ref[at,:]=(z*g2+b2).astype(bf16)
        cot=cot_ref[at,:].astype(f32)
        e=cot*g2
        g=(e-jnp.mean(e,axis=1,keepdims=True)-z*jnp.mean(e*z,axis=1,keepdims=True))*scale
        gsum[at,:]=g
        sl[at,:]=g.astype(bf16)
        acc[at,:]=g
        return (sums[0]+fold(cot*z),sums[1]+fold(cot),sums[2]+fold(g))
    zero=jnp.zeros((8,width),f32)
    sg,sh,sbg=lax.fori_loop(0,rows//RC,second,(zero,zero,zero),unroll=2)
    turn(sl,slT)
    def backward(r,_):
        slot=r%2
        def tile(j,_):
            n=pl.multiple_of((j//mt)*T,T); m=pl.multiple_of((j%mt)*TM,TM)
            ga=lax.dot_general(sl[pl.ds(m,TM),:],ws[r,:,pl.ds(n,T)],NN,preferred_element_type=f32)
            gi=ga*gp[r,pl.ds(m,TM),pl.ds(n,T)]
            il[pl.ds(m,TM),pl.ds(n,T)]=gi.astype(bf16)
            part=fold(gi)
            eb_ref[r,:,pl.ds(n,T)]=jnp.where(m==0,part,eb_ref[r,:,pl.ds(n,T)]+part)
            return 0
        lax.fori_loop(0,per*mt,tile,0,unroll=3)
        def back(j,_):
            n=pl.multiple_of((j//mt)*T,T); m=pl.multiple_of((j%mt)*TM,TM)
            acc[pl.ds(m,TM),pl.ds(n,T)]+=lax.dot_general(il[pl.ds(m,TM),:],we[r,pl.ds(n,T),:],NT,preferred_element_type=f32)
            return 0
        lax.fori_loop(0,(width//T)*mt,back,0,unroll=3)
        for k in range(2,blocks):
            @pl.when(r==k)
            def _():
                for c in sent(k%2,k-2): c.wait()
        def grads(j,_):
            n=pl.multiple_of((j//(width//TG))*T,T); m=pl.multiple_of((j%(width//TG))*TG,TG)
            dt[slot,pl.ds(m,TG),pl.ds(n,T)]=lax.dot_general(slT[pl.ds(m,TG),:],act[r,:,pl.ds(n,T)],NN,preferred_element_type=f32).astype(bf16)
            de[slot,pl.ds(m,TG),pl.ds(n,T)]=lax.dot_general(hlT[pl.ds(m,TG),:],il[:,pl.ds(n,T)],NN,preferred_element_type=f32).astype(bf16)
            return 0
        lax.fori_loop(0,(width//TG)*per,grads,0,unroll=3)
        for k in range(blocks):
            @pl.when(r==k)
            def _():
                for c in sent(k%2,k): c.start()
        return 0
    lax.fori_loop(0,blocks,backward,0)
    def last(i,sums):
        at=pl.ds(pl.multiple_of(i*RC,RC),RC)
        g=acc[at,:]
        z=xhat[at,:]
        e=g*g1
        gm=(e-jnp.mean(e,axis=1,keepdims=True)-z*jnp.mean(e*z,axis=1,keepdims=True))*rs1[at,0:1]
        gm_ref[at,:]=gm
        gml_ref[at,:]=gm.astype(bf16)
        return (sums[0]+fold(g*z),sums[1]+fold(g),sums[2]+fold(gm))
    fg,fs,mbg=lax.fori_loop(0,rows//RC,last,(zero,zero,zero),unroll=2)
    for n,v in enumerate((mbg,fg,fs,sbg,sg,sh)):
        vg_ref[n]=v
    for k in range(max(0,blocks-2),blocks):
        for c in sent(k%2,k): c.wait()

def ffn(home, count, tok, a0, a1, a2, cot, vec, be, pieces):
    rows, width = tok.shape
    blocks, units = be.shape
    table = placements(count, width, blocks)
    n_out = 1 + max(item[2] for block in table for item in block)
    each = len(table[0])
    sizes = [(width * 3 // 2, 2 * units), (width // 2, 2 * units)] * 2 if each > 1 else [(width, blocks * units)] * 2
    grads = tuple(jax.ShapeDtypeStruct(size, bf16) for size in sizes)
    v = pl.BlockSpec(memory_space=pltpu.VMEM)
    h = pl.BlockSpec(memory_space=pltpu.HBM)
    V = pltpu.VMEM
    return pl.pallas_call(
        functools.partial(ffn_kernel, count),
        out_shape=(jax.ShapeDtypeStruct((rows, width), bf16), jax.ShapeDtypeStruct((rows, width), f32), jax.ShapeDtypeStruct((rows, width), bf16),
            jax.ShapeDtypeStruct((6, 8, width), f32), jax.ShapeDtypeStruct((blocks, 8, units), f32)) + grads,
        in_specs=[pl.BlockSpec(memory_space=pltpu.SMEM)] + [v] * 7 + [h] * len(pieces),
        out_specs=[v] * 5 + [h] * n_out,
        scratch_shapes=[V((blocks, width, units), bf16), V((blocks, width, units), bf16),
            V((rows, width), bf16), V((width, rows), bf16), V((rows, width), f32), V((rows, width), f32), V((rows, 128), f32),
            V((blocks, rows, units), bf16), V((blocks, rows, units), f32), V((rows, width), f32), V((rows, width), bf16), V((width, rows), bf16), V((rows, width), f32),
            V((rows, units), bf16), V((2, width, units), bf16), V((2, width, units), bf16),
            pltpu.SemaphoreType.DMA((2, blocks, each)), pltpu.SemaphoreType.DMA((2, 2, each))],
        compiler_params=pltpu.CompilerParams(vmem_limit_bytes=60 << 20),
        cost_estimate=pl.CostEstimate(flops=30 * rows * width * units * blocks, bytes_accessed=8 * blocks * width * units, transcendentals=2 * rows * units * blocks),
        name="feed_forward",
    )(home, tok, a0, a1, a2, cot, vec, be, *pieces)


def proj_kernel(home_ref, x0, x1, x2, x3, wa_ref, wb_ref, bq_ref, bvc_ref, bvr_ref,
                q_ref, kT_ref, vT_ref, k_ref, v_ref, wT, w_ref, wk, wv, x_buf, sem, x_sem):
    model = w_ref.shape[0]
    count, rows = sem.shape[0], model // sem.shape[0]
    width = q_ref.shape[0]
    home = home_ref[0]
    step = pl.program_id(0)
    def copy(r):
        src = (wa_ref, wb_ref)[r % 2].at[(r // 2) * rows : (r // 2 + 1) * rows]
        at = pl.multiple_of(jnp.bitwise_xor(home, r) * rows, rows)
        return pltpu.make_async_copy(src, w_ref.at[pl.ds(at, rows)], sem.at[r])
    if wa_ref.shape[0] == model:
        count = 1
        copy = lambda r: pltpu.make_async_copy(wa_ref, w_ref, sem.at[r])
    fetch = [pltpu.make_async_copy(x, x_buf.at[n], x_sem.at[n]) for n, x in enumerate((x0, x1, x2, x3))]
    @pl.when(step == 0)
    def _():
        for r in range(count):
            copy(r).start()
        for x in fetch:
            x.start()
        for r in range(count):
            copy(r).wait()
        def turn(i, _):
            at = pl.multiple_of(i * 256, 256)
            wT[:, pl.ds(at, 256)] = jnp.transpose(w_ref[pl.ds(at, 256), :].astype(f32)).astype(bf16)
            return 0
        lax.fori_loop(0, model // 256, turn, 0)
        wk[...] = w_ref[:, width : 2 * width]
        wv[...] = w_ref[:, 2 * width : 3 * width]
    for n, x in enumerate(fetch):
        @pl.when(step == n)
        def _():
            x.wait()
    x = x_buf[step]
    k_ref[...] = jnp.dot(x, wk[...], preferred_element_type=f32).astype(bf16)
    v_ref[...] = (jnp.dot(x, wv[...], preferred_element_type=f32) + bvr_ref[...]).astype(bf16)
    q_ref[...] = (lax.dot_general(wT[0:width], x, NT, preferred_element_type=f32) + bq_ref[...]).astype(bf16)
    kT_ref[...] = lax.dot_general(wT[width : 2 * width], x, NT, preferred_element_type=f32).astype(bf16)
    vT_ref[...] = (lax.dot_general(wT[2 * width : 3 * width], x, NT, preferred_element_type=f32) + bvc_ref[...]).astype(bf16)


def project(home, tokens, wa, wb, count, bq, bv):
    size, model = tokens[0].shape
    length = 4 * size
    width = bq.shape[0]
    hbm = pl.BlockSpec(memory_space=pltpu.HBM)
    column = pl.BlockSpec((width, 1), lambda i: (0, 0))
    tall = jax.ShapeDtypeStruct((length, width), bf16)
    flat = jax.ShapeDtypeStruct((width, length), bf16)
    across = pl.BlockSpec((width, size), lambda i: (0, i))
    down = pl.BlockSpec((size, width), lambda i: (i, 0))
    return pl.pallas_call(
        proj_kernel,
        grid=(4,),
        out_shape=(flat, flat, flat, tall, tall, jax.ShapeDtypeStruct((model, model), bf16)),
        in_specs=[pl.BlockSpec(memory_space=pltpu.SMEM)] + [hbm] * 6 + [column, column, pl.BlockSpec((1, width), lambda i: (0, 0))],
        out_specs=[across, across, across, down, down, pl.BlockSpec((model, model), lambda i: (0, 0))],
        scratch_shapes=[pltpu.VMEM((model, model), bf16), pltpu.VMEM((model, width), bf16), pltpu.VMEM((model, width), bf16),
            pltpu.VMEM((4, size, model), bf16), pltpu.SemaphoreType.DMA((count,)), pltpu.SemaphoreType.DMA((4,))],
        compiler_params=pltpu.CompilerParams(dimension_semantics=("arbitrary",), vmem_limit_bytes=60 << 20),
        cost_estimate=pl.CostEstimate(flops=30 * length * model * width, bytes_accessed=4 * length * model, transcendentals=0),
        name="projection",
    )(home, *tokens, wa, wb, bq[:, None], bv[:, None], bv[None, :])


def grads_kernel(home_ref, x0, x1, x2, x3, g0, g1, g2, g3, ca_ref, cb_ref, qa_ref, qb_ref, k_ref, v_ref, *rest):
    *outs, acc, x_buf, g_buf, xT, gT, sem = rest
    home = home_ref[0]
    step = pl.program_id(0)
    size, model = xT.shape[1], xT.shape[0]
    width = k_ref.shape[1]
    fetch = [
        (pltpu.make_async_copy(x, x_buf.at[n], sem.at[0, n]), pltpu.make_async_copy(g, g_buf.at[n], sem.at[1, n]))
        for n, (x, g) in enumerate(zip((x0, x1, x2, x3), (g0, g1, g2, g3)))
    ]
    @pl.when(step == 0)
    def _():
        for x, g in fetch:
            x.start()
            g.start()
    for n, (x, g) in enumerate(fetch):
        @pl.when(step == n)
        def _():
            x.wait()
            g.wait()
    for i in range(0, size, 256):
        xT[:, i : i + 256] = jnp.transpose(x_buf[step, i : i + 256, :].astype(f32)).astype(bf16)
        gT[:, i : i + 256] = jnp.transpose(g_buf[step, i : i + 256, :].astype(f32)).astype(bf16)
    q = jnp.where(step < 2, qa_ref[...], qb_ref[...])
    c = jnp.where(step < 2, ca_ref[...], cb_ref[...])
    pieces = (
        lax.dot_general(xT[...], q, NT, preferred_element_type=f32),
        jnp.dot(xT[...], k_ref[...], preferred_element_type=f32),
        jnp.dot(xT[...], v_ref[...], preferred_element_type=f32),
        lax.dot_general(gT[...], c, NT, preferred_element_type=f32),
    )
    @pl.when(step == 0)
    def _():
        for m, piece in enumerate(pieces):
            acc[m] = piece
    @pl.when(step > 0)
    def _():
        for m, piece in enumerate(pieces):
            acc[m] += piece
    @pl.when(step == 3)
    def _():
        if len(outs) == 1:
            for m in range(4):
                outs[0][:, m * width : (m + 1) * width] = acc[m].astype(bf16)
            return
        rows = model // 8
        for r in range(8):
            at = pl.ds(pl.multiple_of(jnp.bitwise_xor(home, r) * rows, rows), rows)
            to = slice(r // 2 * rows, (r // 2 + 1) * rows)
            for m in range(4):
                outs[r % 2][to, m * width : (m + 1) * width] = acc[m, at, :].astype(bf16)


def halves(width, size):
    return [pl.BlockSpec((width, size), lambda i: (0, jnp.minimum(i, 1))), pl.BlockSpec((width, size), lambda i: (0, jnp.maximum(i, 2) - 2))]


def attn_grads(home, count, tokens, grads, contextT, dqT, dk, dv):
    size, model = tokens[0].shape
    width = dk.shape[1]
    hbm = pl.BlockSpec(memory_space=pltpu.HBM)
    down = pl.BlockSpec((size, width), lambda i: (i, 0))
    parts = 2 if count == 8 else 1
    V = pltpu.VMEM
    return pl.pallas_call(
        grads_kernel,
        grid=(4,),
        out_shape=[jax.ShapeDtypeStruct((model // parts, 4 * width), bf16)] * parts,
        in_specs=[pl.BlockSpec(memory_space=pltpu.SMEM)] + [hbm] * 8 + halves(width, size) * 2 + [down, down],
        out_specs=[pl.BlockSpec((model // parts, 4 * width), lambda i: (0, 0))] * parts,
        scratch_shapes=[V((4, model, width), f32), V((4, size, model), bf16), V((4, size, model), bf16), V((model, size), bf16), V((model, size), bf16),
            pltpu.SemaphoreType.DMA((2, 4))],
        compiler_params=pltpu.CompilerParams(dimension_semantics=("arbitrary",), vmem_limit_bytes=60 << 20),
        cost_estimate=pl.CostEstimate(flops=8 * size * model * width, bytes_accessed=24 * size * model, transcendentals=0),
        name="projection_grads",
    )(home, *tokens, *grads, *contextT, *dqT, dk, dv)


def back_kernel(qa_ref, qb_ref, k_ref, v_ref, wq_ref, wk_ref, wv_ref, near_ref, side_ref, far_ref):
    i = pl.program_id(0)
    size = near_ref.shape[0]
    def block(q_ref):
        q = jnp.transpose(q_ref[...].astype(f32)).astype(bf16)
        total = jnp.dot(q, wq_ref[...], preferred_element_type=f32)
        total = total + jnp.dot(k_ref[...], wk_ref[...], preferred_element_type=f32)
        return (total + jnp.dot(v_ref[...], wv_ref[...], preferred_element_type=f32)).astype(bf16)
    for n, ref in enumerate((near_ref, side_ref, far_ref, side_ref)):
        @pl.when(i == n)
        def _():
            ref[size if n == 3 else 0 : 2 * size if n == 3 else size, :] = block((qa_ref, qb_ref)[n // 2])


def project_back(dqT, dk, dv, wT):
    length, width = dk.shape
    size, model = length // 4, wT.shape[1]
    down = pl.BlockSpec((size, width), lambda i: (i, 0))
    weight = [pl.BlockSpec((width, model), functools.partial(lambda n, i: (n, 0), n)) for n in range(3)]
    return pl.pallas_call(
        back_kernel,
        grid=(4,),
        out_shape=[jax.ShapeDtypeStruct((n * size, model), bf16) for n in (1, 2, 1)],
        in_specs=halves(width, size) + [down, down] + weight,
        out_specs=[pl.BlockSpec((n * size, model), lambda i: (0, 0)) for n in (1, 2, 1)],
        compiler_params=pltpu.CompilerParams(dimension_semantics=("arbitrary",), vmem_limit_bytes=60 << 20),
        cost_estimate=pl.CostEstimate(flops=70 * length * model * width, bytes_accessed=8 * length * model, transcendentals=0),
        name="projection_back",
    )(*dqT, dk, dv, wT, wT, wT)


def hop(value, bit):
    count = lax.axis_size("dp")
    return lax.ppermute(value, "dp", [(i, i ^ bit) for i in range(count)])


def gather_shards(own):
    count = lax.axis_size("dp")
    if count != 8:
        every = lax.all_gather(own, "dp", axis=0, tiled=True)
        return every, every
    even = jnp.concatenate([own] + [hop(own, bit) for bit in (2, 4, 6)], axis=0)
    return even, hop(even, 1)


def later(value, *markers, flops=0):
    anywhere = pl.BlockSpec(memory_space=pl.ANY)
    return pl.pallas_call(
        lambda *refs: None,
        out_shape=jax.ShapeDtypeStruct(value.shape, value.dtype),
        in_specs=[anywhere] * (1 + len(markers)),
        out_specs=anywhere,
        input_output_aliases={0: 0},
        cost_estimate=pl.CostEstimate(flops=flops, bytes_accessed=0, transcendentals=0),
        name="later",
    )(value, *markers)


def exchange(value, bit):
    return lax.ppermute(value, "tensor", [(i, i ^ bit) for i in range(4)])


def row_blocks(own):
    across = exchange(own, 2)
    return [own, exchange(own, 1), across, exchange(across, 1)]


def gather_rows(own):
    return jnp.concatenate(row_blocks(own), axis=0)


def scatter_pieces(near, side, far):
    rows = near.shape[0]
    beside = exchange(side, 1)
    ahead = (far.astype(f32) + beside[rows:].astype(f32)).astype(bf16)
    return (near, beside[:rows], exchange(ahead, 2)), ahead


def gather_blocks(own):
    if lax.axis_size("dp") != 8:
        return [lax.all_gather(jnp.concatenate([own, exchange(own, 2)], axis=1), "dp", axis=0, tiled=True)]
    even = jnp.concatenate([own] + [hop(own, bit) for bit in (2, 4, 6)], axis=0)
    return [even, hop(even, 1), exchange(even, 2)]


def last_blocks(pieces, *markers):
    if len(pieces) == 1:
        return []
    _, odd, beyond = pieces
    cut = odd.shape[0] // 4
    return [later(exchange(odd[:cut], 2), *markers), later(hop(beyond[cut:], 1), *markers)]


def total(*terms):
    result = terms[0].astype(f32)
    for term in terms[1:]:
        result = result + term.astype(f32)
    return result


def fold_both(own, got):
    cut = own.shape[0] // 4
    return total(own[:cut], got[:cut]).astype(bf16), total(own[cut:], got[cut:]).astype(bf16)


def fold_rest(own, got, across, along):
    rows = own.shape[0] // 3
    cut = rows // 4
    part = lambda n: total(own[n * rows : (n + 1) * rows], got[n * rows : (n + 1) * rows])
    odd, beyond = part(1), part(2)
    odd = jnp.concatenate([odd[:cut] + across.astype(f32), odd[cut:]], axis=0).astype(bf16)
    beyond = jnp.concatenate([beyond[:cut], beyond[cut:] + along.astype(f32)], axis=0).astype(bf16)
    return odd, beyond


def fold_even(own, got, odd, beyond):
    rows = own.shape[0] // 3
    return total(own[:rows], got[:rows], odd, beyond).astype(bf16).reshape(4, rows // 4, -1)


def on_device(
    tokens,
    segments,
    query_proj,
    query_bias,
    key_proj,
    value_proj,
    value_bias,
    merge_proj,
    merge_bias,
    first_gain,
    first_shift,
    expand_proj,
    expand_bias,
    shrink_proj,
    shrink_bias,
    second_gain,
    second_shift,
    cotangent,
):
    everyone = ("dp", "tensor")
    part = lax.axis_index("tensor")
    dp = lax.axis_size("dp")
    world = dp * 4
    width = query_proj.shape[1]
    units = expand_proj.shape[1]
    model = width * 4
    share = model // world
    unit_share = units * 4 // world

    shard = jnp.concatenate([query_proj, key_proj, value_proj, merge_proj.T], axis=1)
    shards = gather_shards(shard)
    wide = jnp.concatenate([expand_proj, shrink_proj.T], axis=1)
    pieces = gather_blocks(wide)
    own = jnp.concatenate(
        [query_bias, value_bias, merge_bias, first_gain, first_shift, shrink_bias, second_gain, second_shift, expand_bias]
    )
    rows = tokens.shape[0]
    count = own.shape[0]
    own = jnp.concatenate([own, segments.reshape(-1).astype(f32)])
    slots = -(-own.shape[0] // 1024) * 8
    own = jnp.pad(own, (0, slots * 128 - own.shape[0])).reshape(1, slots, 128)
    vectors = lax.all_to_all(jnp.broadcast_to(own, (world, slots, 128)), everyone, 0, 0, tiled=True)
    vectors = vectors.reshape(world, slots * 128)
    whole = vectors[:, : 8 * share].reshape(world, 8, share).transpose(1, 0, 2).reshape(8, model)
    unit_bias = vectors[:, 8 * share : 8 * share + unit_share].reshape(4, units)
    flips = jnp.bitwise_xor(jnp.arange(4), part)
    seg = lax.dynamic_slice(vectors, (lax.axis_index("dp") * 4, count), (4, rows))
    seg = jnp.take(seg, flips, axis=0).reshape(-1).astype(jnp.int32)
    unit_bias = jnp.take(unit_bias, flips, axis=0)
    query_b = lax.dynamic_slice_in_dim(whole[0], part * width, width)
    value_b = lax.dynamic_slice_in_dim(whole[1], part * width, width)
    rows_b = whole[2:8]

    blocks = row_blocks(tokens)
    segc, segr = seg[:, None], seg[None, :]
    lo, hi = spans(seg)
    flip = (part * (tokens.shape[0] // BK)).astype(jnp.int32).reshape(1)
    home = lax.axis_index("dp").astype(jnp.int32).reshape(1)
    query_t, key_t, value_t, keys, values, attn_wt = project(home, blocks, *shards, dp, query_b, value_b)
    ahead = functools.partial(attn_fwd, 1, query_t, keys, value_t, attn_wt, segc, segr)
    behind = functools.partial(attn_fwd, 0, query_t, keys, value_t, attn_wt, segc, segr)
    context_b, logsum_b, far, side = ahead(later(lo, pieces[0]), hi, flip)
    beside = exchange(side, 1)
    far = (far.astype(f32) + beside.astype(f32)).astype(bf16)
    swapped = [exchange(pieces[0], 1)]
    context_a, logsum_a, a0, side = behind(later(lo, far, swapped[0], *pieces[1:]), hi, flip)
    a1 = exchange(side, 1)
    a2 = later(exchange(far, 2), context_a)

    swapped = swapped + [later(exchange(piece, 1), context_a) for piece in pieces[1:]]
    last = last_blocks(pieces, context_a, a2)
    pieces = pieces + last + swapped + [exchange(piece, 1) for piece in last]
    out = ffn(home, dp, tokens, a0, a1, a2, cotangent, rows_b, unit_bias, pieces)
    output, grad_mixed, mixed_low, row_sums, unit_sums = out[:5]
    beside = exchange(mixed_low, 1)
    across = exchange(mixed_low, 2)
    grads = out[5:]
    local = len(grads) // 2
    swapped = [exchange(grad, 1) for grad in grads[local:]]
    back = functools.partial(attn_bwd, query_t, keys, key_t, values, attn_wt)
    waits = []
    if local == 2:
        waits = fold_both(grads[1], swapped[1])
    dq_a, dk_a, dv_a, q_sums_a = back((mixed_low, beside), context_a, logsum_a, segc, segr, later(lo, *waits), hi, flip)
    across = later(across, q_sums_a)
    mixed_blocks = [mixed_low, beside, across, exchange(across, 1)]
    if local == 2:
        waits = fold_rest(grads[0], swapped[0], later(exchange(waits[0], 2), q_sums_a), later(hop(waits[1], 1), q_sums_a))
    dq_b, dk, dv, q_sums_b, v_sums = back(
        mixed_blocks[2:], context_b, logsum_b, segc, segr, later(lo, *waits), hi, flip, sums=(dk_a, dv_a)
    )
    attn_local = attn_grads(home, dp, blocks, mixed_blocks, (context_a, context_b), (dq_a, dq_b), dk, dv)
    if local == 2:
        waits = [fold_even(grads[0], swapped[0], later(hop(waits[0], 1), attn_local[0]), later(exchange(waits[1], 2), attn_local[0]))]
    even = waits[0] if local == 2 else attn_local[0]
    b0, side, far = project_back((later(dq_a, even), dq_b), dk, dv, attn_wt)

    q_sums = later(q_sums_a, even) + later(q_sums_b, even)
    v_sums = later(v_sums, even)
    mine = (jnp.arange(4) == part).astype(f32)[:, None]
    q_all = (mine * jnp.sum(q_sums, axis=1)[None]).reshape(1, model)
    v_all = (mine * jnp.sum(v_sums, axis=0)[None]).reshape(1, model)
    early = jnp.sum(row_sums, axis=1).reshape(6, world, share).transpose(1, 0, 2).reshape(world, 6 * share)
    late = jnp.concatenate([q_all, v_all], axis=0).reshape(2, world, share).transpose(1, 0, 2).reshape(world, 2 * share)
    u_all = jnp.take(jnp.sum(unit_sums, axis=1), flips, axis=0).reshape(world, unit_share)
    send = jnp.concatenate([late, early, u_all], axis=1)
    send = jnp.pad(send, ((0, 0), (0, slots * 128 - send.shape[1]))).reshape(world, slots, 128)
    got = jnp.sum(lax.all_to_all(send, everyone, 0, 0, tiled=True).reshape(world, slots * 128), axis=0)
    small = [got[n * share : (n + 1) * share] for n in range(8)]

    if local == 2:
        y_came = hop(attn_local[1], 1)
        wide_grad = even[0].astype(f32) + sum(later(hop(even[n], 2 * n), b0, got, y_came).astype(f32) for n in (1, 2, 3))
        rows = attn_local[0].shape[0] // 4
        even = total(attn_local[0], y_came).astype(bf16).reshape(4, rows, -1)
        attn_grad = even[0].astype(f32) + sum(hop(even[n], 2 * n).astype(f32) for n in (1, 2, 3))
    else:
        mine = lax.psum_scatter(total(grads[0], swapped[0]).astype(bf16), "dp", scatter_dimension=0, tiled=True)
        wide_grad = total(mine[:, : 2 * units], exchange(mine[:, 2 * units :], 2))
        attn_grad = lax.all_to_all(attn_local[0], "dp", 0, 0, tiled=True)
        attn_grad = jnp.sum(attn_grad.reshape(dp, -1, model).astype(f32), axis=0)
    (b0, b1, b2), _ = scatter_pieces(b0, later(side, got), far)
    tokens_grad = (grad_mixed + (b0.astype(f32) + b1.astype(f32) + b2.astype(f32))).astype(bf16)
    querygrad, keygrad, valuegrad, mergegrad = (attn_grad[:, n * width : (n + 1) * width] for n in range(4))
    expandgrad = wide_grad[:, :units]
    shrinkgrad = wide_grad[:, units:].T

    qbiasgrad, vbiasgrad, mbiasgrad, fgaingrad, fshiftgrad, sbiasgrad, sgaingrad, sshiftgrad = small
    ebiasgrad = got[8 * share : 8 * share + unit_share]
    return (
        output,
        tokens_grad,
        querygrad,
        qbiasgrad,
        keygrad,
        valuegrad,
        vbiasgrad,
        mergegrad.T,
        mbiasgrad,
        fgaingrad,
        fshiftgrad,
        expandgrad,
        ebiasgrad,
        shrinkgrad,
        sbiasgrad,
        sgaingrad,
        sshiftgrad,
    )


def solution(mesh):
    return jax.shard_map(
        on_device,
        mesh=mesh,
        in_specs=(
            P(("dp", "tensor"), None),
            P("dp", "tensor"),
            P("dp", "tensor"),
            P(("dp", "tensor")),
            P("dp", "tensor"),
            P("dp", "tensor"),
            P(("dp", "tensor")),
            P("tensor", "dp"),
            P(("dp", "tensor")),
            P(("dp", "tensor")),
            P(("dp", "tensor")),
            P("dp", "tensor"),
            P(("dp", "tensor")),
            P("tensor", "dp"),
            P(("dp", "tensor")),
            P(("dp", "tensor")),
            P(("dp", "tensor")),
            P(("dp", "tensor"), None),
        ),
        out_specs=(
            P(("dp", "tensor"), None),
            P(("dp", "tensor"), None),
            P("dp", "tensor"),
            P(("dp", "tensor")),
            P("dp", "tensor"),
            P("dp", "tensor"),
            P(("dp", "tensor")),
            P("tensor", "dp"),
            P(("dp", "tensor")),
            P(("dp", "tensor")),
            P(("dp", "tensor")),
            P("dp", "tensor"),
            P(("dp", "tensor")),
            P("tensor", "dp"),
            P(("dp", "tensor")),
            P(("dp", "tensor")),
            P(("dp", "tensor")),
        ),
        check_vma=False,
    )
```

```python
import functools

import jax
import jax.numpy as jnp
from jax import lax
from jax.sharding import PartitionSpec as P
from jax.experimental import pallas as pl
from jax.experimental.pallas import tpu as pltpu

HD=64
BQ=512
BK=512
LOG2E=1.4426950408889634
NN=(((1,),(0,)),((),()))
NT=(((1,),(1,)),((),()))
TN=(((0,),(0,)),((),()))
f32=jnp.float32; bf16=jnp.bfloat16

def head_cols(h, heads):
    start=(h//2)*128
    stop=min(start+128, heads*HD)
    return start, stop

def padded(ref, h, heads, rows):
    start, stop = head_cols(h, heads)
    piece = ref[h*HD:(h+1)*HD, rows]
    if stop-start == HD: return piece
    zero = jnp.zeros_like(piece)
    return jnp.concatenate([piece, zero] if h%2==0 else [zero, piece], axis=0)

def fwd_kernel(start_at, lo_ref, hi_ref, flip_ref, q_ref, k_ref, v_ref, w_ref, segc_ref, segr_ref, o_ref, lse_ref, first_ref, second_ref, s_ref):
    heads = q_ref.shape[0]//HD
    i = pl.program_id(0)
    lo = lo_ref[start_at+i]; hi = hi_ref[start_at+i]; flip = flip_ref[0]
    c = LOG2E * HD**-0.5
    qz = [padded(q_ref, h, heads, slice(None)) for h in range(heads)]
    segq = segr_ref[...]
    def one(kb, peaks):
        start = pl.multiple_of(jnp.bitwise_xor(kb, flip)*BK, BK)
        same = segc_ref[pl.ds(start,BK),:] == segq
        new=[]
        for h in range(heads):
            a,b = head_cols(h, heads)
            s = lax.dot_general(k_ref[pl.ds(start,BK), a:b], qz[h], NN, preferred_element_type=f32)
            s = jnp.where(same, s, -1e30)
            s_ref[h, kb-lo] = s
            new.append(jnp.maximum(peaks[h], jnp.max(s.reshape(BK//8,8,BQ),axis=0)))
        return tuple(new)
    peaks = lax.fori_loop(lo, hi, one, tuple(jnp.full((8,BQ),-1e30,f32) for _ in range(heads)))
    peaks = [jnp.max(p,axis=0,keepdims=True)*c for p in peaks]
    def two(kb, carry):
        sums, outs = carry
        start = pl.multiple_of(jnp.bitwise_xor(kb, flip)*BK, BK)
        ns=[];no=[]
        for h in range(heads):
            p = jnp.exp2(s_ref[h, kb-lo]*c - peaks[h])
            ns.append(sums[h]+jnp.sum(p.reshape(BK//8,8,BQ),axis=0))
            no.append(outs[h]+lax.dot_general(v_ref[h*HD:(h+1)*HD, pl.ds(start,BK)], p.astype(bf16), NN, preferred_element_type=f32))
        return tuple(ns),tuple(no)
    sums, outs = lax.fori_loop(lo, hi, two, (tuple(jnp.zeros((8,BQ),f32) for _ in range(heads)), tuple(jnp.zeros((HD,BQ),f32) for _ in range(heads))))
    for h in range(heads):
        total = jnp.sum(sums[h],axis=0,keepdims=True)
        o_ref[h*HD:(h+1)*HD,:] = (outs[h]/total).astype(bf16)
        lse_ref[h:h+1,:] = peaks[h]+jnp.log2(total)
    context = jnp.transpose(o_ref[...].astype(f32)).astype(bf16)
    merged = jnp.dot(context, w_ref[...], preferred_element_type=f32).astype(bf16)
    per = first_ref.shape[0]//BQ
    for n, ref in enumerate((first_ref, second_ref)):
        @pl.when(i//per==n)
        def _():
            ref[pl.ds(pl.multiple_of((i%per)*BQ, BQ), BQ),:] = merged

def attn_fwd(second,qT,k,vT,wT,segc,segr,lo,hi,flip):
    width,length=qT.shape
    size,model=length//4,wT.shape[1]
    heads=width//HD
    blocks=length//BQ//2
    first=blocks*second
    col=pl.BlockSpec((width,BQ),lambda i,*_:(0,first+i))
    whole=pl.BlockSpec((size,model),lambda i,*_:(0,0))
    part=jax.ShapeDtypeStruct((size,model),bf16)
    return pl.pallas_call(
        functools.partial(fwd_kernel,first),
        out_shape=(jax.ShapeDtypeStruct((width,length//2),bf16), jax.ShapeDtypeStruct((8,length//2),f32), part, part),
        grid_spec=pltpu.PrefetchScalarGridSpec(num_scalar_prefetch=3, grid=(blocks,),
            in_specs=[col,
                      pl.BlockSpec((length,width),lambda i,*_:(0,0)),
                      pl.BlockSpec((width,length),lambda i,*_:(0,0)),
                      pl.BlockSpec((width,model),lambda i,*_:(model//width-1,0)),
                      pl.BlockSpec((length,1),lambda i,*_:(0,0)),
                      pl.BlockSpec((1,BQ),lambda i,*_:(0,first+i))],
            out_specs=[pl.BlockSpec((width,BQ),lambda i,*_:(0,i)),pl.BlockSpec((8,BQ),lambda i,*_:(0,i)),whole,whole],
            scratch_shapes=[pltpu.VMEM((heads,length//BK,BK,BQ),f32)]),
        compiler_params=pltpu.CompilerParams(dimension_semantics=("arbitrary",),vmem_limit_bytes=60<<20),
        cost_estimate=pl.CostEstimate(flops=25*length*length*width,bytes_accessed=4*length*width,transcendentals=heads*length*length//4),
        name="attention",
    )(lo,hi,flip,qT,k,vT,wT,segc,segr)

def bwd_kernel(start_at, lo_ref, hi_ref, flip_ref, q_ref, k_ref, kT_ref, v_ref, wT_ref, g0, g1, o_ref, lse_ref, segc_ref, segr_ref, *rest):
    if start_at:
        dk_old, dv_old, dq_ref, dk_ref, dv_ref, qb_ref, vb_ref, dk_acc, dv_acc, do_ref = rest
    else:
        dq_ref, dk_ref, dv_ref, qb_ref, dk_acc, dv_acc, do_ref = rest
    heads = q_ref.shape[0]//HD
    width = q_ref.shape[0]
    i = pl.program_id(0)
    @pl.when(i==0)
    def _():
        dk_acc[...]=jnp.zeros_like(dk_acc); dv_acc[...]=jnp.zeros_like(dv_acc)
        qb_ref[...]=jnp.zeros_like(qb_ref)
    lo = lo_ref[start_at+i]; hi = hi_ref[start_at+i]; flip = flip_ref[0]
    scale = HD**-0.5
    per = g0.shape[0]//BQ
    for n, g_ref in enumerate((g0, g1)):
        @pl.when(i//per==n)
        def _():
            at = pl.multiple_of((i%per)*BQ, BQ)
            do_ref[...] = lax.dot_general(wT_ref[...], g_ref[pl.ds(at,BQ),:], NT, preferred_element_type=f32).astype(bf16)
    c = LOG2E*scale
    qz = [padded(q_ref, h, heads, slice(None)) for h in range(heads)]
    dz = [padded(do_ref, h, heads, slice(None)) for h in range(heads)]
    deltas = [jnp.sum(do_ref[h*HD:(h+1)*HD,:].astype(f32)*o_ref[h*HD:(h+1)*HD,:].astype(f32),axis=0,keepdims=True) for h in range(heads)]
    segq = segr_ref[...]
    def one(kb, dqs):
        start = pl.multiple_of(jnp.bitwise_xor(kb, flip)*BK, BK)
        rows = pl.ds(start,BK)
        same = segc_ref[rows,:] == segq
        out=[]
        parts={}
        for h in range(heads):
            a,b = head_cols(h, heads)
            s = lax.dot_general(k_ref[rows, a:b], qz[h], NN, preferred_element_type=f32)
            p = jnp.exp2(jnp.where(same, s*c - lse_ref[h:h+1,:], -1e30))
            dp = lax.dot_general(v_ref[rows, a:b], dz[h], NN, preferred_element_type=f32)
            ds = (p*((dp-deltas[h])*scale)).astype(bf16)
            dvp = lax.dot_general(p.astype(bf16), dz[h], NT, preferred_element_type=f32)
            dkp = lax.dot_general(ds, qz[h], NT, preferred_element_type=f32)
            if (a,b) in parts: parts[a,b]=(parts[a,b][0]+dkp,parts[a,b][1]+dvp)
            else: parts[a,b]=(dkp,dvp)
            out.append(dqs[h]+lax.dot_general(kT_ref[h*HD:(h+1)*HD, rows], ds, NN, preferred_element_type=f32))
        for (a,b),(dkp,dvp) in parts.items():
            dk_acc[rows,a:b]+=dkp
            dv_acc[rows,a:b]+=dvp
        return tuple(out)
    dqs = lax.fori_loop(lo,hi,one,tuple(jnp.zeros((HD,BQ),f32) for _ in range(heads)))
    for h in range(heads):
        dq_ref[h*HD:(h+1)*HD,:]=dqs[h].astype(bf16)
        part = dqs[h][:,:128]
        for n in range(128,BQ,128): part=part+dqs[h][:,n:n+128]
        qb_ref[h*HD:(h+1)*HD,:]+=part
    @pl.when(i==pl.num_programs(0)-1)
    def _():
        if start_at:
            dk_ref[...]=(dk_acc[...]+dk_old[...]).astype(bf16)
            dv=dv_acc[...]+dv_old[...]
            dv_ref[...]=dv.astype(bf16)
            vb_ref[...]=jnp.sum(dv.reshape(dv.shape[0]//8,8,width),axis=0)
        else:
            dk_ref[...]=dk_acc[...]
            dv_ref[...]=dv_acc[...]

def attn_bwd(qT,k,kT,v,wT,grads,oT,lse,segc,segr,lo,hi,flip,sums=()):
    width,length=qT.shape
    heads=width//HD
    blocks=length//BQ//2
    first=blocks if sums else 0
    col=pl.BlockSpec((width,BQ),lambda i,*_:(0,first+i))
    row=pl.BlockSpec((length,width),lambda i,*_:(0,0))
    tall=jax.ShapeDtypeStruct((length,width),bf16 if sums else f32)
    eight=((jax.ShapeDtypeStruct((8,width),f32),),[pl.BlockSpec((8,width),lambda i,*_:(0,0))]) if sums else ((),[])
    return pl.pallas_call(
        functools.partial(bwd_kernel,first),
        out_shape=(jax.ShapeDtypeStruct((width,length//2),bf16), tall, tall, jax.ShapeDtypeStruct((width,128),f32))+eight[0],
        grid_spec=pltpu.PrefetchScalarGridSpec(num_scalar_prefetch=3, grid=(blocks,),
            in_specs=[col,row,pl.BlockSpec((width,length),lambda i,*_:(0,0)),row,pl.BlockSpec((width,wT.shape[1]),lambda i,*_:(wT.shape[1]//width-1,0))]+[pl.BlockSpec(g.shape,lambda i,*_:(0,0)) for g in grads]+[pl.BlockSpec((width,BQ),lambda i,*_:(0,i)),
                      pl.BlockSpec((8,BQ),lambda i,*_:(0,i)),
                      pl.BlockSpec((length,1),lambda i,*_:(0,0)),
                      pl.BlockSpec((1,BQ),lambda i,*_:(0,first+i))]+[row]*len(sums),
            out_specs=[pl.BlockSpec((width,BQ),lambda i,*_:(0,i)),row,row,pl.BlockSpec((width,128),lambda i,*_:(0,0))]+eight[1],
            scratch_shapes=[pltpu.VMEM((length,width),f32),pltpu.VMEM((length,width),f32),pltpu.VMEM((width,BQ),bf16)]),
        compiler_params=pltpu.CompilerParams(dimension_semantics=("arbitrary",),vmem_limit_bytes=60<<20),
        cost_estimate=pl.CostEstimate(flops=30*length*length*width,bytes_accessed=10*length*width,transcendentals=heads*length*length//4),
        name="attention_back",
    )(lo,hi,flip,qT,k,kT,v,wT,*grads,oT,lse,segc,segr,*sums)

def spans(seg_row):
    length=seg_row.shape[0]
    first=seg_row[::BQ]; last=seg_row[BQ-1::BQ]
    lo=jnp.sum(seg_row[None,:]<first[:,None],axis=1,dtype=jnp.int32)//BK
    hi=(jnp.sum(seg_row[None,:]<=last[:,None],axis=1,dtype=jnp.int32)+BK-1)//BK
    return lo,hi

EPSILON=1e-12
T=256
RC=128

def row_stats(values):
    centre=jnp.mean(values,axis=1,keepdims=True)
    centred=values-centre
    spread=jnp.mean(centred*centred,axis=1,keepdims=True)
    scale=lax.rsqrt(spread+EPSILON)
    return centred*scale, scale

def fold(values):
    return jnp.sum(values.reshape(values.shape[0]//8,8,values.shape[1]),axis=0)

def placements(count, model, blocks):
    if count != 8:
        return [[(r % 2, 0, r % 2, 0, None, model)] for r in range(blocks)]
    rows = model // 8
    every = []
    for r in range(blocks):
        core, beyond = r % 2, r // 2
        block = []
        for shard in range(8):
            odd, place = shard % 2, shard // 2
            if not beyond:
                source, first = odd, place
            elif not odd:
                source, first = 2, place
            else:
                source, first = (3, 0) if place == 0 else (4, place - 1)
            group = beyond and odd
            target = 0 if group else beyond * 2 + odd
            block.append((core * 5 + source, first * rows, core * 2 + group, (target * 4 + place) * rows, shard, rows))
        every.append(block)
    return every


def ffn_kernel(count, home_ref, tok_ref, a0_ref, a1_ref, a2_ref, cot_ref, vec_ref, be_ref, *refs):
    rows, width = tok_ref.shape
    blocks, units = be_ref.shape
    table = placements(count, width, blocks)
    n_in = 1 + max(item[0] for block in table for item in block)
    n_out = 1 + max(item[2] for block in table for item in block)
    pieces, refs = refs[:n_in], refs[n_in:]
    (out_ref, gm_ref, gml_ref, vg_ref, eb_ref), refs = refs[:5], refs[5:]
    grads, refs = refs[:n_out], refs[n_out:]
    we, ws, hl, hlT, hid, xhat, rs1, act, gp, acc, sl, slT, gsum, il, de, dt, wsem, osem = refs
    home = home_ref[0]
    def columns(ref, r, half):
        start = half * units + (r // 2 * 2 * units if len(table[0]) == 1 else 0)
        return ref.at[:, start : start + units]
    def spot(shard, size):
        return pl.ds(0 if shard is None else pl.multiple_of(jnp.bitwise_xor(home, shard) * size, size), size)
    def fetched(r, half):
        return [
            pltpu.make_async_copy(columns(pieces[p], r, half).at[first : first + size], (we, ws)[half].at[r, spot(shard, size)], wsem.at[half, r, k])
            for k, (p, first, _, _, shard, size) in enumerate(table[r])
        ]
    def sent(slot, r):
        return [
            pltpu.make_async_copy((de, dt)[half].at[slot, spot(shard, size)], columns(grads[g], r, half).at[first : first + size], osem.at[half, slot, k])
            for half in range(2)
            for k, (_, _, g, first, shard, size) in enumerate(table[r])
        ]
    for r in range(blocks):
        for half in range(2):
            for c in fetched(r, half):
                c.start()
    mb=vec_ref[0:1,:]; g1=vec_ref[1:2,:]; b1=vec_ref[2:3,:]; sb=vec_ref[3:4,:]; g2=vec_ref[4:5,:]; b2=vec_ref[5:6,:]
    def first(i,_):
        at=pl.ds(pl.multiple_of(i*RC,RC),RC)
        mixed=tok_ref[at,:].astype(f32)+(a0_ref[at,:].astype(f32)+a1_ref[at,:].astype(f32)+a2_ref[at,:].astype(f32))+mb
        z,scale=row_stats(mixed)
        xhat[at,:]=z
        rs1[at,:]=jnp.broadcast_to(scale,(RC,128))
        h=z*g1+b1
        hid[at,:]=h
        hl[at,:]=h.astype(bf16)
        acc[at,:]=jnp.zeros((RC,width),f32)
        return 0
    lax.fori_loop(0,rows//RC,first,0,unroll=2)
    def turn(src,dst):
        def go(i,_):
            at=pl.multiple_of(i*T,T)
            dst[:,pl.ds(at,T)]=jnp.transpose(src[pl.ds(at,T),:].astype(f32)).astype(bf16)
            return 0
        lax.fori_loop(0,rows//T,go,0)
    turn(hl,hlT)
    TG=768; TM=min(512,rows); per=units//T; mt=rows//TM
    def forward(r,_):
        for k in range(blocks):
            @pl.when(r==k)
            def _():
                for c in fetched(k, 0): c.wait()
        def tile(j,_):
            n=pl.multiple_of((j//mt)*T,T); m=pl.multiple_of((j%mt)*TM,TM)
            u=lax.dot_general(hl[pl.ds(m,TM),:],we[r,:,pl.ds(n,T)],NN,preferred_element_type=f32)+be_ref[pl.ds(r,1),pl.ds(n,T)]
            cdf=0.5+0.5*lax.erf(u*(0.5**0.5))
            act[r,pl.ds(m,TM),pl.ds(n,T)]=(u*cdf).astype(bf16)
            gp[r,pl.ds(m,TM),pl.ds(n,T)]=cdf+u*(jnp.exp(-0.5*u*u)*0.3989422804014327)
            return 0
        lax.fori_loop(0,per*mt,tile,0,unroll=3)
        for k in range(blocks):
            @pl.when(r==k)
            def _():
                for c in fetched(k, 1): c.wait()
        def shrink(j,_):
            n=pl.multiple_of((j//mt)*T,T); m=pl.multiple_of((j%mt)*TM,TM)
            acc[pl.ds(m,TM),pl.ds(n,T)]+=lax.dot_general(act[r,pl.ds(m,TM),:],ws[r,pl.ds(n,T),:],NT,preferred_element_type=f32)
            return 0
        lax.fori_loop(0,(width//T)*mt,shrink,0,unroll=3)
        return 0
    lax.fori_loop(0,blocks,forward,0)
    def second(i,sums):
        at=pl.ds(pl.multiple_of(i*RC,RC),RC)
        summed=hid[at,:]+acc[at,:]+sb
        z,scale=row_stats(summed)
        out_ref[at,:]=(z*g2+b2).astype(bf16)
        cot=cot_ref[at,:].astype(f32)
        e=cot*g2
        g=(e-jnp.mean(e,axis=1,keepdims=True)-z*jnp.mean(e*z,axis=1,keepdims=True))*scale
        gsum[at,:]=g
        sl[at,:]=g.astype(bf16)
        acc[at,:]=g
        return (sums[0]+fold(cot*z),sums[1]+fold(cot),sums[2]+fold(g))
    zero=jnp.zeros((8,width),f32)
    sg,sh,sbg=lax.fori_loop(0,rows//RC,second,(zero,zero,zero),unroll=2)
    turn(sl,slT)
    def backward(r,_):
        slot=r%2
        def tile(j,_):
            n=pl.multiple_of((j//mt)*T,T); m=pl.multiple_of((j%mt)*TM,TM)
            ga=lax.dot_general(sl[pl.ds(m,TM),:],ws[r,:,pl.ds(n,T)],NN,preferred_element_type=f32)
            gi=ga*gp[r,pl.ds(m,TM),pl.ds(n,T)]
            il[pl.ds(m,TM),pl.ds(n,T)]=gi.astype(bf16)
            part=fold(gi)
            eb_ref[r,:,pl.ds(n,T)]=jnp.where(m==0,part,eb_ref[r,:,pl.ds(n,T)]+part)
            return 0
        lax.fori_loop(0,per*mt,tile,0,unroll=3)
        def back(j,_):
            n=pl.multiple_of((j//mt)*T,T); m=pl.multiple_of((j%mt)*TM,TM)
            acc[pl.ds(m,TM),pl.ds(n,T)]+=lax.dot_general(il[pl.ds(m,TM),:],we[r,pl.ds(n,T),:],NT,preferred_element_type=f32)
            return 0
        lax.fori_loop(0,(width//T)*mt,back,0,unroll=3)
        for k in range(2,blocks):
            @pl.when(r==k)
            def _():
                for c in sent(k%2,k-2): c.wait()
        def grads(j,_):
            n=pl.multiple_of((j//(width//TG))*T,T); m=pl.multiple_of((j%(width//TG))*TG,TG)
            dt[slot,pl.ds(m,TG),pl.ds(n,T)]=lax.dot_general(slT[pl.ds(m,TG),:],act[r,:,pl.ds(n,T)],NN,preferred_element_type=f32).astype(bf16)
            de[slot,pl.ds(m,TG),pl.ds(n,T)]=lax.dot_general(hlT[pl.ds(m,TG),:],il[:,pl.ds(n,T)],NN,preferred_element_type=f32).astype(bf16)
            return 0
        lax.fori_loop(0,(width//TG)*per,grads,0,unroll=3)
        for k in range(blocks):
            @pl.when(r==k)
            def _():
                for c in sent(k%2,k): c.start()
        return 0
    lax.fori_loop(0,blocks,backward,0)
    def last(i,sums):
        at=pl.ds(pl.multiple_of(i*RC,RC),RC)
        g=acc[at,:]
        z=xhat[at,:]
        e=g*g1
        gm=(e-jnp.mean(e,axis=1,keepdims=True)-z*jnp.mean(e*z,axis=1,keepdims=True))*rs1[at,0:1]
        gm_ref[at,:]=gm
        gml_ref[at,:]=gm.astype(bf16)
        return (sums[0]+fold(g*z),sums[1]+fold(g),sums[2]+fold(gm))
    fg,fs,mbg=lax.fori_loop(0,rows//RC,last,(zero,zero,zero),unroll=2)
    for n,v in enumerate((mbg,fg,fs,sbg,sg,sh)):
        vg_ref[n]=v
    for k in range(max(0,blocks-2),blocks):
        for c in sent(k%2,k): c.wait()

def ffn(home, count, tok, a0, a1, a2, cot, vec, be, pieces):
    rows, width = tok.shape
    blocks, units = be.shape
    table = placements(count, width, blocks)
    n_out = 1 + max(item[2] for block in table for item in block)
    each = len(table[0])
    sizes = [(width * 3 // 2, 2 * units), (width // 2, 2 * units)] * 2 if each > 1 else [(width, blocks * units)] * 2
    grads = tuple(jax.ShapeDtypeStruct(size, bf16) for size in sizes)
    v = pl.BlockSpec(memory_space=pltpu.VMEM)
    h = pl.BlockSpec(memory_space=pltpu.HBM)
    V = pltpu.VMEM
    return pl.pallas_call(
        functools.partial(ffn_kernel, count),
        out_shape=(jax.ShapeDtypeStruct((rows, width), bf16), jax.ShapeDtypeStruct((rows, width), f32), jax.ShapeDtypeStruct((rows, width), bf16),
            jax.ShapeDtypeStruct((6, 8, width), f32), jax.ShapeDtypeStruct((blocks, 8, units), f32)) + grads,
        in_specs=[pl.BlockSpec(memory_space=pltpu.SMEM)] + [v] * 7 + [h] * len(pieces),
        out_specs=[v] * 5 + [h] * n_out,
        scratch_shapes=[V((blocks, width, units), bf16), V((blocks, width, units), bf16),
            V((rows, width), bf16), V((width, rows), bf16), V((rows, width), f32), V((rows, width), f32), V((rows, 128), f32),
            V((blocks, rows, units), bf16), V((blocks, rows, units), f32), V((rows, width), f32), V((rows, width), bf16), V((width, rows), bf16), V((rows, width), f32),
            V((rows, units), bf16), V((2, width, units), bf16), V((2, width, units), bf16),
            pltpu.SemaphoreType.DMA((2, blocks, each)), pltpu.SemaphoreType.DMA((2, 2, each))],
        compiler_params=pltpu.CompilerParams(vmem_limit_bytes=60 << 20),
        cost_estimate=pl.CostEstimate(flops=30 * rows * width * units * blocks, bytes_accessed=8 * blocks * width * units, transcendentals=2 * rows * units * blocks),
        name="feed_forward",
    )(home, tok, a0, a1, a2, cot, vec, be, *pieces)


def proj_kernel(home_ref, x0, x1, x2, x3, wa_ref, wb_ref, bq_ref, bvc_ref, bvr_ref,
                q_ref, kT_ref, vT_ref, k_ref, v_ref, wT, w_ref, wk, wv, x_buf, sem, x_sem):
    model = w_ref.shape[0]
    count, rows = sem.shape[0], model // sem.shape[0]
    width = q_ref.shape[0]
    home = home_ref[0]
    step = pl.program_id(0)
    def copy(r):
        src = (wa_ref, wb_ref)[r % 2].at[(r // 2) * rows : (r // 2 + 1) * rows]
        at = pl.multiple_of(jnp.bitwise_xor(home, r) * rows, rows)
        return pltpu.make_async_copy(src, w_ref.at[pl.ds(at, rows)], sem.at[r])
    if wa_ref.shape[0] == model:
        count = 1
        copy = lambda r: pltpu.make_async_copy(wa_ref, w_ref, sem.at[r])
    fetch = [pltpu.make_async_copy(x, x_buf.at[n], x_sem.at[n]) for n, x in enumerate((x0, x1, x2, x3))]
    @pl.when(step == 0)
    def _():
        for r in range(count):
            copy(r).start()
        for x in fetch:
            x.start()
        for r in range(count):
            copy(r).wait()
        def turn(i, _):
            at = pl.multiple_of(i * 256, 256)
            wT[:, pl.ds(at, 256)] = jnp.transpose(w_ref[pl.ds(at, 256), :].astype(f32)).astype(bf16)
            return 0
        lax.fori_loop(0, model // 256, turn, 0)
        wk[...] = w_ref[:, width : 2 * width]
        wv[...] = w_ref[:, 2 * width : 3 * width]
    for n, x in enumerate(fetch):
        @pl.when(step == n)
        def _():
            x.wait()
    x = x_buf[step]
    k_ref[...] = jnp.dot(x, wk[...], preferred_element_type=f32).astype(bf16)
    v_ref[...] = (jnp.dot(x, wv[...], preferred_element_type=f32) + bvr_ref[...]).astype(bf16)
    q_ref[...] = (lax.dot_general(wT[0:width], x, NT, preferred_element_type=f32) + bq_ref[...]).astype(bf16)
    kT_ref[...] = lax.dot_general(wT[width : 2 * width], x, NT, preferred_element_type=f32).astype(bf16)
    vT_ref[...] = (lax.dot_general(wT[2 * width : 3 * width], x, NT, preferred_element_type=f32) + bvc_ref[...]).astype(bf16)


def project(home, tokens, wa, wb, count, bq, bv):
    size, model = tokens[0].shape
    length = 4 * size
    width = bq.shape[0]
    hbm = pl.BlockSpec(memory_space=pltpu.HBM)
    column = pl.BlockSpec((width, 1), lambda i: (0, 0))
    tall = jax.ShapeDtypeStruct((length, width), bf16)
    flat = jax.ShapeDtypeStruct((width, length), bf16)
    across = pl.BlockSpec((width, size), lambda i: (0, i))
    down = pl.BlockSpec((size, width), lambda i: (i, 0))
    return pl.pallas_call(
        proj_kernel,
        grid=(4,),
        out_shape=(flat, flat, flat, tall, tall, jax.ShapeDtypeStruct((model, model), bf16)),
        in_specs=[pl.BlockSpec(memory_space=pltpu.SMEM)] + [hbm] * 6 + [column, column, pl.BlockSpec((1, width), lambda i: (0, 0))],
        out_specs=[across, across, across, down, down, pl.BlockSpec((model, model), lambda i: (0, 0))],
        scratch_shapes=[pltpu.VMEM((model, model), bf16), pltpu.VMEM((model, width), bf16), pltpu.VMEM((model, width), bf16),
            pltpu.VMEM((4, size, model), bf16), pltpu.SemaphoreType.DMA((count,)), pltpu.SemaphoreType.DMA((4,))],
        compiler_params=pltpu.CompilerParams(dimension_semantics=("arbitrary",), vmem_limit_bytes=60 << 20),
        cost_estimate=pl.CostEstimate(flops=30 * length * model * width, bytes_accessed=4 * length * model, transcendentals=0),
        name="projection",
    )(home, *tokens, wa, wb, bq[:, None], bv[:, None], bv[None, :])


def grads_kernel(home_ref, x0, x1, x2, x3, g0, g1, g2, g3, ca_ref, cb_ref, qa_ref, qb_ref, k_ref, v_ref, *rest):
    *outs, acc, x_buf, g_buf, xT, gT, sem = rest
    home = home_ref[0]
    step = pl.program_id(0)
    size, model = xT.shape[1], xT.shape[0]
    width = k_ref.shape[1]
    fetch = [
        (pltpu.make_async_copy(x, x_buf.at[n], sem.at[0, n]), pltpu.make_async_copy(g, g_buf.at[n], sem.at[1, n]))
        for n, (x, g) in enumerate(zip((x0, x1, x2, x3), (g0, g1, g2, g3)))
    ]
    @pl.when(step == 0)
    def _():
        for x, g in fetch:
            x.start()
            g.start()
    for n, (x, g) in enumerate(fetch):
        @pl.when(step == n)
        def _():
            x.wait()
            g.wait()
    for i in range(0, size, 256):
        xT[:, i : i + 256] = jnp.transpose(x_buf[step, i : i + 256, :].astype(f32)).astype(bf16)
        gT[:, i : i + 256] = jnp.transpose(g_buf[step, i : i + 256, :].astype(f32)).astype(bf16)
    q = jnp.where(step < 2, qa_ref[...], qb_ref[...])
    c = jnp.where(step < 2, ca_ref[...], cb_ref[...])
    pieces = (
        lax.dot_general(xT[...], q, NT, preferred_element_type=f32),
        jnp.dot(xT[...], k_ref[...], preferred_element_type=f32),
        jnp.dot(xT[...], v_ref[...], preferred_element_type=f32),
        lax.dot_general(gT[...], c, NT, preferred_element_type=f32),
    )
    @pl.when(step == 0)
    def _():
        for m, piece in enumerate(pieces):
            acc[m] = piece
    @pl.when(step > 0)
    def _():
        for m, piece in enumerate(pieces):
            acc[m] += piece
    @pl.when(step == 3)
    def _():
        if len(outs) == 1:
            for m in range(4):
                outs[0][:, m * width : (m + 1) * width] = acc[m].astype(bf16)
            return
        rows = model // 8
        for r in range(8):
            at = pl.ds(pl.multiple_of(jnp.bitwise_xor(home, r) * rows, rows), rows)
            to = slice(r // 2 * rows, (r // 2 + 1) * rows)
            for m in range(4):
                outs[r % 2][to, m * width : (m + 1) * width] = acc[m, at, :].astype(bf16)


def halves(width, size):
    return [pl.BlockSpec((width, size), lambda i: (0, jnp.minimum(i, 1))), pl.BlockSpec((width, size), lambda i: (0, jnp.maximum(i, 2) - 2))]


def attn_grads(home, count, tokens, grads, contextT, dqT, dk, dv):
    size, model = tokens[0].shape
    width = dk.shape[1]
    hbm = pl.BlockSpec(memory_space=pltpu.HBM)
    down = pl.BlockSpec((size, width), lambda i: (i, 0))
    parts = 2 if count == 8 else 1
    V = pltpu.VMEM
    return pl.pallas_call(
        grads_kernel,
        grid=(4,),
        out_shape=[jax.ShapeDtypeStruct((model // parts, 4 * width), bf16)] * parts,
        in_specs=[pl.BlockSpec(memory_space=pltpu.SMEM)] + [hbm] * 8 + halves(width, size) * 2 + [down, down],
        out_specs=[pl.BlockSpec((model // parts, 4 * width), lambda i: (0, 0))] * parts,
        scratch_shapes=[V((4, model, width), f32), V((4, size, model), bf16), V((4, size, model), bf16), V((model, size), bf16), V((model, size), bf16),
            pltpu.SemaphoreType.DMA((2, 4))],
        compiler_params=pltpu.CompilerParams(dimension_semantics=("arbitrary",), vmem_limit_bytes=60 << 20),
        cost_estimate=pl.CostEstimate(flops=40 * size * model * width, bytes_accessed=24 * size * model, transcendentals=0),
        name="projection_grads",
    )(home, *tokens, *grads, *contextT, *dqT, dk, dv)


def back_kernel(qa_ref, qb_ref, k_ref, v_ref, wq_ref, wk_ref, wv_ref, near_ref, side_ref, far_ref):
    i = pl.program_id(0)
    size = near_ref.shape[0]
    def block(q_ref):
        q = jnp.transpose(q_ref[...].astype(f32)).astype(bf16)
        total = jnp.dot(q, wq_ref[...], preferred_element_type=f32)
        total = total + jnp.dot(k_ref[...], wk_ref[...], preferred_element_type=f32)
        return (total + jnp.dot(v_ref[...], wv_ref[...], preferred_element_type=f32)).astype(bf16)
    for n, ref in enumerate((near_ref, side_ref, far_ref, side_ref)):
        @pl.when(i == n)
        def _():
            ref[size if n == 3 else 0 : 2 * size if n == 3 else size, :] = block((qa_ref, qb_ref)[n // 2])


def project_back(dqT, dk, dv, wT):
    length, width = dk.shape
    size, model = length // 4, wT.shape[1]
    down = pl.BlockSpec((size, width), lambda i: (i, 0))
    weight = [pl.BlockSpec((width, model), functools.partial(lambda n, i: (n, 0), n)) for n in range(3)]
    return pl.pallas_call(
        back_kernel,
        grid=(4,),
        out_shape=[jax.ShapeDtypeStruct((n * size, model), bf16) for n in (1, 2, 1)],
        in_specs=halves(width, size) + [down, down] + weight,
        out_specs=[pl.BlockSpec((n * size, model), lambda i: (0, 0)) for n in (1, 2, 1)],
        compiler_params=pltpu.CompilerParams(dimension_semantics=("arbitrary",), vmem_limit_bytes=60 << 20),
        cost_estimate=pl.CostEstimate(flops=70 * length * model * width, bytes_accessed=8 * length * model, transcendentals=0),
        name="projection_back",
    )(*dqT, dk, dv, wT, wT, wT)


def hop(value, bit):
    count = lax.axis_size("dp")
    return lax.ppermute(value, "dp", [(i, i ^ bit) for i in range(count)])


def gather_shards(own):
    count = lax.axis_size("dp")
    if count != 8:
        every = lax.all_gather(own, "dp", axis=0, tiled=True)
        return every, every
    even = jnp.concatenate([own] + [hop(own, bit) for bit in (2, 4, 6)], axis=0)
    return even, hop(even, 1)


def later(value, *markers, flops=0):
    anywhere = pl.BlockSpec(memory_space=pl.ANY)
    return pl.pallas_call(
        lambda *refs: None,
        out_shape=jax.ShapeDtypeStruct(value.shape, value.dtype),
        in_specs=[anywhere] * (1 + len(markers)),
        out_specs=anywhere,
        input_output_aliases={0: 0},
        cost_estimate=pl.CostEstimate(flops=flops, bytes_accessed=0, transcendentals=0),
        name="later",
    )(value, *markers)


def exchange(value, bit):
    return lax.ppermute(value, "tensor", [(i, i ^ bit) for i in range(4)])


def row_blocks(own):
    across = exchange(own, 2)
    return [own, exchange(own, 1), across, exchange(across, 1)]


def gather_rows(own):
    return jnp.concatenate(row_blocks(own), axis=0)


def scatter_pieces(near, side, far):
    rows = near.shape[0]
    beside = exchange(side, 1)
    ahead = (far.astype(f32) + beside[rows:].astype(f32)).astype(bf16)
    return (near, beside[:rows], exchange(ahead, 2)), ahead


def gather_blocks(own):
    if lax.axis_size("dp") != 8:
        return [lax.all_gather(jnp.concatenate([own, exchange(own, 2)], axis=1), "dp", axis=0, tiled=True)]
    even = jnp.concatenate([own] + [hop(own, bit) for bit in (2, 4, 6)], axis=0)
    return [even, hop(even, 1), exchange(even, 2)]


def last_blocks(pieces, *markers):
    if len(pieces) == 1:
        return []
    _, odd, beyond = pieces
    cut = odd.shape[0] // 4
    return [later(exchange(odd[:cut], 2), *markers), later(hop(beyond[cut:], 1), *markers)]


def total(*terms):
    result = terms[0].astype(f32)
    for term in terms[1:]:
        result = result + term.astype(f32)
    return result


def fold_both(own, got):
    cut = own.shape[0] // 4
    return total(own[:cut], got[:cut]).astype(bf16), total(own[cut:], got[cut:]).astype(bf16)


def fold_rest(own, got, across, along):
    rows = own.shape[0] // 3
    cut = rows // 4
    part = lambda n: total(own[n * rows : (n + 1) * rows], got[n * rows : (n + 1) * rows])
    odd, beyond = part(1), part(2)
    odd = jnp.concatenate([odd[:cut] + across.astype(f32), odd[cut:]], axis=0).astype(bf16)
    beyond = jnp.concatenate([beyond[:cut], beyond[cut:] + along.astype(f32)], axis=0).astype(bf16)
    return odd, beyond


def fold_even(own, got, odd, beyond):
    rows = own.shape[0] // 3
    return total(own[:rows], got[:rows], odd, beyond).astype(bf16).reshape(4, rows // 4, -1)


def on_device(
    tokens,
    segments,
    query_proj,
    query_bias,
    key_proj,
    value_proj,
    value_bias,
    merge_proj,
    merge_bias,
    first_gain,
    first_shift,
    expand_proj,
    expand_bias,
    shrink_proj,
    shrink_bias,
    second_gain,
    second_shift,
    cotangent,
):
    everyone = ("dp", "tensor")
    part = lax.axis_index("tensor")
    dp = lax.axis_size("dp")
    world = dp * 4
    width = query_proj.shape[1]
    units = expand_proj.shape[1]
    model = width * 4
    share = model // world
    unit_share = units * 4 // world

    shard = jnp.concatenate([query_proj, key_proj, value_proj, merge_proj.T], axis=1)
    shards = gather_shards(shard)
    wide = jnp.concatenate([expand_proj, shrink_proj.T], axis=1)
    pieces = gather_blocks(wide)
    own = jnp.concatenate(
        [query_bias, value_bias, merge_bias, first_gain, first_shift, shrink_bias, second_gain, second_shift, expand_bias]
    )
    rows = tokens.shape[0]
    count = own.shape[0]
    own = jnp.concatenate([own, segments.reshape(-1).astype(f32)])
    slots = -(-own.shape[0] // 1024) * 8
    own = jnp.pad(own, (0, slots * 128 - own.shape[0])).reshape(1, slots, 128)
    vectors = lax.all_to_all(jnp.broadcast_to(own, (world, slots, 128)), everyone, 0, 0, tiled=True)
    vectors = vectors.reshape(world, slots * 128)
    whole = vectors[:, : 8 * share].reshape(world, 8, share).transpose(1, 0, 2).reshape(8, model)
    unit_bias = vectors[:, 8 * share : 8 * share + unit_share].reshape(4, units)
    flips = jnp.bitwise_xor(jnp.arange(4), part)
    seg = lax.dynamic_slice(vectors, (lax.axis_index("dp") * 4, count), (4, rows))
    seg = jnp.take(seg, flips, axis=0).reshape(-1).astype(jnp.int32)
    unit_bias = jnp.take(unit_bias, flips, axis=0)
    query_b = lax.dynamic_slice_in_dim(whole[0], part * width, width)
    value_b = lax.dynamic_slice_in_dim(whole[1], part * width, width)
    rows_b = whole[2:8]

    blocks = row_blocks(tokens)
    segc, segr = seg[:, None], seg[None, :]
    lo, hi = spans(seg)
    flip = (part * (tokens.shape[0] // BK)).astype(jnp.int32).reshape(1)
    home = lax.axis_index("dp").astype(jnp.int32).reshape(1)
    query_t, key_t, value_t, keys, values, attn_wt = project(home, blocks, *shards, dp, query_b, value_b)
    ahead = functools.partial(attn_fwd, 1, query_t, keys, value_t, attn_wt, segc, segr)
    behind = functools.partial(attn_fwd, 0, query_t, keys, value_t, attn_wt, segc, segr)
    context_b, logsum_b, far, side = ahead(later(lo, pieces[0]), hi, flip)
    beside = exchange(side, 1)
    far = (far.astype(f32) + beside.astype(f32)).astype(bf16)
    swapped = [exchange(pieces[0], 1)]
    context_a, logsum_a, a0, side = behind(later(lo, far, swapped[0], *pieces[1:]), hi, flip)
    a1 = exchange(side, 1)
    a2 = later(exchange(far, 2), context_a)

    swapped = swapped + [later(exchange(piece, 1), context_a) for piece in pieces[1:]]
    last = last_blocks(pieces, context_a, a2)
    pieces = pieces + last + swapped + [exchange(piece, 1) for piece in last]
    out = ffn(home, dp, tokens, a0, a1, a2, cotangent, rows_b, unit_bias, pieces)
    output, grad_mixed, mixed_low, row_sums, unit_sums = out[:5]
    beside = exchange(mixed_low, 1)
    across = exchange(mixed_low, 2)
    grads = out[5:]
    local = len(grads) // 2
    swapped = [exchange(grad, 1) for grad in grads[local:]]
    back = functools.partial(attn_bwd, query_t, keys, key_t, values, attn_wt)
    waits = []
    if local == 2:
        waits = fold_both(grads[1], swapped[1])
    dq_a, dk_a, dv_a, q_sums_a = back((mixed_low, beside), context_a, logsum_a, segc, segr, later(lo, *waits), hi, flip)
    across = later(across, q_sums_a)
    mixed_blocks = [mixed_low, beside, across, exchange(across, 1)]
    if local == 2:
        waits = fold_rest(grads[0], swapped[0], later(exchange(waits[0], 2), q_sums_a), later(hop(waits[1], 1), q_sums_a))
    dq_b, dk, dv, q_sums_b, v_sums = back(
        mixed_blocks[2:], context_b, logsum_b, segc, segr, later(lo, *waits), hi, flip, sums=(dk_a, dv_a)
    )
    attn_local = attn_grads(home, dp, blocks, mixed_blocks, (context_a, context_b), (dq_a, dq_b), dk, dv)
    if local == 2:
        waits = [fold_even(grads[0], swapped[0], later(hop(waits[0], 1), attn_local[0]), later(exchange(waits[1], 2), attn_local[0]))]
    even = waits[0] if local == 2 else attn_local[0]
    b0, side, far = project_back((later(dq_a, even), dq_b), dk, dv, attn_wt)

    q_sums = later(q_sums_a, even) + later(q_sums_b, even)
    v_sums = later(v_sums, even)
    mine = (jnp.arange(4) == part).astype(f32)[:, None]
    q_all = (mine * jnp.sum(q_sums, axis=1)[None]).reshape(1, model)
    v_all = (mine * jnp.sum(v_sums, axis=0)[None]).reshape(1, model)
    early = jnp.sum(row_sums, axis=1).reshape(6, world, share).transpose(1, 0, 2).reshape(world, 6 * share)
    late = jnp.concatenate([q_all, v_all], axis=0).reshape(2, world, share).transpose(1, 0, 2).reshape(world, 2 * share)
    u_all = jnp.take(jnp.sum(unit_sums, axis=1), flips, axis=0).reshape(world, unit_share)
    send = jnp.concatenate([late, early, u_all], axis=1)
    send = jnp.pad(send, ((0, 0), (0, slots * 128 - send.shape[1]))).reshape(world, slots, 128)
    got = jnp.sum(lax.all_to_all(send, everyone, 0, 0, tiled=True).reshape(world, slots * 128), axis=0)
    small = [got[n * share : (n + 1) * share] for n in range(8)]

    if local == 2:
        y_came = hop(attn_local[1], 1)
        wide_grad = even[0].astype(f32) + sum(later(hop(even[n], 2 * n), b0, got, y_came).astype(f32) for n in (1, 2, 3))
        rows = attn_local[0].shape[0] // 4
        even = total(attn_local[0], y_came).astype(bf16).reshape(4, rows, -1)
        attn_grad = even[0].astype(f32) + sum(hop(even[n], 2 * n).astype(f32) for n in (1, 2, 3))
    else:
        mine = lax.psum_scatter(total(grads[0], swapped[0]).astype(bf16), "dp", scatter_dimension=0, tiled=True)
        wide_grad = total(mine[:, : 2 * units], exchange(mine[:, 2 * units :], 2))
        attn_grad = lax.all_to_all(attn_local[0], "dp", 0, 0, tiled=True)
        attn_grad = jnp.sum(attn_grad.reshape(dp, -1, model).astype(f32), axis=0)
    (b0, b1, b2), _ = scatter_pieces(b0, later(side, got), far)
    tokens_grad = (grad_mixed + (b0.astype(f32) + b1.astype(f32) + b2.astype(f32))).astype(bf16)
    querygrad, keygrad, valuegrad, mergegrad = (attn_grad[:, n * width : (n + 1) * width] for n in range(4))
    expandgrad = wide_grad[:, :units]
    shrinkgrad = wide_grad[:, units:].T

    qbiasgrad, vbiasgrad, mbiasgrad, fgaingrad, fshiftgrad, sbiasgrad, sgaingrad, sshiftgrad = small
    ebiasgrad = got[8 * share : 8 * share + unit_share]
    return (
        output,
        tokens_grad,
        querygrad,
        qbiasgrad,
        keygrad,
        valuegrad,
        vbiasgrad,
        mergegrad.T,
        mbiasgrad,
        fgaingrad,
        fshiftgrad,
        expandgrad,
        ebiasgrad,
        shrinkgrad,
        sbiasgrad,
        sgaingrad,
        sshiftgrad,
    )


def solution(mesh):
    return jax.shard_map(
        on_device,
        mesh=mesh,
        in_specs=(
            P(("dp", "tensor"), None),
            P("dp", "tensor"),
            P("dp", "tensor"),
            P(("dp", "tensor")),
            P("dp", "tensor"),
            P("dp", "tensor"),
            P(("dp", "tensor")),
            P("tensor", "dp"),
            P(("dp", "tensor")),
            P(("dp", "tensor")),
            P(("dp", "tensor")),
            P("dp", "tensor"),
            P(("dp", "tensor")),
            P("tensor", "dp"),
            P(("dp", "tensor")),
            P(("dp", "tensor")),
            P(("dp", "tensor")),
            P(("dp", "tensor"), None),
        ),
        out_specs=(
            P(("dp", "tensor"), None),
            P(("dp", "tensor"), None),
            P("dp", "tensor"),
            P(("dp", "tensor")),
            P("dp", "tensor"),
            P("dp", "tensor"),
            P(("dp", "tensor")),
            P("tensor", "dp"),
            P(("dp", "tensor")),
            P(("dp", "tensor")),
            P(("dp", "tensor")),
            P("dp", "tensor"),
            P(("dp", "tensor")),
            P("tensor", "dp"),
            P(("dp", "tensor")),
            P(("dp", "tensor")),
            P(("dp", "tensor")),
        ),
        check_vma=False,
    )
```

```python
import functools

import jax
import jax.numpy as jnp
from jax import lax
from jax.sharding import PartitionSpec as P
from jax.experimental import pallas as pl
from jax.experimental.pallas import tpu as pltpu

HD=64
BQ=512
BK=512
LOG2E=1.4426950408889634
NN=(((1,),(0,)),((),()))
NT=(((1,),(1,)),((),()))
TN=(((0,),(0,)),((),()))
f32=jnp.float32; bf16=jnp.bfloat16

def head_cols(h, heads):
    start=(h//2)*128
    stop=min(start+128, heads*HD)
    return start, stop

def padded(ref, h, heads, rows):
    start, stop = head_cols(h, heads)
    piece = ref[h*HD:(h+1)*HD, rows]
    if stop-start == HD: return piece
    zero = jnp.zeros_like(piece)
    return jnp.concatenate([piece, zero] if h%2==0 else [zero, piece], axis=0)

def fwd_kernel(start_at, lo_ref, hi_ref, flip_ref, q_ref, k_ref, v_ref, w_ref, segc_ref, segr_ref, o_ref, lse_ref, first_ref, second_ref, s_ref):
    heads = q_ref.shape[0]//HD
    i = pl.program_id(0)
    lo = lo_ref[start_at+i]; hi = hi_ref[start_at+i]; flip = flip_ref[0]
    c = LOG2E * HD**-0.5
    qz = [padded(q_ref, h, heads, slice(None)) for h in range(heads)]
    segq = segr_ref[...]
    def one(kb, peaks):
        start = pl.multiple_of(jnp.bitwise_xor(kb, flip)*BK, BK)
        same = segc_ref[pl.ds(start,BK),:] == segq
        new=[]
        for h in range(heads):
            a,b = head_cols(h, heads)
            s = lax.dot_general(k_ref[pl.ds(start,BK), a:b], qz[h], NN, preferred_element_type=f32)
            s = jnp.where(same, s, -1e30)
            s_ref[h, kb-lo] = s
            new.append(jnp.maximum(peaks[h], jnp.max(s.reshape(BK//8,8,BQ),axis=0)))
        return tuple(new)
    peaks = lax.fori_loop(lo, hi, one, tuple(jnp.full((8,BQ),-1e30,f32) for _ in range(heads)))
    peaks = [jnp.max(p,axis=0,keepdims=True)*c for p in peaks]
    def two(kb, carry):
        sums, outs = carry
        start = pl.multiple_of(jnp.bitwise_xor(kb, flip)*BK, BK)
        ns=[];no=[]
        for h in range(heads):
            p = jnp.exp2(s_ref[h, kb-lo]*c - peaks[h])
            ns.append(sums[h]+jnp.sum(p.reshape(BK//8,8,BQ),axis=0))
            no.append(outs[h]+lax.dot_general(v_ref[h*HD:(h+1)*HD, pl.ds(start,BK)], p.astype(bf16), NN, preferred_element_type=f32))
        return tuple(ns),tuple(no)
    sums, outs = lax.fori_loop(lo, hi, two, (tuple(jnp.zeros((8,BQ),f32) for _ in range(heads)), tuple(jnp.zeros((HD,BQ),f32) for _ in range(heads))))
    for h in range(heads):
        total = jnp.sum(sums[h],axis=0,keepdims=True)
        o_ref[h*HD:(h+1)*HD,:] = (outs[h]/total).astype(bf16)
        lse_ref[h:h+1,:] = peaks[h]+jnp.log2(total)
    context = jnp.transpose(o_ref[...].astype(f32)).astype(bf16)
    merged = jnp.dot(context, w_ref[...], preferred_element_type=f32).astype(bf16)
    per = first_ref.shape[0]//BQ
    for n, ref in enumerate((first_ref, second_ref)):
        @pl.when(i//per==n)
        def _():
            ref[pl.ds(pl.multiple_of((i%per)*BQ, BQ), BQ),:] = merged

def attn_fwd(second,qT,k,vT,wT,segc,segr,lo,hi,flip):
    width,length=qT.shape
    size,model=length//4,wT.shape[1]
    heads=width//HD
    blocks=length//BQ//2
    first=blocks*second
    col=pl.BlockSpec((width,BQ),lambda i,*_:(0,first+i))
    whole=pl.BlockSpec((size,model),lambda i,*_:(0,0))
    part=jax.ShapeDtypeStruct((size,model),bf16)
    return pl.pallas_call(
        functools.partial(fwd_kernel,first),
        out_shape=(jax.ShapeDtypeStruct((width,length//2),bf16), jax.ShapeDtypeStruct((8,length//2),f32), part, part),
        grid_spec=pltpu.PrefetchScalarGridSpec(num_scalar_prefetch=3, grid=(blocks,),
            in_specs=[col,
                      pl.BlockSpec((length,width),lambda i,*_:(0,0)),
                      pl.BlockSpec((width,length),lambda i,*_:(0,0)),
                      pl.BlockSpec((width,model),lambda i,*_:(model//width-1,0)),
                      pl.BlockSpec((length,1),lambda i,*_:(0,0)),
                      pl.BlockSpec((1,BQ),lambda i,*_:(0,first+i))],
            out_specs=[pl.BlockSpec((width,BQ),lambda i,*_:(0,i)),pl.BlockSpec((8,BQ),lambda i,*_:(0,i)),whole,whole],
            scratch_shapes=[pltpu.VMEM((heads,length//BK,BK,BQ),f32)]),
        compiler_params=pltpu.CompilerParams(dimension_semantics=("arbitrary",),vmem_limit_bytes=60<<20),
        cost_estimate=pl.CostEstimate(flops=25*length*length*width,bytes_accessed=4*length*width,transcendentals=heads*length*length//4),
        name="attention",
    )(lo,hi,flip,qT,k,vT,wT,segc,segr)

def bwd_kernel(start_at, lo_ref, hi_ref, flip_ref, q_ref, k_ref, kT_ref, v_ref, wT_ref, g0, g1, o_ref, lse_ref, segc_ref, segr_ref, *rest):
    if start_at:
        dk_old, dv_old, dq_ref, dk_ref, dv_ref, qb_ref, vb_ref, dk_acc, dv_acc, do_ref = rest
    else:
        dq_ref, dk_ref, dv_ref, qb_ref, dk_acc, dv_acc, do_ref = rest
    heads = q_ref.shape[0]//HD
    width = q_ref.shape[0]
    i = pl.program_id(0)
    @pl.when(i==0)
    def _():
        dk_acc[...]=jnp.zeros_like(dk_acc); dv_acc[...]=jnp.zeros_like(dv_acc)
        qb_ref[...]=jnp.zeros_like(qb_ref)
    lo = lo_ref[start_at+i]; hi = hi_ref[start_at+i]; flip = flip_ref[0]
    scale = HD**-0.5
    per = g0.shape[0]//BQ
    for n, g_ref in enumerate((g0, g1)):
        @pl.when(i//per==n)
        def _():
            at = pl.multiple_of((i%per)*BQ, BQ)
            do_ref[...] = lax.dot_general(wT_ref[...], g_ref[pl.ds(at,BQ),:], NT, preferred_element_type=f32).astype(bf16)
    c = LOG2E*scale
    qz = [padded(q_ref, h, heads, slice(None)) for h in range(heads)]
    dz = [padded(do_ref, h, heads, slice(None)) for h in range(heads)]
    deltas = [jnp.sum(do_ref[h*HD:(h+1)*HD,:].astype(f32)*o_ref[h*HD:(h+1)*HD,:].astype(f32),axis=0,keepdims=True) for h in range(heads)]
    segq = segr_ref[...]
    def one(kb, dqs):
        start = pl.multiple_of(jnp.bitwise_xor(kb, flip)*BK, BK)
        rows = pl.ds(start,BK)
        same = segc_ref[rows,:] == segq
        out=[]
        parts={}
        for h in range(heads):
            a,b = head_cols(h, heads)
            s = lax.dot_general(k_ref[rows, a:b], qz[h], NN, preferred_element_type=f32)
            p = jnp.exp2(jnp.where(same, s*c - lse_ref[h:h+1,:], -1e30))
            dp = lax.dot_general(v_ref[rows, a:b], dz[h], NN, preferred_element_type=f32)
            ds = (p*((dp-deltas[h])*scale)).astype(bf16)
            dvp = lax.dot_general(p.astype(bf16), dz[h], NT, preferred_element_type=f32)
            dkp = lax.dot_general(ds, qz[h], NT, preferred_element_type=f32)
            if (a,b) in parts: parts[a,b]=(parts[a,b][0]+dkp,parts[a,b][1]+dvp)
            else: parts[a,b]=(dkp,dvp)
            out.append(dqs[h]+lax.dot_general(kT_ref[h*HD:(h+1)*HD, rows], ds, NN, preferred_element_type=f32))
        for (a,b),(dkp,dvp) in parts.items():
            dk_acc[rows,a:b]+=dkp
            dv_acc[rows,a:b]+=dvp
        return tuple(out)
    dqs = lax.fori_loop(lo,hi,one,tuple(jnp.zeros((HD,BQ),f32) for _ in range(heads)))
    for h in range(heads):
        dq_ref[h*HD:(h+1)*HD,:]=dqs[h].astype(bf16)
        part = dqs[h][:,:128]
        for n in range(128,BQ,128): part=part+dqs[h][:,n:n+128]
        qb_ref[h*HD:(h+1)*HD,:]+=part
    @pl.when(i==pl.num_programs(0)-1)
    def _():
        if start_at:
            dk_ref[...]=(dk_acc[...]+dk_old[...]).astype(bf16)
            dv=dv_acc[...]+dv_old[...]
            dv_ref[...]=dv.astype(bf16)
            vb_ref[...]=jnp.sum(dv.reshape(dv.shape[0]//8,8,width),axis=0)
        else:
            dk_ref[...]=dk_acc[...]
            dv_ref[...]=dv_acc[...]

def attn_bwd(qT,k,kT,v,wT,grads,oT,lse,segc,segr,lo,hi,flip,sums=()):
    width,length=qT.shape
    heads=width//HD
    blocks=length//BQ//2
    first=blocks if sums else 0
    col=pl.BlockSpec((width,BQ),lambda i,*_:(0,first+i))
    row=pl.BlockSpec((length,width),lambda i,*_:(0,0))
    tall=jax.ShapeDtypeStruct((length,width),bf16 if sums else f32)
    eight=((jax.ShapeDtypeStruct((8,width),f32),),[pl.BlockSpec((8,width),lambda i,*_:(0,0))]) if sums else ((),[])
    return pl.pallas_call(
        functools.partial(bwd_kernel,first),
        out_shape=(jax.ShapeDtypeStruct((width,length//2),bf16), tall, tall, jax.ShapeDtypeStruct((width,128),f32))+eight[0],
        grid_spec=pltpu.PrefetchScalarGridSpec(num_scalar_prefetch=3, grid=(blocks,),
            in_specs=[col,row,pl.BlockSpec((width,length),lambda i,*_:(0,0)),row,pl.BlockSpec((width,wT.shape[1]),lambda i,*_:(wT.shape[1]//width-1,0))]+[pl.BlockSpec(g.shape,lambda i,*_:(0,0)) for g in grads]+[pl.BlockSpec((width,BQ),lambda i,*_:(0,i)),
                      pl.BlockSpec((8,BQ),lambda i,*_:(0,i)),
                      pl.BlockSpec((length,1),lambda i,*_:(0,0)),
                      pl.BlockSpec((1,BQ),lambda i,*_:(0,first+i))]+[row]*len(sums),
            out_specs=[pl.BlockSpec((width,BQ),lambda i,*_:(0,i)),row,row,pl.BlockSpec((width,128),lambda i,*_:(0,0))]+eight[1],
            scratch_shapes=[pltpu.VMEM((length,width),f32),pltpu.VMEM((length,width),f32),pltpu.VMEM((width,BQ),bf16)]),
        compiler_params=pltpu.CompilerParams(dimension_semantics=("arbitrary",),vmem_limit_bytes=60<<20),
        cost_estimate=pl.CostEstimate(flops=30*length*length*width,bytes_accessed=10*length*width,transcendentals=heads*length*length//4),
        name="attention_back",
    )(lo,hi,flip,qT,k,kT,v,wT,*grads,oT,lse,segc,segr,*sums)

def spans(seg_row):
    length=seg_row.shape[0]
    first=seg_row[::BQ]; last=seg_row[BQ-1::BQ]
    lo=jnp.sum(seg_row[None,:]<first[:,None],axis=1,dtype=jnp.int32)//BK
    hi=(jnp.sum(seg_row[None,:]<=last[:,None],axis=1,dtype=jnp.int32)+BK-1)//BK
    return lo,hi

EPSILON=1e-12
T=256
RC=128

def row_stats(values):
    centre=jnp.mean(values,axis=1,keepdims=True)
    centred=values-centre
    spread=jnp.mean(centred*centred,axis=1,keepdims=True)
    scale=lax.rsqrt(spread+EPSILON)
    return centred*scale, scale

def fold(values):
    return jnp.sum(values.reshape(values.shape[0]//8,8,values.shape[1]),axis=0)

def placements(count, model, blocks):
    if count != 8:
        return [[(r % 2, 0, r % 2, 0, None, model)] for r in range(blocks)]
    rows = model // 8
    every = []
    for r in range(blocks):
        core, beyond = r % 2, r // 2
        block = []
        for shard in range(8):
            odd, place = shard % 2, shard // 2
            if not beyond:
                source, first = odd, place
            elif not odd:
                source, first = 2, place
            else:
                source, first = (3, 0) if place == 0 else (4, place - 1)
            group = beyond and odd
            target = 0 if group else beyond * 2 + odd
            block.append((core * 5 + source, first * rows, core * 2 + group, (target * 4 + place) * rows, shard, rows))
        every.append(block)
    return every


def ffn_kernel(count, home_ref, tok_ref, a0_ref, a1_ref, a2_ref, cot_ref, vec_ref, be_ref, *refs):
    rows, width = tok_ref.shape
    blocks, units = be_ref.shape
    table = placements(count, width, blocks)
    n_in = 1 + max(item[0] for block in table for item in block)
    n_out = 1 + max(item[2] for block in table for item in block)
    pieces, refs = refs[:n_in], refs[n_in:]
    (out_ref, gm_ref, gml_ref, vg_ref, eb_ref), refs = refs[:5], refs[5:]
    grads, refs = refs[:n_out], refs[n_out:]
    we, ws, hl, hlT, hid, xhat, rs1, act, gp, acc, sl, slT, gsum, il, de, dt, wsem, osem = refs
    home = home_ref[0]
    def columns(ref, r, half):
        start = half * units + (r // 2 * 2 * units if len(table[0]) == 1 else 0)
        return ref.at[:, start : start + units]
    def spot(shard, size):
        return pl.ds(0 if shard is None else pl.multiple_of(jnp.bitwise_xor(home, shard) * size, size), size)
    def fetched(r, half):
        return [
            pltpu.make_async_copy(columns(pieces[p], r, half).at[first : first + size], (we, ws)[half].at[r, spot(shard, size)], wsem.at[half, r, k])
            for k, (p, first, _, _, shard, size) in enumerate(table[r])
        ]
    def sent(slot, r):
        return [
            pltpu.make_async_copy((de, dt)[half].at[slot, spot(shard, size)], columns(grads[g], r, half).at[first : first + size], osem.at[half, slot, k])
            for half in range(2)
            for k, (_, _, g, first, shard, size) in enumerate(table[r])
        ]
    for r in range(blocks):
        for half in range(2):
            for c in fetched(r, half):
                c.start()
    mb=vec_ref[0:1,:]; g1=vec_ref[1:2,:]; b1=vec_ref[2:3,:]; sb=vec_ref[3:4,:]; g2=vec_ref[4:5,:]; b2=vec_ref[5:6,:]
    def first(i,_):
        at=pl.ds(pl.multiple_of(i*RC,RC),RC)
        mixed=tok_ref[at,:].astype(f32)+(a0_ref[at,:].astype(f32)+a1_ref[at,:].astype(f32)+a2_ref[at,:].astype(f32))+mb
        z,scale=row_stats(mixed)
        xhat[at,:]=z
        rs1[at,:]=jnp.broadcast_to(scale,(RC,128))
        h=z*g1+b1
        hid[at,:]=h
        hl[at,:]=h.astype(bf16)
        acc[at,:]=jnp.zeros((RC,width),f32)
        return 0
    lax.fori_loop(0,rows//RC,first,0,unroll=2)
    def turn(src,dst):
        def go(i,_):
            at=pl.multiple_of(i*T,T)
            dst[:,pl.ds(at,T)]=jnp.transpose(src[pl.ds(at,T),:].astype(f32)).astype(bf16)
            return 0
        lax.fori_loop(0,rows//T,go,0)
    turn(hl,hlT)
    TG=768; TM=min(512,rows); per=units//T; mt=rows//TM
    def forward(r,_):
        for k in range(blocks):
            @pl.when(r==k)
            def _():
                for c in fetched(k, 0): c.wait()
        def tile(j,_):
            n=pl.multiple_of((j//mt)*T,T); m=pl.multiple_of((j%mt)*TM,TM)
            u=lax.dot_general(hl[pl.ds(m,TM),:],we[r,:,pl.ds(n,T)],NN,preferred_element_type=f32)+be_ref[pl.ds(r,1),pl.ds(n,T)]
            cdf=0.5+0.5*lax.erf(u*(0.5**0.5))
            act[r,pl.ds(m,TM),pl.ds(n,T)]=(u*cdf).astype(bf16)
            gp[r,pl.ds(m,TM),pl.ds(n,T)]=cdf+u*(jnp.exp(-0.5*u*u)*0.3989422804014327)
            return 0
        lax.fori_loop(0,per*mt,tile,0,unroll=3)
        for k in range(blocks):
            @pl.when(r==k)
            def _():
                for c in fetched(k, 1): c.wait()
        def shrink(j,_):
            n=pl.multiple_of((j//mt)*T,T); m=pl.multiple_of((j%mt)*TM,TM)
            acc[pl.ds(m,TM),pl.ds(n,T)]+=lax.dot_general(act[r,pl.ds(m,TM),:],ws[r,pl.ds(n,T),:],NT,preferred_element_type=f32)
            return 0
        lax.fori_loop(0,(width//T)*mt,shrink,0,unroll=3)
        return 0
    lax.fori_loop(0,blocks,forward,0)
    def second(i,sums):
        at=pl.ds(pl.multiple_of(i*RC,RC),RC)
        summed=hid[at,:]+acc[at,:]+sb
        z,scale=row_stats(summed)
        out_ref[at,:]=(z*g2+b2).astype(bf16)
        cot=cot_ref[at,:].astype(f32)
        e=cot*g2
        g=(e-jnp.mean(e,axis=1,keepdims=True)-z*jnp.mean(e*z,axis=1,keepdims=True))*scale
        gsum[at,:]=g
        sl[at,:]=g.astype(bf16)
        acc[at,:]=g
        return (sums[0]+fold(cot*z),sums[1]+fold(cot),sums[2]+fold(g))
    zero=jnp.zeros((8,width),f32)
    sg,sh,sbg=lax.fori_loop(0,rows//RC,second,(zero,zero,zero),unroll=2)
    turn(sl,slT)
    def backward(r,_):
        slot=r%2
        def tile(j,_):
            n=pl.multiple_of((j//mt)*T,T); m=pl.multiple_of((j%mt)*TM,TM)
            ga=lax.dot_general(sl[pl.ds(m,TM),:],ws[r,:,pl.ds(n,T)],NN,preferred_element_type=f32)
            gi=ga*gp[r,pl.ds(m,TM),pl.ds(n,T)]
            il[pl.ds(m,TM),pl.ds(n,T)]=gi.astype(bf16)
            part=fold(gi)
            eb_ref[r,:,pl.ds(n,T)]=jnp.where(m==0,part,eb_ref[r,:,pl.ds(n,T)]+part)
            return 0
        lax.fori_loop(0,per*mt,tile,0,unroll=3)
        def back(j,_):
            n=pl.multiple_of((j//mt)*T,T); m=pl.multiple_of((j%mt)*TM,TM)
            acc[pl.ds(m,TM),pl.ds(n,T)]+=lax.dot_general(il[pl.ds(m,TM),:],we[r,pl.ds(n,T),:],NT,preferred_element_type=f32)
            return 0
        lax.fori_loop(0,(width//T)*mt,back,0,unroll=3)
        for k in range(2,blocks):
            @pl.when(r==k)
            def _():
                for c in sent(k%2,k-2): c.wait()
        def grads(j,_):
            n=pl.multiple_of((j//(width//TG))*T,T); m=pl.multiple_of((j%(width//TG))*TG,TG)
            dt[slot,pl.ds(m,TG),pl.ds(n,T)]=lax.dot_general(slT[pl.ds(m,TG),:],act[r,:,pl.ds(n,T)],NN,preferred_element_type=f32).astype(bf16)
            de[slot,pl.ds(m,TG),pl.ds(n,T)]=lax.dot_general(hlT[pl.ds(m,TG),:],il[:,pl.ds(n,T)],NN,preferred_element_type=f32).astype(bf16)
            return 0
        lax.fori_loop(0,(width//TG)*per,grads,0,unroll=3)
        for k in range(blocks):
            @pl.when(r==k)
            def _():
                for c in sent(k%2,k): c.start()
        return 0
    lax.fori_loop(0,blocks,backward,0)
    def last(i,sums):
        at=pl.ds(pl.multiple_of(i*RC,RC),RC)
        g=acc[at,:]
        z=xhat[at,:]
        e=g*g1
        gm=(e-jnp.mean(e,axis=1,keepdims=True)-z*jnp.mean(e*z,axis=1,keepdims=True))*rs1[at,0:1]
        gm_ref[at,:]=gm
        gml_ref[at,:]=gm.astype(bf16)
        return (sums[0]+fold(g*z),sums[1]+fold(g),sums[2]+fold(gm))
    fg,fs,mbg=lax.fori_loop(0,rows//RC,last,(zero,zero,zero),unroll=2)
    for n,v in enumerate((mbg,fg,fs,sbg,sg,sh)):
        vg_ref[n]=v
    for k in range(max(0,blocks-2),blocks):
        for c in sent(k%2,k): c.wait()

def ffn(home, count, tok, a0, a1, a2, cot, vec, be, pieces):
    rows, width = tok.shape
    blocks, units = be.shape
    table = placements(count, width, blocks)
    n_out = 1 + max(item[2] for block in table for item in block)
    each = len(table[0])
    sizes = [(width * 3 // 2, 2 * units), (width // 2, 2 * units)] * 2 if each > 1 else [(width, blocks * units)] * 2
    grads = tuple(jax.ShapeDtypeStruct(size, bf16) for size in sizes)
    v = pl.BlockSpec(memory_space=pltpu.VMEM)
    h = pl.BlockSpec(memory_space=pltpu.HBM)
    V = pltpu.VMEM
    return pl.pallas_call(
        functools.partial(ffn_kernel, count),
        out_shape=(jax.ShapeDtypeStruct((rows, width), bf16), jax.ShapeDtypeStruct((rows, width), f32), jax.ShapeDtypeStruct((rows, width), bf16),
            jax.ShapeDtypeStruct((6, 8, width), f32), jax.ShapeDtypeStruct((blocks, 8, units), f32)) + grads,
        in_specs=[pl.BlockSpec(memory_space=pltpu.SMEM)] + [v] * 7 + [h] * len(pieces),
        out_specs=[v] * 5 + [h] * n_out,
        scratch_shapes=[V((blocks, width, units), bf16), V((blocks, width, units), bf16),
            V((rows, width), bf16), V((width, rows), bf16), V((rows, width), f32), V((rows, width), f32), V((rows, 128), f32),
            V((blocks, rows, units), bf16), V((blocks, rows, units), f32), V((rows, width), f32), V((rows, width), bf16), V((width, rows), bf16), V((rows, width), f32),
            V((rows, units), bf16), V((2, width, units), bf16), V((2, width, units), bf16),
            pltpu.SemaphoreType.DMA((2, blocks, each)), pltpu.SemaphoreType.DMA((2, 2, each))],
        compiler_params=pltpu.CompilerParams(vmem_limit_bytes=60 << 20),
        cost_estimate=pl.CostEstimate(flops=30 * rows * width * units * blocks, bytes_accessed=8 * blocks * width * units, transcendentals=2 * rows * units * blocks),
        name="feed_forward",
    )(home, tok, a0, a1, a2, cot, vec, be, *pieces)


def proj_kernel(home_ref, x0, x1, x2, x3, wa_ref, wb_ref, bq_ref, bvc_ref, bvr_ref,
                q_ref, kT_ref, vT_ref, k_ref, v_ref, wT, w_ref, wk, wv, x_buf, sem, x_sem):
    model = w_ref.shape[0]
    count, rows = sem.shape[0], model // sem.shape[0]
    width = q_ref.shape[0]
    home = home_ref[0]
    step = pl.program_id(0)
    def copy(r):
        src = (wa_ref, wb_ref)[r % 2].at[(r // 2) * rows : (r // 2 + 1) * rows]
        at = pl.multiple_of(jnp.bitwise_xor(home, r) * rows, rows)
        return pltpu.make_async_copy(src, w_ref.at[pl.ds(at, rows)], sem.at[r])
    if wa_ref.shape[0] == model:
        count = 1
        copy = lambda r: pltpu.make_async_copy(wa_ref, w_ref, sem.at[r])
    fetch = [pltpu.make_async_copy(x, x_buf.at[n], x_sem.at[n]) for n, x in enumerate((x0, x1, x2, x3))]
    @pl.when(step == 0)
    def _():
        for r in range(count):
            copy(r).start()
        for x in fetch:
            x.start()
        for r in range(count):
            copy(r).wait()
        def turn(i, _):
            at = pl.multiple_of(i * 256, 256)
            wT[:, pl.ds(at, 256)] = jnp.transpose(w_ref[pl.ds(at, 256), :].astype(f32)).astype(bf16)
            return 0
        lax.fori_loop(0, model // 256, turn, 0)
        wk[...] = w_ref[:, width : 2 * width]
        wv[...] = w_ref[:, 2 * width : 3 * width]
    for n, x in enumerate(fetch):
        @pl.when(step == n)
        def _():
            x.wait()
    x = x_buf[step]
    k_ref[...] = jnp.dot(x, wk[...], preferred_element_type=f32).astype(bf16)
    v_ref[...] = (jnp.dot(x, wv[...], preferred_element_type=f32) + bvr_ref[...]).astype(bf16)
    q_ref[...] = (lax.dot_general(wT[0:width], x, NT, preferred_element_type=f32) + bq_ref[...]).astype(bf16)
    kT_ref[...] = lax.dot_general(wT[width : 2 * width], x, NT, preferred_element_type=f32).astype(bf16)
    vT_ref[...] = (lax.dot_general(wT[2 * width : 3 * width], x, NT, preferred_element_type=f32) + bvc_ref[...]).astype(bf16)


def project(home, tokens, wa, wb, count, bq, bv):
    size, model = tokens[0].shape
    length = 4 * size
    width = bq.shape[0]
    hbm = pl.BlockSpec(memory_space=pltpu.HBM)
    column = pl.BlockSpec((width, 1), lambda i: (0, 0))
    tall = jax.ShapeDtypeStruct((length, width), bf16)
    flat = jax.ShapeDtypeStruct((width, length), bf16)
    across = pl.BlockSpec((width, size), lambda i: (0, i))
    down = pl.BlockSpec((size, width), lambda i: (i, 0))
    return pl.pallas_call(
        proj_kernel,
        grid=(4,),
        out_shape=(flat, flat, flat, tall, tall, jax.ShapeDtypeStruct((model, model), bf16)),
        in_specs=[pl.BlockSpec(memory_space=pltpu.SMEM)] + [hbm] * 6 + [column, column, pl.BlockSpec((1, width), lambda i: (0, 0))],
        out_specs=[across, across, across, down, down, pl.BlockSpec((model, model), lambda i: (0, 0))],
        scratch_shapes=[pltpu.VMEM((model, model), bf16), pltpu.VMEM((model, width), bf16), pltpu.VMEM((model, width), bf16),
            pltpu.VMEM((4, size, model), bf16), pltpu.SemaphoreType.DMA((count,)), pltpu.SemaphoreType.DMA((4,))],
        compiler_params=pltpu.CompilerParams(dimension_semantics=("arbitrary",), vmem_limit_bytes=60 << 20),
        cost_estimate=pl.CostEstimate(flops=30 * length * model * width, bytes_accessed=4 * length * model, transcendentals=0),
        name="projection",
    )(home, *tokens, wa, wb, bq[:, None], bv[:, None], bv[None, :])


def grads_kernel(home_ref, x0, x1, x2, x3, g0, g1, g2, g3, ca_ref, cb_ref, qa_ref, qb_ref, k_ref, v_ref, *rest):
    *outs, acc, x_buf, g_buf, xT, gT, sem = rest
    home = home_ref[0]
    step = pl.program_id(0)
    size, model = xT.shape[1], xT.shape[0]
    width = k_ref.shape[1]
    fetch = [
        (pltpu.make_async_copy(x, x_buf.at[n], sem.at[0, n]), pltpu.make_async_copy(g, g_buf.at[n], sem.at[1, n]))
        for n, (x, g) in enumerate(zip((x0, x1, x2, x3), (g0, g1, g2, g3)))
    ]
    @pl.when(step == 0)
    def _():
        for x, g in fetch:
            x.start()
            g.start()
    for n, (x, g) in enumerate(fetch):
        @pl.when(step == n)
        def _():
            x.wait()
            g.wait()
    for i in range(0, size, 256):
        xT[:, i : i + 256] = jnp.transpose(x_buf[step, i : i + 256, :].astype(f32)).astype(bf16)
        gT[:, i : i + 256] = jnp.transpose(g_buf[step, i : i + 256, :].astype(f32)).astype(bf16)
    q = jnp.where(step < 2, qa_ref[...], qb_ref[...])
    c = jnp.where(step < 2, ca_ref[...], cb_ref[...])
    pieces = (
        lax.dot_general(xT[...], q, NT, preferred_element_type=f32),
        jnp.dot(xT[...], k_ref[...], preferred_element_type=f32),
        jnp.dot(xT[...], v_ref[...], preferred_element_type=f32),
        lax.dot_general(gT[...], c, NT, preferred_element_type=f32),
    )
    @pl.when(step == 0)
    def _():
        for m, piece in enumerate(pieces):
            acc[m] = piece
    @pl.when(step > 0)
    def _():
        for m, piece in enumerate(pieces):
            acc[m] += piece
    @pl.when(step == 3)
    def _():
        if len(outs) == 1:
            for m in range(4):
                outs[0][:, m * width : (m + 1) * width] = acc[m].astype(bf16)
            return
        rows = model // 8
        for r in range(8):
            at = pl.ds(pl.multiple_of(jnp.bitwise_xor(home, r) * rows, rows), rows)
            to = slice(r // 2 * rows, (r // 2 + 1) * rows)
            for m in range(4):
                outs[r % 2][to, m * width : (m + 1) * width] = acc[m, at, :].astype(bf16)


def halves(width, size):
    return [pl.BlockSpec((width, size), lambda i: (0, jnp.minimum(i, 1))), pl.BlockSpec((width, size), lambda i: (0, jnp.maximum(i, 2) - 2))]


def attn_grads(home, count, tokens, grads, contextT, dqT, dk, dv):
    size, model = tokens[0].shape
    width = dk.shape[1]
    hbm = pl.BlockSpec(memory_space=pltpu.HBM)
    down = pl.BlockSpec((size, width), lambda i: (i, 0))
    parts = 2 if count == 8 else 1
    V = pltpu.VMEM
    return pl.pallas_call(
        grads_kernel,
        grid=(4,),
        out_shape=[jax.ShapeDtypeStruct((model // parts, 4 * width), bf16)] * parts,
        in_specs=[pl.BlockSpec(memory_space=pltpu.SMEM)] + [hbm] * 8 + halves(width, size) * 2 + [down, down],
        out_specs=[pl.BlockSpec((model // parts, 4 * width), lambda i: (0, 0))] * parts,
        scratch_shapes=[V((4, model, width), f32), V((4, size, model), bf16), V((4, size, model), bf16), V((model, size), bf16), V((model, size), bf16),
            pltpu.SemaphoreType.DMA((2, 4))],
        compiler_params=pltpu.CompilerParams(dimension_semantics=("arbitrary",), vmem_limit_bytes=60 << 20),
        cost_estimate=pl.CostEstimate(flops=100 * size * model * width, bytes_accessed=24 * size * model, transcendentals=0),
        name="projection_grads",
    )(home, *tokens, *grads, *contextT, *dqT, dk, dv)


def back_kernel(qa_ref, qb_ref, k_ref, v_ref, wq_ref, wk_ref, wv_ref, near_ref, side_ref, far_ref):
    i = pl.program_id(0)
    size = near_ref.shape[0]
    def block(q_ref):
        q = jnp.transpose(q_ref[...].astype(f32)).astype(bf16)
        total = jnp.dot(q, wq_ref[...], preferred_element_type=f32)
        total = total + jnp.dot(k_ref[...], wk_ref[...], preferred_element_type=f32)
        return (total + jnp.dot(v_ref[...], wv_ref[...], preferred_element_type=f32)).astype(bf16)
    for n, ref in enumerate((near_ref, side_ref, far_ref, side_ref)):
        @pl.when(i == n)
        def _():
            ref[size if n == 3 else 0 : 2 * size if n == 3 else size, :] = block((qa_ref, qb_ref)[n // 2])


def project_back(dqT, dk, dv, wT):
    length, width = dk.shape
    size, model = length // 4, wT.shape[1]
    down = pl.BlockSpec((size, width), lambda i: (i, 0))
    weight = [pl.BlockSpec((width, model), functools.partial(lambda n, i: (n, 0), n)) for n in range(3)]
    return pl.pallas_call(
        back_kernel,
        grid=(4,),
        out_shape=[jax.ShapeDtypeStruct((n * size, model), bf16) for n in (1, 2, 1)],
        in_specs=halves(width, size) + [down, down] + weight,
        out_specs=[pl.BlockSpec((n * size, model), lambda i: (0, 0)) for n in (1, 2, 1)],
        compiler_params=pltpu.CompilerParams(dimension_semantics=("arbitrary",), vmem_limit_bytes=60 << 20),
        cost_estimate=pl.CostEstimate(flops=70 * length * model * width, bytes_accessed=8 * length * model, transcendentals=0),
        name="projection_back",
    )(*dqT, dk, dv, wT, wT, wT)


def hop(value, bit):
    count = lax.axis_size("dp")
    return lax.ppermute(value, "dp", [(i, i ^ bit) for i in range(count)])


def gather_shards(own):
    count = lax.axis_size("dp")
    if count != 8:
        every = lax.all_gather(own, "dp", axis=0, tiled=True)
        return every, every
    even = jnp.concatenate([own] + [hop(own, bit) for bit in (2, 4, 6)], axis=0)
    return even, hop(even, 1)


def later(value, *markers, flops=0):
    anywhere = pl.BlockSpec(memory_space=pl.ANY)
    return pl.pallas_call(
        lambda *refs: None,
        out_shape=jax.ShapeDtypeStruct(value.shape, value.dtype),
        in_specs=[anywhere] * (1 + len(markers)),
        out_specs=anywhere,
        input_output_aliases={0: 0},
        cost_estimate=pl.CostEstimate(flops=flops, bytes_accessed=0, transcendentals=0),
        name="later",
    )(value, *markers)


def exchange(value, bit):
    return lax.ppermute(value, "tensor", [(i, i ^ bit) for i in range(4)])


def row_blocks(own):
    across = exchange(own, 2)
    return [own, exchange(own, 1), across, exchange(across, 1)]


def gather_rows(own):
    return jnp.concatenate(row_blocks(own), axis=0)


def scatter_pieces(near, side, far):
    rows = near.shape[0]
    beside = exchange(side, 1)
    ahead = (far.astype(f32) + beside[rows:].astype(f32)).astype(bf16)
    return (near, beside[:rows], exchange(ahead, 2)), ahead


def gather_blocks(own):
    if lax.axis_size("dp") != 8:
        return [lax.all_gather(jnp.concatenate([own, exchange(own, 2)], axis=1), "dp", axis=0, tiled=True)]
    even = jnp.concatenate([own] + [hop(own, bit) for bit in (2, 4, 6)], axis=0)
    return [even, hop(even, 1), exchange(even, 2)]


def last_blocks(pieces, *markers):
    if len(pieces) == 1:
        return []
    _, odd, beyond = pieces
    cut = odd.shape[0] // 4
    return [later(exchange(odd[:cut], 2), *markers), later(hop(beyond[cut:], 1), *markers)]


def total(*terms):
    result = terms[0].astype(f32)
    for term in terms[1:]:
        result = result + term.astype(f32)
    return result


def fold_both(own, got):
    cut = own.shape[0] // 4
    return total(own[:cut], got[:cut]).astype(bf16), total(own[cut:], got[cut:]).astype(bf16)


def fold_rest(own, got, across, along):
    rows = own.shape[0] // 3
    cut = rows // 4
    part = lambda n: total(own[n * rows : (n + 1) * rows], got[n * rows : (n + 1) * rows])
    odd, beyond = part(1), part(2)
    odd = jnp.concatenate([odd[:cut] + across.astype(f32), odd[cut:]], axis=0).astype(bf16)
    beyond = jnp.concatenate([beyond[:cut], beyond[cut:] + along.astype(f32)], axis=0).astype(bf16)
    return odd, beyond


def fold_even(own, got, odd, beyond):
    rows = own.shape[0] // 3
    return total(own[:rows], got[:rows], odd, beyond).astype(bf16).reshape(4, rows // 4, -1)


def on_device(
    tokens,
    segments,
    query_proj,
    query_bias,
    key_proj,
    value_proj,
    value_bias,
    merge_proj,
    merge_bias,
    first_gain,
    first_shift,
    expand_proj,
    expand_bias,
    shrink_proj,
    shrink_bias,
    second_gain,
    second_shift,
    cotangent,
):
    everyone = ("dp", "tensor")
    part = lax.axis_index("tensor")
    dp = lax.axis_size("dp")
    world = dp * 4
    width = query_proj.shape[1]
    units = expand_proj.shape[1]
    model = width * 4
    share = model // world
    unit_share = units * 4 // world

    shard = jnp.concatenate([query_proj, key_proj, value_proj, merge_proj.T], axis=1)
    shards = gather_shards(shard)
    wide = jnp.concatenate([expand_proj, shrink_proj.T], axis=1)
    pieces = gather_blocks(wide)
    own = jnp.concatenate(
        [query_bias, value_bias, merge_bias, first_gain, first_shift, shrink_bias, second_gain, second_shift, expand_bias]
    )
    rows = tokens.shape[0]
    count = own.shape[0]
    own = jnp.concatenate([own, segments.reshape(-1).astype(f32)])
    slots = -(-own.shape[0] // 1024) * 8
    own = jnp.pad(own, (0, slots * 128 - own.shape[0])).reshape(1, slots, 128)
    vectors = lax.all_to_all(jnp.broadcast_to(own, (world, slots, 128)), everyone, 0, 0, tiled=True)
    vectors = vectors.reshape(world, slots * 128)
    whole = vectors[:, : 8 * share].reshape(world, 8, share).transpose(1, 0, 2).reshape(8, model)
    unit_bias = vectors[:, 8 * share : 8 * share + unit_share].reshape(4, units)
    flips = jnp.bitwise_xor(jnp.arange(4), part)
    seg = lax.dynamic_slice(vectors, (lax.axis_index("dp") * 4, count), (4, rows))
    seg = jnp.take(seg, flips, axis=0).reshape(-1).astype(jnp.int32)
    unit_bias = jnp.take(unit_bias, flips, axis=0)
    query_b = lax.dynamic_slice_in_dim(whole[0], part * width, width)
    value_b = lax.dynamic_slice_in_dim(whole[1], part * width, width)
    rows_b = whole[2:8]

    blocks = row_blocks(tokens)
    segc, segr = seg[:, None], seg[None, :]
    lo, hi = spans(seg)
    flip = (part * (tokens.shape[0] // BK)).astype(jnp.int32).reshape(1)
    home = lax.axis_index("dp").astype(jnp.int32).reshape(1)
    query_t, key_t, value_t, keys, values, attn_wt = project(home, blocks, *shards, dp, query_b, value_b)
    ahead = functools.partial(attn_fwd, 1, query_t, keys, value_t, attn_wt, segc, segr)
    behind = functools.partial(attn_fwd, 0, query_t, keys, value_t, attn_wt, segc, segr)
    context_b, logsum_b, far, side = ahead(later(lo, pieces[0]), hi, flip)
    beside = exchange(side, 1)
    far = (far.astype(f32) + beside.astype(f32)).astype(bf16)
    swapped = [exchange(pieces[0], 1)]
    context_a, logsum_a, a0, side = behind(later(lo, far, swapped[0], *pieces[1:]), hi, flip)
    a1 = exchange(side, 1)
    a2 = later(exchange(far, 2), context_a)

    swapped = swapped + [later(exchange(piece, 1), context_a) for piece in pieces[1:]]
    last = last_blocks(pieces, context_a, a2)
    pieces = pieces + last + swapped + [exchange(piece, 1) for piece in last]
    out = ffn(home, dp, tokens, a0, a1, a2, cotangent, rows_b, unit_bias, pieces)
    output, grad_mixed, mixed_low, row_sums, unit_sums = out[:5]
    beside = exchange(mixed_low, 1)
    across = exchange(mixed_low, 2)
    grads = out[5:]
    local = len(grads) // 2
    swapped = [exchange(grad, 1) for grad in grads[local:]]
    back = functools.partial(attn_bwd, query_t, keys, key_t, values, attn_wt)
    waits = []
    if local == 2:
        waits = fold_both(grads[1], swapped[1])
    dq_a, dk_a, dv_a, q_sums_a = back((mixed_low, beside), context_a, logsum_a, segc, segr, later(lo, *waits), hi, flip)
    across = later(across, q_sums_a)
    mixed_blocks = [mixed_low, beside, across, exchange(across, 1)]
    if local == 2:
        waits = fold_rest(grads[0], swapped[0], later(exchange(waits[0], 2), q_sums_a), later(hop(waits[1], 1), q_sums_a))
    dq_b, dk, dv, q_sums_b, v_sums = back(
        mixed_blocks[2:], context_b, logsum_b, segc, segr, later(lo, *waits), hi, flip, sums=(dk_a, dv_a)
    )
    attn_local = attn_grads(home, dp, blocks, mixed_blocks, (context_a, context_b), (dq_a, dq_b), dk, dv)
    if local == 2:
        waits = [fold_even(grads[0], swapped[0], later(hop(waits[0], 1), attn_local[0]), later(exchange(waits[1], 2), attn_local[0]))]
    even = waits[0] if local == 2 else attn_local[0]
    b0, side, far = project_back((later(dq_a, even), dq_b), dk, dv, attn_wt)

    q_sums = later(q_sums_a, even) + later(q_sums_b, even)
    v_sums = later(v_sums, even)
    mine = (jnp.arange(4) == part).astype(f32)[:, None]
    q_all = (mine * jnp.sum(q_sums, axis=1)[None]).reshape(1, model)
    v_all = (mine * jnp.sum(v_sums, axis=0)[None]).reshape(1, model)
    early = jnp.sum(row_sums, axis=1).reshape(6, world, share).transpose(1, 0, 2).reshape(world, 6 * share)
    late = jnp.concatenate([q_all, v_all], axis=0).reshape(2, world, share).transpose(1, 0, 2).reshape(world, 2 * share)
    u_all = jnp.take(jnp.sum(unit_sums, axis=1), flips, axis=0).reshape(world, unit_share)
    send = jnp.concatenate([late, early, u_all], axis=1)
    send = jnp.pad(send, ((0, 0), (0, slots * 128 - send.shape[1]))).reshape(world, slots, 128)
    got = jnp.sum(lax.all_to_all(send, everyone, 0, 0, tiled=True).reshape(world, slots * 128), axis=0)
    small = [got[n * share : (n + 1) * share] for n in range(8)]

    if local == 2:
        y_came = hop(attn_local[1], 1)
        wide_grad = even[0].astype(f32) + sum(later(hop(even[n], 2 * n), b0, got, y_came).astype(f32) for n in (1, 2, 3))
        rows = attn_local[0].shape[0] // 4
        even = total(attn_local[0], y_came).astype(bf16).reshape(4, rows, -1)
        attn_grad = even[0].astype(f32) + sum(hop(even[n], 2 * n).astype(f32) for n in (1, 2, 3))
    else:
        mine = lax.psum_scatter(total(grads[0], swapped[0]).astype(bf16), "dp", scatter_dimension=0, tiled=True)
        wide_grad = total(mine[:, : 2 * units], exchange(mine[:, 2 * units :], 2))
        attn_grad = lax.all_to_all(attn_local[0], "dp", 0, 0, tiled=True)
        attn_grad = jnp.sum(attn_grad.reshape(dp, -1, model).astype(f32), axis=0)
    (b0, b1, b2), _ = scatter_pieces(b0, later(side, got), far)
    tokens_grad = (grad_mixed + (b0.astype(f32) + b1.astype(f32) + b2.astype(f32))).astype(bf16)
    querygrad, keygrad, valuegrad, mergegrad = (attn_grad[:, n * width : (n + 1) * width] for n in range(4))
    expandgrad = wide_grad[:, :units]
    shrinkgrad = wide_grad[:, units:].T

    qbiasgrad, vbiasgrad, mbiasgrad, fgaingrad, fshiftgrad, sbiasgrad, sgaingrad, sshiftgrad = small
    ebiasgrad = got[8 * share : 8 * share + unit_share]
    return (
        output,
        tokens_grad,
        querygrad,
        qbiasgrad,
        keygrad,
        valuegrad,
        vbiasgrad,
        mergegrad.T,
        mbiasgrad,
        fgaingrad,
        fshiftgrad,
        expandgrad,
        ebiasgrad,
        shrinkgrad,
        sbiasgrad,
        sgaingrad,
        sshiftgrad,
    )


def solution(mesh):
    return jax.shard_map(
        on_device,
        mesh=mesh,
        in_specs=(
            P(("dp", "tensor"), None),
            P("dp", "tensor"),
            P("dp", "tensor"),
            P(("dp", "tensor")),
            P("dp", "tensor"),
            P("dp", "tensor"),
            P(("dp", "tensor")),
            P("tensor", "dp"),
            P(("dp", "tensor")),
            P(("dp", "tensor")),
            P(("dp", "tensor")),
            P("dp", "tensor"),
            P(("dp", "tensor")),
            P("tensor", "dp"),
            P(("dp", "tensor")),
            P(("dp", "tensor")),
            P(("dp", "tensor")),
            P(("dp", "tensor"), None),
        ),
        out_specs=(
            P(("dp", "tensor"), None),
            P(("dp", "tensor"), None),
            P("dp", "tensor"),
            P(("dp", "tensor")),
            P("dp", "tensor"),
            P("dp", "tensor"),
            P(("dp", "tensor")),
            P("tensor", "dp"),
            P(("dp", "tensor")),
            P(("dp", "tensor")),
            P(("dp", "tensor")),
            P("dp", "tensor"),
            P(("dp", "tensor")),
            P("tensor", "dp"),
            P(("dp", "tensor")),
            P(("dp", "tensor")),
            P(("dp", "tensor")),
        ),
        check_vma=False,
    )
```
